128 devices in a mesh: section: 4 (over z_lo, core), dp: 8 (over x, z_hi), mp: 4 (over y).
Axes of the slice: x: 4, y: 4, z: 4 (z_hi: 2, z_lo: 2; z = z_hi * 2 + z_lo), core: 2. Of those that a mesh axis runs over, the one named last changes fastest.
Arguments:
- entrance: bfloat16 [8, 2, 96, 4096], P('dp'), may hold values from -6 to 6
- lengths: int32 [8, 2], P('dp'), may hold values from 24 to 96
- positives: int32 [8], replicated, may hold values from 0 to 7, each once
- norm_gains: float32 [4, 4096], P('section'), may hold values from 0.5 to 1.5
- query_proj: bfloat16 [4, 4096, 2048], P('section', None, 'mp'), may hold values from -0.09375 to 0.09375
- key_proj: bfloat16 [4, 4096, 512], P('section', None, 'mp'), may hold values from -0.09375 to 0.09375
- value_proj: bfloat16 [4, 4096, 512], P('section', None, 'mp'), may hold values from -0.09375 to 0.09375
- out_proj: bfloat16 [4, 2048, 4096], P('section', 'mp'), may hold values from -0.125 to 0.125
Outputs:
- losses: float32 [4, 7], P('section')
- norm_gain_grad: float32 [4, 4096], P('section', ('dp', 'mp'))
- query_proj_grad: float32 [4, 4096, 2048], P('section', 'dp', 'mp')
- key_proj_grad: float32 [4, 4096, 512], P('section', 'dp', 'mp')
- value_proj_grad: float32 [4, 4096, 512], P('section', 'dp', 'mp')
- out_proj_grad: float32 [4, 2048, 4096], P('section', 'mp', 'dp')
The draws below stay inside these ranges and needn't reach their ends.
Inputs may be any that keep to these rules, and one draw needn't show every extreme that they name: positives is a permutation of the pair indices. `lengths`: tokens at or past a sequence's length are padding.
All inputs are finite; a program needn't handle non-finite values.
Results may differ from the reference program's by a relative error of at most 0.039.
Values may be sent and summed in bfloat16 or wider, within the bound.
No kernel may reach another device: no remote copies, remote signals or barrier semaphores. Data moves between devices by JAX's collectives and lax.ppermute only.
A program may use at most 128 MiB of HBM per device.

```python
import jax
import jax.numpy as jnp
from jax import lax

D = 4096
HQ = 16
HK = 4
HEAD = 128
WIDTHS = 7
LEN = 96
PAIRS = 8
N_SECTION = 4
N_MP = 4


def with_ends(entries, stream_key, low, high):
    longest = entries.shape.index(max(entries.shape))
    spots = []
    for shift in (0, 1):
        where = [jax.random.randint(jax.random.fold_in(stream_key, axis), (), 0, length) for axis, length in enumerate(entries.shape)]
        where[longest] = (where[longest] + shift) % entries.shape[longest]
        spots.append(tuple(where))
    return entries.at[spots[0]].set(low).at[spots[1]].set(high)


def block_levels(rng, shape, split, low, largest):
    loudness = 1.0
    for axis_at, shards_of in split:
        heights = jax.random.uniform(jax.random.fold_in(jax.random.fold_in(rng, 6), axis_at), (shards_of,), jnp.float32, low / len(split), largest / len(split))
        loudness = loudness * jnp.repeat(jnp.exp(heights), shape[axis_at] // shards_of).reshape((-1,) + (1,) * (len(shape) - 1 - axis_at))
    return loudness


def gaussian(stream_key, dims, spread, limit, split=(), held_as=jnp.bfloat16):
    loudness = block_levels(stream_key, dims, split, -0.22, 0.18) if split else 1.0
    values = jax.random.normal(stream_key, dims, jnp.float32) * spread * loudness
    return jnp.minimum(jnp.maximum(values, -limit), limit).astype(held_as)


def setup_inputs(seed: int = 0) -> dict:
    seeds = jax.random.split(jax.random.key(seed), 9)
    entrance = gaussian(seeds[0], (PAIRS, 2, LEN, D), 1.0, 6.0, ((0, 8),))
    lengths = with_ends(jax.random.randint(seeds[1], (PAIRS, 2), LEN // 4, LEN + 1), jax.random.fold_in(seeds[1], 1), LEN // 4, LEN).astype(jnp.int32)
    positives = jax.random.permutation(seeds[2], PAIRS).astype(jnp.int32)
    norm_gains = jnp.clip(1.0 + 0.1 * jax.random.normal(seeds[3], (N_SECTION, D), jnp.float32), 0.5, 1.5)
    query_proj = gaussian(seeds[4], (N_SECTION, D, HQ * HEAD), D ** -0.5, 0.09375, ((0, 4), (2, 4)))
    key_proj = gaussian(seeds[5], (N_SECTION, D, HK * HEAD), D ** -0.5, 0.09375, ((0, 4), (2, 4)))
    value_proj = gaussian(seeds[6], (N_SECTION, D, HK * HEAD), D ** -0.5, 0.09375, ((0, 4), (2, 4)))
    out_proj = gaussian(seeds[7], (N_SECTION, HQ * HEAD, D), (HQ * HEAD) ** -0.5, 0.125, ((0, 4), (1, 4)))
    return dict(entrance=entrance, lengths=lengths, positives=positives, norm_gains=norm_gains, query_proj=query_proj, key_proj=key_proj, value_proj=value_proj, out_proj=out_proj)


EPSILON = 1e-05
SOFTMAX_TEMPER = 0.05
ROPE_BASE = 500000.0

def rope_tables(length, head_size):
    half_size = head_size // 2
    inverse_freq = ROPE_BASE ** (-jnp.arange(half_size, dtype=jnp.float32) * 2.0 / head_size)
    angles = jnp.arange(length, dtype=jnp.float32)[:, None] * inverse_freq[None, :]
    return (jnp.cos(angles), jnp.sin(angles))

def rotate(values, cosine, sine_table):
    half_size = values.shape[-1] // 2
    first_half = values[..., :half_size]
    second = values[..., half_size:]
    cosine = cosine[None, :, None, :]
    sine_table = sine_table[None, :, None, :]
    return jnp.concatenate([first_half * cosine - second * sine_table, second * cosine + first_half * sine_table], axis=-1)

def attend(query_pre, key_pre, value_pre):
    seq_count, length, query_width = query_pre.shape
    query_heads = query_width // HEAD
    kv_heads = key_pre.shape[-1] // HEAD
    group_size = query_heads // kv_heads
    cosine, sine_table = rope_tables(length, HEAD)
    query_vectors = rotate(query_pre.reshape(seq_count, length, query_heads, HEAD), cosine, sine_table).astype(jnp.bfloat16)
    key_rows = rotate(key_pre.reshape(seq_count, length, kv_heads, HEAD), cosine, sine_table).astype(jnp.bfloat16)
    values = value_pre.reshape(seq_count, length, kv_heads, HEAD).astype(jnp.bfloat16)
    query_vectors = query_vectors.reshape(seq_count, length, kv_heads, group_size, HEAD)
    scores = jnp.einsum('sikge,sjke->skgij', query_vectors.astype(jnp.float32), key_rows.astype(jnp.float32)) * HEAD ** (-0.5)
    causal = jnp.arange(length, dtype=jnp.int32)[:, None] >= jnp.arange(length, dtype=jnp.int32)[None, :]
    scores = jnp.where(causal, scores, -1e+30)
    weights = jax.nn.softmax(scores, axis=-1).astype(jnp.bfloat16)
    mixture = jnp.einsum('skgij,sjke->sikge', weights.astype(jnp.float32), values.astype(jnp.float32))
    return mixture.reshape(seq_count, length, query_heads * HEAD)

def normalize(hidden_f, gain_vector):
    inv_rms = lax.rsqrt(lax.optimization_barrier(jnp.mean(hidden_f * hidden_f, axis=-1, keepdims=True)) + EPSILON)
    return hidden_f * inv_rms * gain_vector

def contract_rows(left, right):
    return lax.dot_general(left, right, (((0,), (0,)), ((), ())), preferred_element_type=jnp.float32)

def contract_last(left, right):
    return lax.dot_general(left, right, (((left.ndim - 1,), (1,)), ((), ())), preferred_element_type=jnp.float32)

def pool_exits(batch_rows, mask_of_valid, counts):
    total_value = jnp.einsum('ki,kiu->ku', mask_of_valid, batch_rows.astype(jnp.float32))
    return total_value / counts[:, None]

def spread_grad(exit_grad, mask_of_valid, counts):
    return mask_of_valid[:, :, None] * (exit_grad / counts[:, None])[:, None, :]

def matryoshka_losses(pooled, positives):
    pair_total = pooled.shape[0]
    target = (jnp.arange(pair_total, dtype=jnp.int32)[None, :] == positives[:, None]).astype(jnp.float32)
    losses = []
    for level_index in range(WIDTHS):
        leading_width = pooled.shape[-1] // 2 ** level_index
        query_vectors = pooled[:, 0, :leading_width]
        passage_rows = pooled[:, 1, :leading_width]
        query_vectors = query_vectors * lax.rsqrt(lax.optimization_barrier(jnp.mean(query_vectors * query_vectors, axis=-1, keepdims=True)) + 1e-06)
        passage_rows = passage_rows * lax.rsqrt(lax.optimization_barrier(jnp.mean(passage_rows * passage_rows, axis=-1, keepdims=True)) + 1e-06)
        score_matrix = jnp.dot(query_vectors, passage_rows.T, precision=lax.Precision.HIGHEST) / (leading_width * SOFTMAX_TEMPER)
        picked = lax.optimization_barrier(jnp.sum(score_matrix * target, axis=-1))
        losses.append(jnp.mean(jax.nn.logsumexp(score_matrix, axis=-1) - picked))
    return jnp.stack(losses)

def section_forward(hidden, gain_vector, query_weight, key_weight, value_weight, out_weight):
    hidden_f = hidden.astype(jnp.float32)
    normed = normalize(hidden_f, gain_vector).astype(jnp.bfloat16)
    query_cols = query_weight.shape[1] // N_MP
    kv_cols = key_weight.shape[1] // N_MP
    total_value = jnp.zeros(hidden_f.shape, jnp.float32)
    for member in range(N_MP):
        query_slice = query_weight[:, member * query_cols:(member + 1) * query_cols]
        key_slice = key_weight[:, member * kv_cols:(member + 1) * kv_cols]
        value_slice = value_weight[:, member * kv_cols:(member + 1) * kv_cols]
        out_slice = out_weight[member * query_cols:(member + 1) * query_cols]
        mixture = attend(jnp.dot(normed, query_slice, preferred_element_type=jnp.float32), jnp.dot(normed, key_slice, preferred_element_type=jnp.float32), jnp.dot(normed, value_slice, preferred_element_type=jnp.float32)).astype(jnp.bfloat16)
        partial_value = jnp.dot(mixture, out_slice, preferred_element_type=jnp.float32).astype(jnp.bfloat16)
        total_value = total_value + partial_value.astype(jnp.float32)
    return (hidden_f + total_value).astype(jnp.bfloat16)

def section_backward(hidden, upstream, gain_vector, query_weight, key_weight, value_weight, out_weight):
    hidden_f = hidden.astype(jnp.float32)
    inv_rms = lax.rsqrt(lax.optimization_barrier(jnp.mean(hidden_f * hidden_f, axis=-1, keepdims=True)) + EPSILON)
    normed = normalize(hidden_f, gain_vector).astype(jnp.bfloat16)
    out_grad = upstream.astype(jnp.bfloat16)
    query_cols = query_weight.shape[1] // N_MP
    kv_cols = key_weight.shape[1] // N_MP
    width_all = hidden.shape[-1]
    normed_rows = normed.reshape(-1, width_all)
    out_rows = out_grad.reshape(-1, width_all)
    normed_grad = jnp.zeros(hidden_f.shape, jnp.float32)
    query_parts, key_parts, value_parts, out_parts = ([], [], [], [])
    for member in range(N_MP):
        query_slice = query_weight[:, member * query_cols:(member + 1) * query_cols]
        key_slice = key_weight[:, member * kv_cols:(member + 1) * kv_cols]
        value_slice = value_weight[:, member * kv_cols:(member + 1) * kv_cols]
        out_slice = out_weight[member * query_cols:(member + 1) * query_cols]
        mixture_f, pullback = jax.vjp(attend, jnp.dot(normed, query_slice, preferred_element_type=jnp.float32), jnp.dot(normed, key_slice, preferred_element_type=jnp.float32), jnp.dot(normed, value_slice, preferred_element_type=jnp.float32))
        mixture = mixture_f.astype(jnp.bfloat16)
        mixture_grad = contract_last(out_grad, out_slice).astype(jnp.bfloat16)
        pulled = pullback(lax.optimization_barrier(mixture_grad).astype(jnp.float32))
        query_grad, key_grad, value_grad = [piece_grad.astype(jnp.bfloat16) for piece_grad in pulled]
        member_grad = contract_last(query_grad, query_slice) + contract_last(key_grad, key_slice) + contract_last(value_grad, value_slice)
        normed_grad = normed_grad + lax.optimization_barrier(member_grad.astype(jnp.bfloat16)).astype(jnp.float32)
        query_parts.append(contract_rows(normed_rows, query_grad.reshape(-1, query_cols)))
        key_parts.append(contract_rows(normed_rows, key_grad.reshape(-1, kv_cols)))
        value_parts.append(contract_rows(normed_rows, value_grad.reshape(-1, kv_cols)))
        out_parts.append(contract_rows(mixture.reshape(-1, query_cols), out_rows))
    gain_grad = lax.optimization_barrier(jnp.sum(normed_grad * hidden_f * inv_rms, axis=(0, 1)))
    _, norm_pull = jax.vjp(lambda values: normalize(values, gain_vector), hidden_f)
    input_grad = (upstream + norm_pull(normed_grad)[0]).astype(jnp.bfloat16)
    return (input_grad, (gain_grad, jnp.concatenate(query_parts, axis=1), jnp.concatenate(key_parts, axis=1), jnp.concatenate(value_parts, axis=1), jnp.concatenate(out_parts, axis=0)))

def reference(entrance, lengths, positives, norm_gains, query_proj, key_proj, value_proj, out_proj):
    seq_count = 2 * PAIRS
    hidden = entrance.reshape(seq_count, LEN, D)
    mask_of_valid = (jnp.arange(LEN, dtype=jnp.int32)[None, :] < lengths.reshape(seq_count, 1)).astype(jnp.float32)
    counts = lax.optimization_barrier(jnp.sum(mask_of_valid, axis=1))
    section_inputs = []
    loss_rows = []
    token_grads = []
    for section_index in range(N_SECTION):
        section_inputs.append(hidden)
        hidden = section_forward(hidden, norm_gains[section_index], query_proj[section_index], key_proj[section_index], value_proj[section_index], out_proj[section_index])
        pooled = pool_exits(hidden, mask_of_valid, counts).reshape(PAIRS, 2, D)
        losses_now, pullback = jax.vjp(lambda embedded: matryoshka_losses(embedded, positives), pooled)
        exit_grad = pullback(jnp.ones((WIDTHS,), jnp.float32))[0]
        loss_rows.append(losses_now)
        token_grads.append(spread_grad(exit_grad.reshape(seq_count, D), mask_of_valid, counts))
    incoming = jnp.zeros((seq_count, LEN, D), jnp.bfloat16)
    results = [None] * N_SECTION
    for section_index in reversed(range(N_SECTION)):
        upstream = token_grads[section_index] + incoming.astype(jnp.float32)
        incoming, grads_now = section_backward(section_inputs[section_index], upstream, norm_gains[section_index], query_proj[section_index], key_proj[section_index], value_proj[section_index], out_proj[section_index])
        results[section_index] = grads_now
    return (jnp.stack(loss_rows), jnp.stack([entry[0] for entry in results]), jnp.stack([entry[1] for entry in results]), jnp.stack([entry[2] for entry in results]), jnp.stack([entry[3] for entry in results]), jnp.stack([entry[4] for entry in results]))
```

```python
import functools

import jax
import jax.numpy as jnp
import numpy as np
from jax import lax
from jax.experimental import pallas as pl
from jax.experimental.pallas import tpu as pltpu
from jax.sharding import PartitionSpec as P

HEAD = 128
WIDTHS = 7
EPSILON = 1e-05
SOFTMAX_TEMPER = 0.05
ROPE_BASE = 500000.0

LEN = 96
D = 4096
MP = 4
SECTIONS = 4
ROWS = 2 * LEN
BLOCK = ROWS // MP
QC = 512
KC = 128
HEADS = QC // HEAD
CH = 1024
NC = D // CH
SCALE = HEAD**-0.5
BF = jnp.bfloat16
F32 = jnp.float32
VMEM_LIMIT = 40 << 20


def chip_of(section):
    return section // 2


def reduce_pairs(active, shift):
    others = [s for s in range(SECTIONS) if s != active]
    pairs = [(active * MP + j, active * MP + (j + shift) % MP) for j in range(MP)]
    for a, b in zip(others, others[1:] + others[:1]):
        pairs += [(a * MP + j, b * MP + j) for j in range(MP)]
    return pairs


def hop_pairs(source, target, shift):
    pairs = [(source * MP + j, target * MP + (j + shift) % MP) for j in range(MP)]
    others = [s for s in range(SECTIONS) if s not in (source, target)]
    if chip_of(source) == chip_of(target):
        moves = [(target, source), (others[0], others[1]), (others[1], others[0])]
    else:
        near = source ^ 1
        far = target ^ 1
        moves = [(target, far), (far, near), (near, source)]
    for a, b in moves:
        pairs += [(a * MP + j, b * MP + j) for j in range(MP)]
    return pairs


def scattered(parts, active):
    arrived = [
        lax.ppermute(parts[(MP - k) % MP], ("section", "mp"), reduce_pairs(active, k))
        for k in (1, 3, 2)
    ]
    return [parts[0]] + arrived


def sent_on(share, source, target):
    return [
        lax.ppermute(share, ("section", "mp"), hop_pairs(source, target, k)) for k in (0, 1, 3, 2)
    ]


def in_slots(arrived):
    return [arrived[0], arrived[1], arrived[3], arrived[2]]


def rope_tables():
    half = HEAD // 2
    inverse_freq = np.float32(ROPE_BASE) ** (-np.arange(half, dtype=np.float32) * 2.0 / HEAD)
    angles = np.arange(LEN, dtype=np.float32)[:, None] * inverse_freq.astype(np.float32)[None, :]
    cosine, sine = np.cos(angles).astype(np.float32), np.sin(angles).astype(np.float32)
    cosine = np.concatenate([cosine, cosine], axis=1)
    sine = np.concatenate([-sine, sine], axis=1)
    return np.tile(cosine, (2, 1)), np.tile(sine, (2, 1))


def token_of(member, dim):
    shape = (ROWS, 1) if dim == 0 else (1, ROWS)
    i = lax.broadcasted_iota(jnp.int32, shape, dim)
    slot = (
        (i >= BLOCK).astype(jnp.int32)
        + (i >= 2 * BLOCK).astype(jnp.int32)
        + (i >= 3 * BLOCK).astype(jnp.int32)
    )
    block = (member - slot) & (MP - 1)
    return block * BLOCK + i - slot * BLOCK


def dot(a, b, dims):
    return lax.dot_general(a, b, (dims, ((), ())), preferred_element_type=F32)


NN = ((1,), (0,))
NT = ((1,), (1,))
TN = ((0,), (0,))


def rotated(x, cosine, sine):
    return x * cosine + pltpu.roll(x, HEAD // 2, 1) * sine


def rotated_back(x, cosine, sine):
    return x * cosine - pltpu.roll(x, HEAD // 2, 1) * sine


def attention_mask(member):
    row = token_of(member, 0)
    col = token_of(member, 1)
    first = jnp.where(row >= LEN, LEN, 0)
    return (col <= row) & (col >= first)


def probabilities(query, key, mask):
    scores = dot(query, key, NT) * SCALE
    scores = jnp.where(mask, scores, -1e30)
    top = jnp.max(scores, axis=-1, keepdims=True)
    weights = jnp.exp(scores - top)
    return weights / jnp.sum(weights, axis=-1, keepdims=True)


def slots_at(ref, at):
    return jnp.concatenate([ref[k, :, pl.ds(at, CH)] for k in range(MP)], axis=0)


def forward_kernel(received, last, *refs):
    refs = list(refs)
    meta = refs.pop(0)
    cur = refs.pop(0)
    arrivals = [refs.pop(0) for _ in range(MP)] if received else None
    gain, cos_ref, sin_ref, wq, wk, wv, wo = [refs.pop(0) for _ in range(7)]
    held = refs.pop(0) if received else cur
    if last:
        normed_out, qkv_out, mix_out, pool_out, inv = [refs.pop(0) for _ in range(5)]
    else:
        part_refs = [refs.pop(0) for _ in range(MP)]
        inv = refs.pop(0)
        mix_out = refs.pop(0)
    acc_q, acc_k, acc_v = refs[:3]
    pooled_scr = refs[3] if last else None
    step = pl.program_id(0)
    member = meta[0]

    @pl.when(step == 0)
    def _():
        for k in range(MP):
            if received:
                rows = jnp.where(meta[1] == 1, arrivals[k][...], cur[k])
                held[k] = rows
            else:
                rows = cur[k]
            rows = rows.astype(F32)
            inv[k * BLOCK : (k + 1) * BLOCK, :] = lax.rsqrt(
                jnp.mean(rows * rows, axis=-1, keepdims=True) + EPSILON
            )
        acc_q[...] = jnp.zeros_like(acc_q)
        acc_k[...] = jnp.zeros_like(acc_k)
        acc_v[...] = jnp.zeros_like(acc_v)

    @pl.when(step < NC)
    def _():
        at = pl.multiple_of(step * CH, CH)
        hidden = slots_at(held, at).astype(F32)
        normed = (hidden * inv[...] * gain[...]).astype(BF)
        if last:
            normed_out[...] = normed
        acc_q[...] += dot(normed, wq[...], NN)
        acc_k[...] += dot(normed, wk[...], NN)
        acc_v[...] += dot(normed, wv[...], NN)

    @pl.when(step == NC - 1)
    def _():
        cosine, sine = cos_ref[...], sin_ref[...]
        mask = attention_mask(member)
        key = rotated(acc_k[...], cosine, sine).astype(BF)
        value = acc_v[...].astype(BF)
        if last:
            qkv_out[:, QC : QC + KC] = key
            qkv_out[:, QC + KC :] = value
        for j in range(HEADS):
            cols = slice(j * HEAD, (j + 1) * HEAD)
            query = rotated(acc_q[:, cols], cosine, sine).astype(BF)
            if last:
                qkv_out[:, cols] = query
            weights = probabilities(query, key, mask).astype(BF)
            mix_out[:, cols] = dot(weights, value, NN).astype(BF)
        if last:
            lens = (meta[2], meta[3])
            token = token_of(member, 1)
            seq = lax.broadcasted_iota(jnp.int32, (8, ROWS), 0)
            low = seq * LEN
            high = jnp.where(seq == 0, lens[0], LEN + lens[1])
            pool = ((token >= low) & (token < high) & (seq < 2)).astype(BF)
            total = dot(pool, mix_out[...], NN)
            top = total.astype(BF)
            pooled_scr[0] = top
            pooled_scr[1] = (total - top.astype(F32)).astype(BF)

    @pl.when(step >= NC)
    def _():
        if last:
            at = pl.multiple_of((step - NC) * CH, CH)
            lens = (meta[2], meta[3])
            token = token_of(member, 1)
            seq = lax.broadcasted_iota(jnp.int32, (8, ROWS), 0)
            low = seq * LEN
            high = jnp.where(seq == 0, lens[0], LEN + lens[1])
            pool = ((token >= low) & (token < high) & (seq < 2)).astype(BF)
            hidden = slots_at(held, at)
            total = dot(pooled_scr[0], wo[...], NN) + dot(pooled_scr[1], wo[...], NN)
            total = total + dot(pool, hidden, NN) * (1.0 / MP)
            row = lax.broadcasted_iota(jnp.int32, (8, 1), 0)
            count = jnp.where(row == 0, lens[0], lens[1]).astype(F32)
            pool_out[...] = (total / count)[:2].astype(BF)
        else:
            part = dot(mix_out[...], wo[...], NN).astype(BF)
            for k in range(MP):
                part_refs[k][...] = part[k * BLOCK : (k + 1) * BLOCK]


def whole(shape):
    zeros = (0,) * len(shape)
    return pl.BlockSpec(shape, lambda i: zeros)


def first_phase(i):
    return jnp.minimum(i, NC - 1)


def second_phase(i):
    return jnp.maximum(i - NC, 0)


def forward_turn(meta, cur, arrivals, gain, tables, weights, last):
    received = arrivals is not None
    wq, wk, wv, wo = weights
    in_specs = [pl.BlockSpec(memory_space=pltpu.SMEM), whole((MP, BLOCK, D))]
    operands = [meta, cur]
    if received:
        in_specs += [whole((BLOCK, D))] * MP
        operands += list(arrivals)
    in_specs += [
        pl.BlockSpec((1, CH), lambda i: (0, first_phase(i))),
        whole((ROWS, HEAD)),
        whole((ROWS, HEAD)),
        pl.BlockSpec((CH, QC), lambda i: (first_phase(i), 0)),
        pl.BlockSpec((CH, KC), lambda i: (first_phase(i), 0)),
        pl.BlockSpec((CH, KC), lambda i: (first_phase(i), 0)),
        pl.BlockSpec((QC, CH), lambda i: (0, second_phase(i))),
    ]
    operands += [gain, *tables, wq, wk, wv, wo]
    out_shape, out_specs = [], []
    if received:
        out_shape.append(jax.ShapeDtypeStruct((MP, BLOCK, D), BF))
        out_specs.append(whole((MP, BLOCK, D)))
    scratch = []
    if last:
        out_shape += [
            jax.ShapeDtypeStruct((ROWS, D), BF),
            jax.ShapeDtypeStruct((ROWS, QC + 2 * KC), BF),
            jax.ShapeDtypeStruct((ROWS, QC), BF),
            jax.ShapeDtypeStruct((2, D), BF),
            jax.ShapeDtypeStruct((ROWS, 1), F32),
        ]
        out_specs += [
            pl.BlockSpec((ROWS, CH), lambda i: (0, first_phase(i))),
            whole((ROWS, QC + 2 * KC)),
            whole((ROWS, QC)),
            pl.BlockSpec((2, CH), lambda i: (0, second_phase(i))),
            whole((ROWS, 1)),
        ]
    else:
        out_shape += [jax.ShapeDtypeStruct((BLOCK, D), BF)] * MP
        out_specs += [pl.BlockSpec((BLOCK, CH), lambda i: (0, second_phase(i)))] * MP
        scratch += [pltpu.VMEM((ROWS, 1), F32), pltpu.VMEM((ROWS, QC), BF)]
    scratch += [pltpu.VMEM((ROWS, QC), F32), pltpu.VMEM((ROWS, KC), F32), pltpu.VMEM((ROWS, KC), F32)]
    if last:
        scratch += [pltpu.VMEM((2, 8, QC), BF)]
    outs = pl.pallas_call(
        functools.partial(forward_kernel, received, last),
        grid=(2 * NC,),
        in_specs=in_specs,
        out_specs=out_specs,
        out_shape=out_shape,
        scratch_shapes=scratch,
        compiler_params=pltpu.CompilerParams(
            dimension_semantics=("arbitrary",), vmem_limit_bytes=VMEM_LIMIT
        ),
        name="forward_last" if last else "forward_turn",
    )(*operands)
    if received:
        return outs[0], outs[1:]
    return cur, outs


def token_grad(meta, gl, token):
    first = (token < meta[2]).astype(F32)
    second = ((token >= LEN) & (token < LEN + meta[3])).astype(F32)
    return first * gl[0:1, :] + second * gl[1:2, :]


def backward_kernel(received, carried, last, *refs):
    refs = list(refs)
    meta = refs.pop(0)
    inc = refs.pop(0) if carried else None
    arrivals = [refs.pop(0) for _ in range(MP)] if received else None
    gl, qkv, cos_ref, sin_ref, wq, wk, wv, wo = [refs.pop(0) for _ in range(8)]
    if last:
        hidden_ref, inv = refs.pop(0), refs.pop(0)
        dpart_out, grads, gain_out = [refs.pop(0) for _ in range(3)]
        held = refs.pop(0)
    else:
        held = refs.pop(0) if received else None
        part_refs = [refs.pop(0) for _ in range(MP)]
        grads = refs.pop(0)
    acc = refs.pop(0)
    step = pl.program_id(0)
    member = meta[0]

    @pl.when(step == 0)
    def _():
        if received:
            for k in range(MP):
                old = inc[k] if carried else jnp.zeros((BLOCK, D), BF)
                held[k] = jnp.where(meta[1] == 1, arrivals[k][...], old)
        acc[...] = jnp.zeros_like(acc)

    @pl.when(step < NC)
    def _():
        at = pl.multiple_of(step * CH, CH)
        grad = token_grad(meta, gl[...], token_of(member, 0))
        if received:
            grad = grad + slots_at(held, at).astype(F32)
        dpart = grad.astype(BF)
        if last:
            dpart_out[...] = dpart
        acc[...] += dot(dpart, wo[...], NT)

    @pl.when(step == NC - 1)
    def _():
        cosine, sine = cos_ref[...], sin_ref[...]
        mask = attention_mask(member)
        key = qkv[:, QC : QC + KC]
        value = qkv[:, QC + KC :]
        dkey = jnp.zeros((ROWS, HEAD), F32)
        dvalue = jnp.zeros((ROWS, HEAD), F32)
        for j in range(HEADS):
            cols = slice(j * HEAD, (j + 1) * HEAD)
            query = qkv[:, cols]
            dmix = acc[:, cols].astype(BF)
            weights = probabilities(query, key, mask)
            dvalue += dot(weights.astype(BF), dmix, TN)
            dweights = dot(dmix, value, NT).astype(BF).astype(F32)
            moved = weights * dweights
            dscores = (moved - weights * jnp.sum(moved, axis=-1, keepdims=True)) * SCALE
            dscores = dscores.astype(BF)
            dquery = dot(dscores, key, NN).astype(BF).astype(F32)
            grads[:, cols] = rotated_back(dquery, cosine, sine).astype(BF)
            dkey += dot(dscores, query, TN)
        dkey = dkey.astype(BF).astype(F32)
        grads[:, QC : QC + KC] = rotated_back(dkey, cosine, sine).astype(BF)
        grads[:, QC + KC :] = dvalue.astype(BF)

    @pl.when(step >= NC)
    def _():
        dnormed = dot(grads[:, :QC], wq[...], NT)
        dnormed += dot(grads[:, QC : QC + KC], wk[...], NT)
        dnormed += dot(grads[:, QC + KC :], wv[...], NT)
        dnormed = dnormed.astype(BF)
        if last:
            hidden = jnp.concatenate([hidden_ref[k] for k in range(MP)], axis=0).astype(F32)
            gain_out[...] = jnp.sum(
                dnormed.astype(F32) * hidden * inv[...], axis=0, keepdims=True
            )
        else:
            for k in range(MP):
                part_refs[k][...] = dnormed[k * BLOCK : (k + 1) * BLOCK]


def backward_turn(meta, inc, arrivals, gl, qkv, tables, weights, hidden=None, inv=None):
    received = arrivals is not None
    carried = inc is not None
    last = hidden is not None
    wq, wk, wv, wo = weights
    in_specs = [pl.BlockSpec(memory_space=pltpu.SMEM)]
    operands = [meta]
    if carried:
        in_specs.append(whole((MP, BLOCK, D)))
        operands.append(inc)
    if received:
        in_specs += [whole((BLOCK, D))] * MP
        operands += list(arrivals)
    in_specs += [
        pl.BlockSpec((2, CH), lambda i: (0, first_phase(i))),
        whole((ROWS, QC + 2 * KC)),
        whole((ROWS, HEAD)),
        whole((ROWS, HEAD)),
        pl.BlockSpec((CH, QC), lambda i: (second_phase(i), 0)),
        pl.BlockSpec((CH, KC), lambda i: (second_phase(i), 0)),
        pl.BlockSpec((CH, KC), lambda i: (second_phase(i), 0)),
        pl.BlockSpec((QC, CH), lambda i: (0, first_phase(i))),
    ]
    operands += [gl, qkv, *tables, wq, wk, wv, wo]
    out_shape, out_specs, scratch = [], [], []
    if last:
        in_specs += [
            pl.BlockSpec((MP, BLOCK, CH), lambda i: (0, 0, second_phase(i))),
            whole((ROWS, 1)),
        ]
        operands += [hidden, inv]
        out_shape += [
            jax.ShapeDtypeStruct((ROWS, D), BF),
            jax.ShapeDtypeStruct((ROWS, QC + 2 * KC), BF),
            jax.ShapeDtypeStruct((1, D), F32),
        ]
        out_specs += [
            pl.BlockSpec((ROWS, CH), lambda i: (0, first_phase(i))),
            whole((ROWS, QC + 2 * KC)),
            pl.BlockSpec((1, CH), lambda i: (0, second_phase(i))),
        ]
        scratch.append(pltpu.VMEM((MP, BLOCK, D), BF))
    else:
        if received:
            out_shape.append(jax.ShapeDtypeStruct((MP, BLOCK, D), BF))
            out_specs.append(whole((MP, BLOCK, D)))
        out_shape += [jax.ShapeDtypeStruct((BLOCK, D), BF)] * MP
        out_specs += [pl.BlockSpec((BLOCK, CH), lambda i: (0, second_phase(i)))] * MP
        scratch.append(pltpu.VMEM((ROWS, QC + 2 * KC), BF))
    scratch.append(pltpu.VMEM((ROWS, QC), F32))
    return pl.pallas_call(
        functools.partial(backward_kernel, received, carried, last),
        grid=(2 * NC,),
        in_specs=in_specs,
        out_specs=out_specs,
        out_shape=out_shape,
        scratch_shapes=scratch,
        compiler_params=pltpu.CompilerParams(
            dimension_semantics=("arbitrary",), vmem_limit_bytes=VMEM_LIMIT
        ),
        name="backward_last" if last else "backward_turn",
    )(*operands)


def forward_share_kernel(hidden, p0, p1, p2, p3, out):
    total = p0[...].astype(F32) + p1[...].astype(F32) + p2[...].astype(F32) + p3[...].astype(F32)
    out[...] = (hidden[0].astype(F32) + total).astype(BF)


def forward_share(cur, parts):
    return pl.pallas_call(
        forward_share_kernel,
        grid=(2,),
        in_specs=[pl.BlockSpec((1, BLOCK, D // 2), lambda i: (0, 0, i))]
        + [pl.BlockSpec((BLOCK, D // 2), lambda i: (0, i))] * MP,
        out_specs=pl.BlockSpec((BLOCK, D // 2), lambda i: (0, i)),
        out_shape=jax.ShapeDtypeStruct((BLOCK, D), BF),
        name="forward_share",
    )(cur, *parts)


def backward_share_kernel(received, *refs):
    refs = list(refs)
    meta, hidden = refs.pop(0), refs.pop(0)
    inc = refs.pop(0) if received else None
    gl, gain, p0, p1, p2, p3, out = refs
    token = meta[0] * BLOCK + lax.broadcasted_iota(jnp.int32, (BLOCK, 1), 0)
    upstream = token_grad(meta, gl[...], token)
    if received:
        upstream = upstream + inc[0].astype(F32)
    rows = hidden[0].astype(F32)
    inv = lax.rsqrt(jnp.mean(rows * rows, axis=-1, keepdims=True) + EPSILON)
    dnormed = p0[...].astype(F32) + p1[...].astype(F32) + p2[...].astype(F32) + p3[...].astype(F32)
    dnormed = dnormed * gain[...]
    along = jnp.mean(dnormed * rows, axis=-1, keepdims=True)
    out[...] = (upstream + inv * dnormed - rows * (inv * inv * inv * along)).astype(BF)


def backward_share(meta, cur, inc, gl, gain, parts):
    received = inc is not None
    slot = pl.BlockSpec((1, BLOCK, D), lambda i: (0, 0, 0))
    in_specs = [pl.BlockSpec(memory_space=pltpu.SMEM), slot]
    operands = [meta, cur]
    if received:
        in_specs.append(slot)
        operands.append(inc)
    in_specs += [whole((2, D)), whole((1, D))] + [whole((BLOCK, D))] * MP
    return pl.pallas_call(
        functools.partial(backward_share_kernel, received),
        grid=(1,),
        in_specs=in_specs,
        out_specs=whole((BLOCK, D)),
        out_shape=jax.ShapeDtypeStruct((BLOCK, D), BF),
        compiler_params=pltpu.CompilerParams(vmem_limit_bytes=VMEM_LIMIT),
        name="backward_share",
    )(*operands, gl, gain, *parts)


def precise(a, b, dims):
    return lax.dot_general(
        a, b, (dims, ((), ())), precision=lax.Precision.HIGHEST, preferred_element_type=F32
    )


def loss_kernel(pairs, meta, positives, raw, losses, gl):
    raw_count = raw.shape[0]
    row = lax.broadcasted_iota(jnp.int32, (pairs, raw_count), 0)
    col = lax.broadcasted_iota(jnp.int32, (pairs, raw_count), 1)
    mine = (col // (2 * MP)) == row
    pick_q = (mine & (col % 2 == 0)).astype(BF)
    pick_z = (mine & (col % 2 == 1)).astype(BF)
    every = raw[...]
    q = dot(pick_q, every, NN)
    z = dot(pick_z, every, NN)
    eye = (
        lax.broadcasted_iota(jnp.int32, (pairs, pairs), 0)
        == lax.broadcasted_iota(jnp.int32, (pairs, pairs), 1)
    ).astype(F32)
    target = (lax.broadcasted_iota(jnp.int32, (pairs, pairs), 1) == positives[...]).astype(F32)
    narrow = D // 2 ** (WIDTHS - 1)
    lane = lax.broadcasted_iota(jnp.int32, (1, 2 * narrow), 1) < narrow

    def block(x, b):
        if b == WIDTHS - 1:
            return jnp.where(lane, x[:, : 2 * narrow], 0.0)
        if b == WIDTHS - 2:
            return jnp.where(lane, 0.0, x[:, : 2 * narrow])
        return x[:, D // 2 ** (b + 1) : D // 2**b]

    gram = [None] * WIDTHS
    sq = [None] * WIDTHS
    sz = [None] * WIDTHS
    total = (jnp.zeros((pairs, pairs), F32), jnp.zeros((pairs, 1), F32), jnp.zeros((pairs, 1), F32))
    for b in reversed(range(WIDTHS)):
        qb, zb = block(q, b), block(z, b)
        total = (
            total[0] + precise(qb, zb, NT),
            total[1] + jnp.sum(qb * qb, axis=-1, keepdims=True),
            total[2] + jnp.sum(zb * zb, axis=-1, keepdims=True),
        )
        gram[b], sq[b], sz[b] = total
    cross = jnp.zeros((pairs, pairs), F32)
    pull_q = jnp.zeros((pairs, 1), F32)
    pull_z = jnp.zeros((pairs, 1), F32)
    own = (lax.broadcasted_iota(jnp.int32, (pairs, 1), 0) == meta[4]).astype(F32)
    out_lane = lax.broadcasted_iota(jnp.int32, (1, 128), 1)
    loss_row = jnp.zeros((1, 128), F32)

    def flat(column):
        return jnp.sum(column * eye, axis=0, keepdims=True)

    for b in range(WIDTHS):
        width = D // 2**b
        inv_q = lax.rsqrt(sq[b] / width + 1e-06)
        inv_z = lax.rsqrt(sz[b] / width + 1e-06)
        inv_z_row = flat(inv_z)
        weight = inv_q * inv_z_row / (width * SOFTMAX_TEMPER)
        scores = gram[b] * weight
        top = jnp.max(scores, axis=-1, keepdims=True)
        raised = jnp.exp(scores - top)
        norm = jnp.sum(raised, axis=-1, keepdims=True)
        each = jnp.log(norm) + top - jnp.sum(scores * target, axis=-1, keepdims=True)
        loss_row = loss_row + jnp.where(
            out_lane == b, jnp.sum(each, axis=0, keepdims=True) / pairs, 0.0
        )
        dscores = (raised / norm - target) / pairs
        cross = cross + dscores * weight
        ds = dscores * scores
        pull_q = pull_q + jnp.sum(ds, axis=-1, keepdims=True) * inv_q * inv_q / width
        ds_z = jnp.sum(jnp.sum(ds, axis=0, keepdims=True) * eye, axis=-1, keepdims=True)
        pull_z = pull_z + ds_z * inv_z * inv_z / width
        qb, zb = block(q, b), block(z, b)
        dq = precise(cross, zb, NN) - pull_q * qb
        dz = precise(cross, qb, TN) - pull_z * zb
        dq = jnp.sum(dq * own, axis=0, keepdims=True) / meta[2].astype(F32)
        dz = jnp.sum(dz * own, axis=0, keepdims=True) / meta[3].astype(F32)
        if b == WIDTHS - 2:
            held_q, held_z = dq, dz
        elif b == WIDTHS - 1:
            gl[0:1, : 2 * narrow] = jnp.where(lane, dq, held_q)
            gl[1:2, : 2 * narrow] = jnp.where(lane, dz, held_z)
        else:
            gl[0:1, width // 2 : width] = dq
            gl[1:2, width // 2 : width] = dz
    losses[...] = loss_row


def loss_and_grad(meta, positives, raw):
    pairs = positives.shape[0]
    return pl.pallas_call(
        functools.partial(loss_kernel, pairs),
        grid=(1,),
        in_specs=[
            pl.BlockSpec(memory_space=pltpu.SMEM),
            whole((pairs, 1)),
            whole(raw.shape),
        ],
        out_specs=[whole((1, 128)), whole((2, D))],
        out_shape=[jax.ShapeDtypeStruct((1, 128), F32), jax.ShapeDtypeStruct((2, D), F32)],
        compiler_params=pltpu.CompilerParams(vmem_limit_bytes=VMEM_LIMIT),
        name="loss_grad",
    )(meta, positives.reshape(pairs, 1), raw)


def contract_rows(left, right):
    return lax.dot_general(
        left, right, (((0,), (0,)), ((), ())), preferred_element_type=jnp.float32
    )


def columns_exchanged(array):
    count = lax.axis_size("dp")
    blocks = jnp.moveaxis(array.reshape(ROWS, count, -1), 1, 0)
    return lax.all_to_all(blocks, "dp", 0, 0, tiled=True).reshape(count * ROWS, -1)


def local(entrance, lengths, positives, norm_gains, query_proj, key_proj, value_proj, out_proj):
    section = lax.axis_index("section")
    member = lax.axis_index("mp")
    blocks = entrance.reshape(MP, BLOCK, D)
    cur = jnp.stack(
        [lax.dynamic_index_in_dim(blocks, (member - k) % MP, 0, False) for k in range(MP)]
    )
    tables = []
    for table in rope_tables():
        table = jnp.asarray(table).reshape(MP, BLOCK, HEAD)
        tables.append(
            jnp.concatenate(
                [lax.dynamic_index_in_dim(table, (member - k) % MP, 0, False) for k in range(MP)]
            )
        )
    gain = norm_gains
    weights = (query_proj[0], key_proj[0], value_proj[0], out_proj[0])

    def meta_for(active):
        return jnp.stack(
            [
                member.astype(jnp.int32),
                (section == active).astype(jnp.int32),
                lengths[0, 0],
                lengths[0, 1],
                lax.axis_index("dp").astype(jnp.int32),
            ]
        )

    metas = [meta_for(s) for s in range(SECTIONS)]
    arrived = None
    for turn in range(SECTIONS - 1):
        cur, parts = forward_turn(metas[turn], cur, arrived, gain, tables, weights, False)
        share = forward_share(cur, scattered(parts, turn))
        arrived = in_slots(sent_on(share, turn, turn + 1))
    cur, (normed, qkv, mixture, pooled, inv) = forward_turn(
        metas[SECTIONS - 1], cur, arrived, gain, tables, weights, True
    )
    group = lax.axis_size("dp") * MP
    raw = lax.all_to_all(
        jnp.broadcast_to(pooled[None], (group, 2, D)), ("dp", "mp"), 0, 0, tiled=True
    ).reshape(2 * group, D)
    losses, gl = loss_and_grad(metas[0], positives, raw)

    inc, arrived = None, None
    for turn in reversed(range(1, SECTIONS)):
        outs = backward_turn(metas[turn], inc, arrived, gl, qkv, tables, weights)
        if arrived is not None:
            inc, parts = outs[0], outs[1:]
        else:
            parts = outs
        share = backward_share(metas[turn], cur, inc, gl, gain, scattered(parts, turn))
        arrived = in_slots(sent_on(share, turn, turn - 1))
    dpart, head_grads, gain_term = backward_turn(
        metas[0], inc, arrived, gl, qkv, tables, weights, cur, inv
    )
    gain_pieces = lax.all_to_all(
        gain_term.reshape(group, 1, D // group), ("dp", "mp"), 0, 0, tiled=True
    )
    gain_share = jnp.sum(gain_pieces, axis=0)
    normed_cols = columns_exchanged(normed)
    mixture_all = lax.all_gather(mixture, "dp", axis=0, tiled=True)
    dpart_cols = columns_exchanged(dpart)
    head_all = lax.all_gather(head_grads, "dp", axis=0, tiled=True)
    sums = contract_rows(normed_cols, head_all)
    out_grad = contract_rows(mixture_all, dpart_cols)
    return (
        losses[:, :WIDTHS],
        gain_share,
        sums[None, :, :QC],
        sums[None, :, QC : QC + KC],
        sums[None, :, QC + KC :],
        out_grad[None],
    )


def solution(mesh):
    in_specs = (
        P("dp", None, None, None),
        P("dp", None),
        P(),
        P("section", None),
        P("section", None, "mp"),
        P("section", None, "mp"),
        P("section", None, "mp"),
        P("section", "mp", None),
    )
    out_specs = (
        P("section", None),
        P("section", ("dp", "mp")),
        P("section", "dp", "mp"),
        P("section", "dp", "mp"),
        P("section", "dp", "mp"),
        P("section", "mp", "dp"),
    )
    return jax.shard_map(local, mesh=mesh, in_specs=in_specs, out_specs=out_specs, check_vma=False)
```

```python
import functools

import jax
import jax.numpy as jnp
import numpy as np
from jax import lax
from jax.experimental import pallas as pl
from jax.experimental.pallas import tpu as pltpu
from jax.sharding import PartitionSpec as P

HEAD = 128
WIDTHS = 7
EPSILON = 1e-05
SOFTMAX_TEMPER = 0.05
ROPE_BASE = 500000.0

LEN = 96
D = 4096
MP = 4
SECTIONS = 4
ROWS = 2 * LEN
BLOCK = ROWS // MP
QC = 512
KC = 128
HEADS = QC // HEAD
CH = 1024
NC = D // CH
SCALE = HEAD**-0.5
BF = jnp.bfloat16
F32 = jnp.float32
VMEM_LIMIT = 16 << 20
COLS = D // 8


def chip_of(section):
    return section // 2


def reduce_pairs(active, shift):
    others = [s for s in range(SECTIONS) if s != active]
    pairs = [(active * MP + j, active * MP + (j + shift) % MP) for j in range(MP)]
    for a, b in zip(others, others[1:] + others[:1]):
        pairs += [(a * MP + j, b * MP + j) for j in range(MP)]
    return pairs


def hop_pairs(source, target, shift):
    pairs = [(source * MP + j, target * MP + (j + shift) % MP) for j in range(MP)]
    others = [s for s in range(SECTIONS) if s not in (source, target)]
    if chip_of(source) == chip_of(target):
        moves = [(target, source), (others[0], others[1]), (others[1], others[0])]
    else:
        near = source ^ 1
        far = target ^ 1
        moves = [(target, far), (far, near), (near, source)]
    for a, b in moves:
        pairs += [(a * MP + j, b * MP + j) for j in range(MP)]
    return pairs


def scattered(parts, active):
    arrived = [
        lax.ppermute(parts[(MP - k) % MP], ("section", "mp"), reduce_pairs(active, k))
        for k in (2, 1, 3)
    ]
    return [parts[0]] + arrived


def sent_on(share, source, target):
    axes = ("section", "mp")
    if chip_of(source) == chip_of(target):
        got = {k: lax.ppermute(share, axes, hop_pairs(source, target, k)) for k in (0, 2, 1, 3)}
    else:
        got = {k: lax.ppermute(share, axes, hop_pairs(source, target, k)) for k in (0, 2)}
        for k in (1, 3):
            got[k] = lax.ppermute(got[0], axes, reduce_pairs(target, k))
    return [got[k] for k in range(MP)]


def rope_tables():
    half = HEAD // 2
    inverse_freq = np.float32(ROPE_BASE) ** (-np.arange(half, dtype=np.float32) * 2.0 / HEAD)
    angles = np.arange(LEN, dtype=np.float32)[:, None] * inverse_freq.astype(np.float32)[None, :]
    cosine, sine = np.cos(angles).astype(np.float32), np.sin(angles).astype(np.float32)
    cosine = np.concatenate([cosine, cosine], axis=1)
    sine = np.concatenate([-sine, sine], axis=1)
    return cosine, sine


def block_of(member, slot):
    return (member - slot) & (MP - 1)


def token_of(member, dim):
    shape = (ROWS, 1) if dim == 0 else (1, ROWS)
    i = lax.broadcasted_iota(jnp.int32, shape, dim)
    slot = (
        (i >= BLOCK).astype(jnp.int32)
        + (i >= 2 * BLOCK).astype(jnp.int32)
        + (i >= 3 * BLOCK).astype(jnp.int32)
    )
    return block_of(member, slot) * BLOCK + i - slot * BLOCK


def dot(a, b, dims):
    return lax.dot_general(a, b, (dims, ((), ())), preferred_element_type=F32)


NN = ((1,), (0,))
NT = ((1,), (1,))
TN = ((0,), (0,))


def in_slot_order(table, member):
    pieces = []
    for k in range(MP):
        start = (block_of(member, k) & 1) * BLOCK
        pieces.append(table[pl.ds(pl.multiple_of(start, BLOCK), BLOCK), :])
    return jnp.concatenate(pieces, axis=0)


def rotated(x, cosine, sine):
    return x * cosine + pltpu.roll(x, HEAD // 2, 1) * sine


def rotated_back(x, cosine, sine):
    return x * cosine - pltpu.roll(x, HEAD // 2, 1) * sine


def attention_mask(member):
    row = token_of(member, 0)
    col = token_of(member, 1)
    first = jnp.where(row >= LEN, LEN, 0)
    return (col <= row) & (col >= first)


def probabilities(query, key, mask):
    scores = dot(query, key, NT) * SCALE
    scores = jnp.where(mask, scores, -1e30)
    top = jnp.max(scores, axis=-1, keepdims=True)
    weights = jnp.exp(scores - top)
    return weights / jnp.sum(weights, axis=-1, keepdims=True)


def slots_at(ref, cols):
    return jnp.concatenate([ref[k, :, cols] for k in range(MP)], axis=0)


def chunk(c):
    return slice(c * CH, (c + 1) * CH)


def valid_tokens(meta, rows):
    token = token_of(meta[0], 1)
    seq = lax.broadcasted_iota(jnp.int32, (rows, ROWS), 0)
    high = jnp.where(seq == 0, meta[2], LEN + meta[3])
    return ((token >= seq * LEN) & (token < high) & (seq < 2)).astype(BF)


def forward_kernel(turn, last, group, *refs):
    refs = list(refs)
    meta, cur = refs[:2]
    refs = refs[2:]
    received = turn > 0
    arrivals = [refs.pop(0) for _ in range(MP)] if received else None
    gain, cos_ref, sin_ref, wq, wk, wv, wo = refs[:7]
    held = refs[7]
    outs = refs[8:]
    member = meta[0]
    if received:

        @pl.when(meta[1] == turn)
        def _():
            for k in range(MP):
                held[k] = arrivals[k][...]

        @pl.when(meta[1] != turn)
        def _():
            for k in range(MP):
                held[k] = cur[k]
    else:
        for k in range(MP):
            held[k] = cur[block_of(member, k)]
    inv = []
    for k in range(MP):
        rows = held[k].astype(F32)
        inv.append(lax.rsqrt(jnp.mean(rows * rows, axis=-1, keepdims=True) + EPSILON))
    inv = jnp.concatenate(inv, axis=0)
    acc_q = jnp.zeros((ROWS, QC), F32)
    acc_k = jnp.zeros((ROWS, KC), F32)
    acc_v = jnp.zeros((ROWS, KC), F32)
    for c in range(NC):
        cols = chunk(c)
        normed = (slots_at(held, cols).astype(F32) * inv * gain[:, cols]).astype(BF)
        if last:
            for b in range(CH // COLS):
                outs[0][c * (CH // COLS) + b] = normed[:, b * COLS : (b + 1) * COLS]
        acc_q += dot(normed, wq[cols, :], NN)
        acc_k += dot(normed, wk[cols, :], NN)
        acc_v += dot(normed, wv[cols, :], NN)
    cosine, sine = in_slot_order(cos_ref, member), in_slot_order(sin_ref, member)
    mask = attention_mask(member)
    key = rotated(acc_k, cosine, sine).astype(BF)
    value = acc_v.astype(BF)
    mixed = []
    for j in range(HEADS):
        cols = slice(j * HEAD, (j + 1) * HEAD)
        query = rotated(acc_q[:, cols], cosine, sine).astype(BF)
        if last:
            outs[1][:, cols] = query
        weights = probabilities(query, key, mask).astype(BF)
        mixed.append(dot(weights, value, NN).astype(BF))
    mixed = jnp.concatenate(mixed, axis=1)
    if not last:
        for c in range(NC):
            cols = chunk(c)
            part = dot(mixed, wo[:, cols], NN).astype(BF)
            for k in range(MP):
                outs[k][:, cols] = part[k * BLOCK : (k + 1) * BLOCK]
        return
    qkv_out, mix_out, pool_out = outs[1:4]
    qkv_out[:, QC : QC + KC] = key
    qkv_out[:, QC + KC :] = value
    mix_out[...] = mixed
    pool = valid_tokens(meta, 8)
    row = lax.broadcasted_iota(jnp.int32, (8, 1), 0)
    count = jnp.where(row == 0, meta[2], meta[3]).astype(F32)
    total = dot(pool, mixed, NN)
    top = total.astype(BF)
    low = (total - top.astype(F32)).astype(BF)
    pieces = []
    for c in range(NC):
        cols = chunk(c)
        pooled = dot(top, wo[:, cols], NN) + dot(low, wo[:, cols], NN)
        pooled = pooled + dot(pool, slots_at(held, cols), NN) * (1.0 / MP)
        pieces.append(pooled / count)
    rows = []
    for seq in range(2):
        for c in range(NC):
            for b in range(CH // COLS):
                rows.append(pieces[c][seq : seq + 1, b * COLS : (b + 1) * COLS])
    pooled = jnp.concatenate(rows, axis=0).astype(BF)
    for j in range(group):
        pool_out[j] = pooled


def call(kernel, in_count, out_shape, name, scratch=()):
    vmem = pl.BlockSpec(memory_space=pltpu.VMEM)
    return pl.pallas_call(
        kernel,
        in_specs=[pl.BlockSpec(memory_space=pltpu.SMEM)] + [vmem] * (in_count - 1),
        out_specs=jax.tree.map(lambda _: vmem, out_shape),
        out_shape=out_shape,
        scratch_shapes=list(scratch),
        compiler_params=pltpu.CompilerParams(vmem_limit_bytes=VMEM_LIMIT),
        name=name,
    )


def shaped(*dims, dtype=BF):
    return jax.ShapeDtypeStruct(dims, dtype)


def forward_turn(turn, meta, cur, arrivals, gain, tables, weights, last, group):
    operands = [meta, cur] + list(arrivals or []) + [gain, *tables, *weights]
    out_shape = [shaped(MP, BLOCK, D)]
    if last:
        out_shape += [
            shaped(D // COLS, ROWS, COLS),
            shaped(ROWS, QC + 2 * KC),
            shaped(ROWS, QC),
            shaped(group, 2 * D // COLS, COLS),
        ]
    else:
        out_shape += [shaped(BLOCK, D)] * MP
    outs = call(
        functools.partial(forward_kernel, turn, last, group),
        len(operands),
        out_shape,
        "forward_last" if last else "forward_turn",
    )(*operands)
    return outs[0], outs[1:]


def slot_grad(meta, gl, slot, cols):
    block = block_of(meta[0], slot)
    seq = block >> 1
    token = (block & 1) * BLOCK + lax.broadcasted_iota(jnp.int32, (BLOCK, 1), 0)
    valid = (token < meta[2 + seq]).astype(F32)
    return valid * gl[pl.ds(seq, 1), cols]


def backward_kernel(turn, received, carried, last, *refs):
    refs = list(refs)
    meta = refs.pop(0)
    inc = refs.pop(0) if carried else None
    arrivals = [refs.pop(0) for _ in range(MP)] if received else None
    gl, qkv, cos_ref, sin_ref, wq, wk, wv, wo = refs[:8]
    refs = refs[8:]
    member = meta[0]
    if last:
        dpart_out, grads, held = refs
    else:
        held = refs.pop(0) if received else None
        part_refs, grads = refs[:MP], refs[MP]
    if received:

        @pl.when(meta[1] == turn)
        def _():
            for k in range(MP):
                held[k] = arrivals[k][...]

        @pl.when(meta[1] != turn)
        def _():
            for k in range(MP):
                held[k] = inc[k] if carried else jnp.zeros((BLOCK, D), BF)

    acc = jnp.zeros((ROWS, QC), F32)
    for c in range(NC):
        cols = chunk(c)
        rows = []
        for k in range(MP):
            grad = slot_grad(meta, gl, k, cols)
            if received:
                grad = grad + held[k, :, cols].astype(F32)
            rows.append(grad.astype(BF))
        dpart = jnp.concatenate(rows, axis=0)
        if last:
            for b in range(CH // COLS):
                dpart_out[c * (CH // COLS) + b] = dpart[:, b * COLS : (b + 1) * COLS]
        acc += dot(dpart, wo[:, cols], NT)
    cosine, sine = in_slot_order(cos_ref, member), in_slot_order(sin_ref, member)
    mask = attention_mask(member)
    key = qkv[:, QC : QC + KC]
    value = qkv[:, QC + KC :]
    dkey = jnp.zeros((ROWS, HEAD), F32)
    dvalue = jnp.zeros((ROWS, HEAD), F32)
    for j in range(HEADS):
        cols = slice(j * HEAD, (j + 1) * HEAD)
        query = qkv[:, cols]
        dmix = acc[:, cols].astype(BF)
        weights = probabilities(query, key, mask)
        dvalue += dot(weights.astype(BF), dmix, TN)
        dweights = dot(dmix, value, NT).astype(BF).astype(F32)
        moved = weights * dweights
        dscores = (moved - weights * jnp.sum(moved, axis=-1, keepdims=True)) * SCALE
        dscores = dscores.astype(BF)
        dquery = dot(dscores, key, NN).astype(BF).astype(F32)
        grads[:, cols] = rotated_back(dquery, cosine, sine).astype(BF)
        dkey += dot(dscores, query, TN)
    dkey = dkey.astype(BF).astype(F32)
    grads[:, QC : QC + KC] = rotated_back(dkey, cosine, sine).astype(BF)
    grads[:, QC + KC :] = dvalue.astype(BF)
    if last:
        return
    for c in range(NC):
        cols = chunk(c)
        dnormed = dot(grads[:, :QC], wq[cols, :], NT)
        dnormed += dot(grads[:, QC : QC + KC], wk[cols, :], NT)
        dnormed += dot(grads[:, QC + KC :], wv[cols, :], NT)
        dnormed = dnormed.astype(BF)
        for k in range(MP):
            part_refs[k][:, cols] = dnormed[k * BLOCK : (k + 1) * BLOCK]


def backward_turn(turn, meta, inc, arrivals, gl, qkv, tables, weights, last):
    received = arrivals is not None
    carried = inc is not None
    operands = [meta] + ([inc] if carried else []) + list(arrivals or [])
    operands += [gl, qkv, *tables, *weights]
    if last:
        out_shape = [shaped(D // COLS, ROWS, COLS), shaped(ROWS, QC + 2 * KC)]
        scratch = [pltpu.VMEM((MP, BLOCK, D), BF)]
    else:
        out_shape = ([shaped(MP, BLOCK, D)] if received else []) + [shaped(BLOCK, D)] * MP
        scratch = [pltpu.VMEM((ROWS, QC + 2 * KC), BF)]
    return call(
        functools.partial(backward_kernel, turn, received, carried, last),
        len(operands),
        out_shape,
        "backward_last" if last else "backward_turn",
        scratch,
    )(*operands)


def summed(parts, cols):
    total = parts[0][:, cols].astype(F32)
    for part in parts[1:]:
        total = total + part[:, cols].astype(F32)
    return total


def forward_share_kernel(meta, hidden, p0, p1, p2, p3, out):
    for c in range(NC):
        cols = chunk(c)
        total = summed((p0, p1, p2, p3), cols)
        out[:, cols] = (hidden[0, :, cols].astype(F32) + total).astype(BF)


def forward_share(meta, cur, parts):
    return call(forward_share_kernel, 6, shaped(BLOCK, D), "forward_share")(meta, cur, *parts)


def backward_share_kernel(received, *refs):
    refs = list(refs)
    meta, hidden = refs.pop(0), refs.pop(0)
    inc = refs.pop(0) if received else None
    gl, gain, p0, p1, p2, p3, out, scaled = refs
    square = jnp.zeros((BLOCK, 1), F32)
    along = jnp.zeros((BLOCK, 1), F32)
    for c in range(NC):
        cols = chunk(c)
        rows = hidden[0, :, cols].astype(F32)
        dnormed = summed((p0, p1, p2, p3), cols) * gain[:, cols]
        scaled[:, cols] = dnormed
        square += jnp.sum(rows * rows, axis=-1, keepdims=True)
        along += jnp.sum(dnormed * rows, axis=-1, keepdims=True)
    inv = lax.rsqrt(square / D + EPSILON)
    pull = inv * inv * inv * (along / D)
    for c in range(NC):
        cols = chunk(c)
        upstream = slot_grad(meta, gl, 0, cols)
        if received:
            upstream = upstream + inc[0, :, cols].astype(F32)
        rows = hidden[0, :, cols].astype(F32)
        out[:, cols] = (upstream + inv * scaled[:, cols] - rows * pull).astype(BF)


def backward_share(meta, cur, inc, gl, gain, parts):
    received = inc is not None
    operands = [meta, cur] + ([inc] if received else []) + [gl, gain, *parts]
    return call(
        functools.partial(backward_share_kernel, received),
        len(operands),
        shaped(BLOCK, D),
        "backward_share",
        [pltpu.VMEM((BLOCK, D), F32)],
    )(*operands)


def precise(a, b, dims):
    return lax.dot_general(
        a, b, (dims, ((), ())), precision=lax.Precision.HIGHEST, preferred_element_type=F32
    )


def loss_kernel(pairs, meta, positives, raw, losses, gl):
    group, lines, width_of = raw.shape
    every = raw[...].reshape(group * lines, width_of)
    shape = (lines * pairs, group * lines)
    row = lax.broadcasted_iota(jnp.int32, shape, 0)
    col = lax.broadcasted_iota(jnp.int32, shape, 1)
    pick = (col // (lines * MP) == row % pairs) & (col % lines == row // pairs)
    gathered = dot(pick.astype(BF), every, NN)
    half = lines // 2

    def joined(seq):
        start = seq * half * pairs
        pieces = [gathered[start + c * pairs : start + (c + 1) * pairs] for c in range(half)]
        return jnp.concatenate(pieces, axis=1)

    q, z = joined(0), joined(1)
    eye = (
        lax.broadcasted_iota(jnp.int32, (pairs, pairs), 0)
        == lax.broadcasted_iota(jnp.int32, (pairs, pairs), 1)
    ).astype(F32)
    target = (lax.broadcasted_iota(jnp.int32, (pairs, pairs), 1) == positives[...]).astype(F32)
    narrow = D // 2 ** (WIDTHS - 1)
    lane = lax.broadcasted_iota(jnp.int32, (1, 2 * narrow), 1) < narrow

    def block(x, b):
        if b == WIDTHS - 1:
            return jnp.where(lane, x[:, : 2 * narrow], 0.0)
        if b == WIDTHS - 2:
            return jnp.where(lane, 0.0, x[:, : 2 * narrow])
        return x[:, D // 2 ** (b + 1) : D // 2**b]

    gram = [None] * WIDTHS
    sq = [None] * WIDTHS
    sz = [None] * WIDTHS
    total = (jnp.zeros((pairs, pairs), F32), jnp.zeros((pairs, 1), F32), jnp.zeros((pairs, 1), F32))
    for b in reversed(range(WIDTHS)):
        qb, zb = block(q, b), block(z, b)
        total = (
            total[0] + precise(qb, zb, NT),
            total[1] + jnp.sum(qb * qb, axis=-1, keepdims=True),
            total[2] + jnp.sum(zb * zb, axis=-1, keepdims=True),
        )
        gram[b], sq[b], sz[b] = total
    cross = jnp.zeros((pairs, pairs), F32)
    pull_q = jnp.zeros((pairs, 1), F32)
    pull_z = jnp.zeros((pairs, 1), F32)
    own = (lax.broadcasted_iota(jnp.int32, (pairs, 1), 0) == meta[4]).astype(F32)
    out_lane = lax.broadcasted_iota(jnp.int32, (1, 128), 1)
    loss_row = jnp.zeros((1, 128), F32)

    def flat(column):
        return jnp.sum(column * eye, axis=0, keepdims=True)

    for b in range(WIDTHS):
        width = D // 2**b
        inv_q = lax.rsqrt(sq[b] / width + 1e-06)
        inv_z = lax.rsqrt(sz[b] / width + 1e-06)
        inv_z_row = flat(inv_z)
        weight = inv_q * inv_z_row / (width * SOFTMAX_TEMPER)
        scores = gram[b] * weight
        top = jnp.max(scores, axis=-1, keepdims=True)
        raised = jnp.exp(scores - top)
        norm = jnp.sum(raised, axis=-1, keepdims=True)
        each = jnp.log(norm) + top - jnp.sum(scores * target, axis=-1, keepdims=True)
        loss_row = loss_row + jnp.where(
            out_lane == b, jnp.sum(each, axis=0, keepdims=True) / pairs, 0.0
        )
        dscores = (raised / norm - target) / pairs
        cross = cross + dscores * weight
        ds = dscores * scores
        pull_q = pull_q + jnp.sum(ds, axis=-1, keepdims=True) * inv_q * inv_q / width
        ds_z = jnp.sum(jnp.sum(ds, axis=0, keepdims=True) * eye, axis=-1, keepdims=True)
        pull_z = pull_z + ds_z * inv_z * inv_z / width
        qb, zb = block(q, b), block(z, b)
        dq = precise(cross, zb, NN) - pull_q * qb
        dz = precise(cross, qb, TN) - pull_z * zb
        dq = jnp.sum(dq * own, axis=0, keepdims=True) / meta[2].astype(F32)
        dz = jnp.sum(dz * own, axis=0, keepdims=True) / meta[3].astype(F32)
        if b == WIDTHS - 2:
            held_q, held_z = dq, dz
        elif b == WIDTHS - 1:
            gl[0:1, : 2 * narrow] = jnp.where(lane, dq, held_q)
            gl[1:2, : 2 * narrow] = jnp.where(lane, dz, held_z)
        else:
            gl[0:1, width // 2 : width] = dq
            gl[1:2, width // 2 : width] = dz
    losses[...] = loss_row


def loss_and_grad(meta, positives, raw):
    pairs = positives.shape[0]
    return call(
        functools.partial(loss_kernel, pairs),
        3,
        [shaped(1, 128, dtype=F32), shaped(2, D, dtype=F32)],
        "loss_grad",
    )(meta, positives.reshape(pairs, 1), raw)


def weight_kernel(count, *refs):
    refs = list(refs)
    meta, normed = refs[:2]
    pieces = refs[2 : 2 + count]
    gain, wq, wk, wv, dq, dk, dv, scale_out, row_scr = refs[2 + count :]
    place = meta[4]
    total = None
    for k in range(count):
        block = (place - k) & (count - 1)
        term = dot(normed[block], pieces[k][...], NN)
        total = term if total is None else total + term
    dq[...] = total[:, :QC]
    dk[...] = total[:, QC : QC + KC]
    dv[...] = total[:, QC + KC :]
    rows = pl.ds(pl.multiple_of(place * COLS, COLS), COLS)
    ones = jnp.ones((8, QC), F32)
    scale = precise(ones, total[:, :QC] * wq[rows, :].astype(F32), NT)
    kv = total[:, QC : QC + KC] * wk[rows, :].astype(F32)
    kv = kv + total[:, QC + KC :] * wv[rows, :].astype(F32)
    scale = scale + precise(ones[:, :KC], kv, NT)
    row_scr[...] = scale[0:1] / gain[:, rows]
    for k in range(MP):
        at = pl.multiple_of(((meta[0] + k) & (MP - 1)) * 128, 128)
        scale_out[k] = row_scr[:, pl.ds(at, 128)]


def weight_grads(meta, normed, pieces, gain, wq, wk, wv):
    count = len(pieces)
    return call(
        functools.partial(weight_kernel, count),
        6 + count,
        [
            shaped(COLS, QC, dtype=F32),
            shaped(COLS, KC, dtype=F32),
            shaped(COLS, KC, dtype=F32),
            shaped(MP, 1, 128, dtype=F32),
        ],
        "weight_grads",
        [pltpu.VMEM((1, COLS), F32)],
    )(meta, normed, *pieces, gain, wq, wk, wv)


def out_kernel(meta, mixed, dpart, out):
    total = None
    for j in range(mixed.shape[0]):
        term = dot(mixed[j], dpart[j], NN)
        total = term if total is None else total + term
    out[...] = total


def out_grads(meta, mixed, dpart):
    return call(out_kernel, 3, shaped(QC, COLS, dtype=F32), "out_grads")(meta, mixed, dpart)


def local(entrance, lengths, positives, norm_gains, query_proj, key_proj, value_proj, out_proj):
    count = lax.axis_size("dp")
    group = count * MP
    gain = norm_gains
    weights = (query_proj[0], key_proj[0], value_proj[0], out_proj[0])
    tables = [jnp.asarray(table) for table in rope_tables()]
    places = [lax.axis_index(name).astype(jnp.int32) for name in ("mp", "section", "dp")]
    meta = jnp.stack([places[0], places[1], lengths[0, 0], lengths[0, 1], places[2]])

    cur = entrance.reshape(MP, BLOCK, D)
    arrived = None
    for turn in range(SECTIONS - 1):
        cur, parts = forward_turn(turn, meta, cur, arrived, gain, tables, weights, False, group)
        share = forward_share(meta, cur, scattered(parts, turn))
        arrived = sent_on(share, turn, turn + 1)
    cur, (normed, qkv, mixture, pooled) = forward_turn(
        SECTIONS - 1, meta, cur, arrived, gain, tables, weights, True, group
    )
    raw = lax.all_to_all(pooled, ("dp", "mp"), 0, 0, tiled=True)
    losses, gl = loss_and_grad(meta, positives, raw)

    inc, arrived = None, None
    for turn in reversed(range(1, SECTIONS)):
        outs = backward_turn(turn, meta, inc, arrived, gl, qkv, tables, weights, False)
        if arrived is not None:
            inc, parts = outs[0], outs[1:]
        else:
            parts = outs
        share = backward_share(meta, cur, inc, gl, gain, scattered(parts, turn))
        if turn == SECTIONS - 1:
            share, normed, mixture = lax.optimization_barrier((share, normed, mixture))
            arrived = sent_on(share, turn, turn - 1)
            mixed = lax.all_gather(mixture, "dp", axis=0)
            mixed = jnp.swapaxes(mixed, 1, 2)
            normed = jnp.swapaxes(lax.all_to_all(normed, "dp", 0, 0, tiled=True), 1, 2)
        else:
            arrived = sent_on(share, turn, turn - 1)
    *arrived, mixed, normed = lax.optimization_barrier((*arrived, mixed, normed))
    dpart, grads = backward_turn(0, meta, inc, arrived, gl, qkv, tables, weights, True)
    pieces = [grads]
    for k in range(1, count):
        pairs = [(j, (j + k) % count) for j in range(count)]
        pieces.append(lax.ppermute(grads, "dp", pairs))
    dpart = lax.all_to_all(dpart, "dp", 0, 0, tiled=True)
    dq, dk, dv, scales = weight_grads(meta, normed, pieces, gain, *weights[:3])
    scale = scales[0]
    for k in range(1, MP):
        pairs = [(j, (j + k) % MP) for j in range(MP)]
        scale = scale + lax.ppermute(scales[k], "mp", pairs)
    out_grad = out_grads(meta, mixed, dpart)
    return (losses[:, :WIDTHS], scale, dq[None], dk[None], dv[None], out_grad[None])


def solution(mesh):
    in_specs = (
        P("dp", None, None, None),
        P("dp", None),
        P(),
        P("section", None),
        P("section", None, "mp"),
        P("section", None, "mp"),
        P("section", None, "mp"),
        P("section", "mp", None),
    )
    out_specs = (
        P("section", None),
        P("section", ("dp", "mp")),
        P("section", "dp", "mp"),
        P("section", "dp", "mp"),
        P("section", "dp", "mp"),
        P("section", "mp", "dp"),
    )
    return jax.shard_map(local, mesh=mesh, in_specs=in_specs, out_specs=out_specs, check_vma=False)
```

```python
import functools

import jax
import jax.numpy as jnp
import numpy as np
from jax import lax
from jax.experimental import pallas as pl
from jax.experimental.pallas import tpu as pltpu
from jax.sharding import PartitionSpec as P

HEAD = 128
WIDTHS = 7
EPSILON = 1e-05
SOFTMAX_TEMPER = 0.05
ROPE_BASE = 500000.0

LEN = 96
D = 4096
MP = 4
SECTIONS = 4
ROWS = 2 * LEN
BLOCK = ROWS // MP
QC = 512
KC = 128
HEADS = QC // HEAD
CH = 1024
NC = D // CH
SCALE = HEAD**-0.5
BF = jnp.bfloat16
F32 = jnp.float32
VMEM_LIMIT = 16 << 20
DP = 8
COLS = D // DP


def chip_of(section):
    return section // 2


def reduce_pairs(active, shift):
    pairs = []
    for s in range(SECTIONS):
        for j in range(MP):
            if s % 2 == active % 2:
                pairs.append((s * MP + j, s * MP + (j + shift) % MP))
            else:
                pairs.append((s * MP + j, (s ^ 2) * MP + j))
    return pairs


def hop_pairs(source, target, shift):
    hops = [(source, target)]
    if chip_of(source) == chip_of(target):
        hops.append((source ^ 2, target ^ 2))
    return [(a * MP + j, b * MP + (j + shift) % MP) for a, b in sorted(hops) for j in range(MP)]


def scattered(parts, active):
    arrived = [
        lax.ppermute(parts[(MP - k) % MP], ("section", "mp"), reduce_pairs(active, k))
        for k in (2, 1, 3)
    ]
    return [parts[0]] + arrived


def sent_on(share, source, target):
    axes = ("section", "mp")
    got = {k: lax.ppermute(share, axes, hop_pairs(source, target, k)) for k in (0, 1, 3)}
    if chip_of(source) == chip_of(target):
        got[2] = lax.ppermute(share, axes, hop_pairs(source, target, 2))
    else:
        got[2] = lax.ppermute(got[0], axes, reduce_pairs(target, 2))
    return [got[k] for k in range(MP)]


def rope_tables():
    half = HEAD // 2
    inverse_freq = np.float32(ROPE_BASE) ** (-np.arange(half, dtype=np.float32) * 2.0 / HEAD)
    angles = np.arange(LEN, dtype=np.float32)[:, None] * inverse_freq.astype(np.float32)[None, :]
    cosine, sine = np.cos(angles).astype(np.float32), np.sin(angles).astype(np.float32)
    cosine = np.concatenate([cosine, cosine], axis=1)
    sine = np.concatenate([-sine, sine], axis=1)
    return np.stack([cosine, sine])


def block_of(member, slot):
    return (member - slot) & (MP - 1)


def token_of(member, dim):
    shape = (ROWS, 1) if dim == 0 else (1, ROWS)
    i = lax.broadcasted_iota(jnp.int32, shape, dim)
    slot = (
        (i >= BLOCK).astype(jnp.int32)
        + (i >= 2 * BLOCK).astype(jnp.int32)
        + (i >= 3 * BLOCK).astype(jnp.int32)
    )
    return block_of(member, slot) * BLOCK + i - slot * BLOCK


def dot(a, b, dims):
    return lax.dot_general(a, b, (dims, ((), ())), preferred_element_type=F32)


NN = ((1,), (0,))
NT = ((1,), (1,))
TN = ((0,), (0,))


def in_slot_order(tables, member):
    ordered = []
    for t in range(2):
        pieces = []
        for k in range(MP):
            start = (block_of(member, k) & 1) * BLOCK
            pieces.append(tables[t, pl.ds(pl.multiple_of(start, BLOCK), BLOCK), :])
        ordered.append(jnp.concatenate(pieces, axis=0))
    return ordered


def rotated(x, cosine, sine):
    return x * cosine + pltpu.roll(x, HEAD // 2, 1) * sine


def rotated_back(x, cosine, sine):
    return x * cosine - pltpu.roll(x, HEAD // 2, 1) * sine


def attention_mask(member):
    row = token_of(member, 0)
    col = token_of(member, 1)
    first = jnp.where(row >= LEN, LEN, 0)
    return (col <= row) & (col >= first)


def probabilities(query, key, mask):
    scores = dot(query, key, NT) * SCALE
    scores = jnp.where(mask, scores, -1e30)
    top = jnp.max(scores, axis=-1, keepdims=True)
    weights = jnp.exp(scores - top)
    return weights / jnp.sum(weights, axis=-1, keepdims=True)


def slots_at(ref, cols):
    return jnp.concatenate([ref[k, :, cols] for k in range(MP)], axis=0)


def chunk(c):
    return slice(c * CH, (c + 1) * CH)


def valid_tokens(meta, rows):
    token = token_of(meta[0], 1)
    seq = lax.broadcasted_iota(jnp.int32, (rows, ROWS), 0)
    high = jnp.where(seq == 0, meta[2], LEN + meta[3])
    return ((token >= seq * LEN) & (token < high) & (seq < 2)).astype(BF)


def sent_cols(meta, k):
    block = meta[4] ^ k
    return pl.ds(pl.multiple_of(block * COLS, COLS), COLS)


def forward_kernel(turn, last, *refs):
    refs = list(refs)
    meta, cur = refs[:2]
    refs = refs[2:]
    received = turn > 0
    arrivals = [refs.pop(0) for _ in range(MP)] if received else None
    if received:
        gain, tables, wq, wk, wv, wo = refs[:6]
        held = refs[6]
        outs = refs[7:]
        if last:
            *sent, qkv_out, pool_out, normed_scr = outs
    else:
        stored = refs[:6]
        held = refs[6]
        outs = refs[7 : 7 + MP]
        gain, tables, wq, wk, wv, wo = refs[7 + MP : 13 + MP]
        sems = refs[13 + MP]
    member = meta[0]
    if received:

        @pl.when(meta[1] == turn)
        def _():
            for k in range(MP):
                held[k] = arrivals[k][...]

        @pl.when(meta[1] != turn)
        def _():
            for k in range(MP):
                held[k] = cur[k]
    else:
        copies = [
            pltpu.make_async_copy(cur.at[block_of(member, k)], held.at[k], sems.at[k])
            for k in range(MP)
        ]
        copies += [
            pltpu.make_async_copy(stored[i], kept, sems.at[MP + i])
            for i, kept in enumerate((gain, tables))
        ]
        small = len(copies)
        for c in range(NC):
            for i, kept in ((2, wq), (3, wk), (4, wv)):
                copies.append(
                    pltpu.make_async_copy(
                        stored[i].at[chunk(c), :], kept.at[chunk(c), :], sems.at[len(copies)]
                    )
                )
        copies.append(pltpu.make_async_copy(stored[5], wo, sems.at[len(copies)]))
        for copy in copies:
            copy.start()
        for copy in copies[:small]:
            copy.wait()
    inv = []
    for k in range(MP):
        rows = held[k].astype(F32)
        inv.append(lax.rsqrt(jnp.mean(rows * rows, axis=-1, keepdims=True) + EPSILON))
    inv = jnp.concatenate(inv, axis=0)
    acc_q = jnp.zeros((ROWS, QC), F32)
    acc_k = jnp.zeros((ROWS, KC), F32)
    acc_v = jnp.zeros((ROWS, KC), F32)
    for c in range(NC):
        cols = chunk(c)
        if not received:
            for copy in copies[small + 3 * c : small + 3 * c + 3]:
                copy.wait()
        normed = (slots_at(held, cols).astype(F32) * inv * gain[:, cols]).astype(BF)
        if last:
            normed_scr[:, cols] = normed
        acc_q += dot(normed, wq[cols, :], NN)
        acc_k += dot(normed, wk[cols, :], NN)
        acc_v += dot(normed, wv[cols, :], NN)
    cosine, sine = in_slot_order(tables, member)
    mask = attention_mask(member)
    key = rotated(acc_k, cosine, sine).astype(BF)
    value = acc_v.astype(BF)
    mixed = []
    for j in range(HEADS):
        cols = slice(j * HEAD, (j + 1) * HEAD)
        query = rotated(acc_q[:, cols], cosine, sine).astype(BF)
        if last:
            qkv_out[:, cols] = query
        weights = probabilities(query, key, mask).astype(BF)
        mixed.append(dot(weights, value, NN).astype(BF))
    mixed = jnp.concatenate(mixed, axis=1)
    if not last:
        if not received:
            copies[-1].wait()
        for c in range(NC):
            cols = chunk(c)
            part = dot(mixed, wo[:, cols], NN).astype(BF)
            for k in range(MP):
                outs[k][:, cols] = part[k * BLOCK : (k + 1) * BLOCK]
        return
    qkv_out[:, QC : QC + KC] = key
    qkv_out[:, QC + KC :] = value
    for k, out in enumerate(sent):
        out[:ROWS, :] = normed_scr[:, sent_cols(meta, k)]
        out[ROWS:, :] = mixed
    pool = valid_tokens(meta, 8)
    row = lax.broadcasted_iota(jnp.int32, (8, 1), 0)
    count = jnp.where(row == 0, meta[2], meta[3]).astype(F32)
    total = dot(pool, mixed, NN)
    top = total.astype(BF)
    low = (total - top.astype(F32)).astype(BF)
    pieces = []
    for c in range(NC):
        cols = chunk(c)
        pooled = dot(top, wo[:, cols], NN) + dot(low, wo[:, cols], NN)
        pooled = pooled + dot(pool, slots_at(held, cols), NN) * (1.0 / MP)
        pieces.append(pooled / count)
    rows = []
    for seq in range(2):
        for c in range(NC):
            for b in range(CH // COLS):
                rows.append(pieces[c][seq : seq + 1, b * COLS : (b + 1) * COLS])
    pool_out[...] = jnp.concatenate(rows, axis=0).astype(BF)


def call(kernel, in_count, out_shape, name, scratch=(), stored=False):
    vmem = pl.BlockSpec(memory_space=pltpu.VMEM)
    source = pl.BlockSpec(memory_space=pl.ANY) if stored else vmem
    return pl.pallas_call(
        kernel,
        in_specs=[pl.BlockSpec(memory_space=pltpu.SMEM)] + [source] * (in_count - 1),
        out_specs=jax.tree.map(lambda _: vmem, out_shape),
        out_shape=out_shape,
        scratch_shapes=list(scratch),
        compiler_params=pltpu.CompilerParams(vmem_limit_bytes=VMEM_LIMIT),
        name=name,
    )


def shaped(*dims, dtype=BF):
    return jax.ShapeDtypeStruct(dims, dtype)


def kept(*dims, dtype=BF):
    return pltpu.VMEM(dims, dtype)


def forward_turn(turn, meta, cur, arrivals, gain, tables, weights, last):
    operands = [meta, cur] + list(arrivals or []) + [gain, tables, *weights]
    out_shape = [kept(MP, BLOCK, D)]
    scratch = ()
    if last:
        out_shape += [shaped(2 * ROWS, COLS)] * DP
        out_shape += [shaped(ROWS, QC + 2 * KC), shaped(2 * D // COLS, COLS)]
        scratch = [pltpu.VMEM((ROWS, D), BF)]
    else:
        out_shape += [shaped(BLOCK, D)] * MP
    if turn == 0:
        for array in operands[2:]:
            out_shape.append(kept(*array.shape, dtype=array.dtype))
        scratch = [pltpu.SemaphoreType.DMA((MP + 2 + 3 * NC + 1,))]
    if turn == 0:
        operands[1:] = [pltpu.with_memory_space_constraint(x, pltpu.HBM) for x in operands[1:]]
    outs = call(
        functools.partial(forward_kernel, turn, last),
        len(operands),
        out_shape,
        "forward_last" if last else "forward_turn",
        scratch,
        turn == 0,
    )(*operands)
    return outs[0], outs[1:]


def slot_grad(meta, gl, slot, cols):
    block = block_of(meta[0], slot)
    seq = block >> 1
    token = (block & 1) * BLOCK + lax.broadcasted_iota(jnp.int32, (BLOCK, 1), 0)
    valid = (token < meta[2 + seq]).astype(F32)
    return valid * gl[pl.ds(seq, 1), cols]


def backward_kernel(turn, received, carried, last, *refs):
    refs = list(refs)
    meta = refs.pop(0)
    inc = refs.pop(0) if carried else None
    arrivals = [refs.pop(0) for _ in range(MP)] if received else None
    gl, qkv, tables, wq, wk, wv, wo = refs[:7]
    refs = refs[7:]
    member = meta[0]
    if last:
        grads, *sent = refs[: 1 + DP]
        held, dpart_scr = refs[1 + DP :]
    else:
        held = refs.pop(0) if received else None
        part_refs, grads = refs[:MP], refs[MP]
    if received:

        @pl.when(meta[1] == turn)
        def _():
            for k in range(MP):
                held[k] = arrivals[k][...]

        @pl.when(meta[1] != turn)
        def _():
            for k in range(MP):
                held[k] = inc[k] if carried else jnp.zeros((BLOCK, D), BF)

    acc = jnp.zeros((ROWS, QC), F32)
    for c in range(NC):
        cols = chunk(c)
        rows = []
        for k in range(MP):
            grad = slot_grad(meta, gl, k, cols)
            if received:
                grad = grad + held[k, :, cols].astype(F32)
            rows.append(grad.astype(BF))
        dpart = jnp.concatenate(rows, axis=0)
        if last:
            dpart_scr[:, cols] = dpart[:BLOCK]
        acc += dot(dpart, wo[:, cols], NT)
    cosine, sine = in_slot_order(tables, member)
    mask = attention_mask(member)
    key = qkv[:, QC : QC + KC]
    value = qkv[:, QC + KC :]
    dkey = jnp.zeros((ROWS, HEAD), F32)
    dvalue = jnp.zeros((ROWS, HEAD), F32)
    for j in range(HEADS):
        cols = slice(j * HEAD, (j + 1) * HEAD)
        query = qkv[:, cols]
        dmix = acc[:, cols].astype(BF)
        weights = probabilities(query, key, mask)
        dvalue += dot(weights.astype(BF), dmix, TN)
        dweights = dot(dmix, value, NT).astype(BF).astype(F32)
        moved = weights * dweights
        dscores = (moved - weights * jnp.sum(moved, axis=-1, keepdims=True)) * SCALE
        dscores = dscores.astype(BF)
        dquery = dot(dscores, key, NN).astype(BF).astype(F32)
        grads[:, cols] = rotated_back(dquery, cosine, sine).astype(BF)
        dkey += dot(dscores, query, TN)
    dkey = dkey.astype(BF).astype(F32)
    grads[:, QC : QC + KC] = rotated_back(dkey, cosine, sine).astype(BF)
    grads[:, QC + KC :] = dvalue.astype(BF)
    if last:
        for k, out in enumerate(sent):
            out[...] = dpart_scr[:, sent_cols(meta, k)]
        return
    for c in range(NC):
        cols = chunk(c)
        dnormed = dot(grads[:, :QC], wq[cols, :], NT)
        dnormed += dot(grads[:, QC : QC + KC], wk[cols, :], NT)
        dnormed += dot(grads[:, QC + KC :], wv[cols, :], NT)
        dnormed = dnormed.astype(BF)
        for k in range(MP):
            part_refs[k][:, cols] = dnormed[k * BLOCK : (k + 1) * BLOCK]


def backward_turn(turn, meta, inc, arrivals, gl, qkv, tables, weights, last):
    received = arrivals is not None
    carried = inc is not None
    operands = [meta] + ([inc] if carried else []) + list(arrivals or [])
    operands += [gl, qkv, tables, *weights]
    if last:
        out_shape = [shaped(ROWS, QC + 2 * KC)] + [shaped(BLOCK, COLS)] * DP
        scratch = [pltpu.VMEM((MP, BLOCK, D), BF), pltpu.VMEM((BLOCK, D), BF)]
    else:
        out_shape = ([kept(MP, BLOCK, D)] if received else []) + [shaped(BLOCK, D)] * MP
        scratch = [pltpu.VMEM((ROWS, QC + 2 * KC), BF)]
    return call(
        functools.partial(backward_kernel, turn, received, carried, last),
        len(operands),
        out_shape,
        "backward_last" if last else "backward_turn",
        scratch,
    )(*operands)


def summed(parts, cols):
    total = parts[0][:, cols].astype(F32)
    for part in parts[1:]:
        total = total + part[:, cols].astype(F32)
    return total


def forward_share_kernel(meta, hidden, p0, p1, p2, p3, out):
    for c in range(NC):
        cols = chunk(c)
        total = summed((p0, p1, p2, p3), cols)
        out[:, cols] = (hidden[0, :, cols].astype(F32) + total).astype(BF)


def forward_share(meta, cur, parts):
    return call(forward_share_kernel, 6, shaped(BLOCK, D), "forward_share")(meta, cur, *parts)


def backward_share_kernel(received, *refs):
    refs = list(refs)
    meta, hidden = refs.pop(0), refs.pop(0)
    inc = refs.pop(0) if received else None
    gl, gain, p0, p1, p2, p3, out, scaled = refs
    square = jnp.zeros((BLOCK, 1), F32)
    along = jnp.zeros((BLOCK, 1), F32)
    for c in range(NC):
        cols = chunk(c)
        rows = hidden[0, :, cols].astype(F32)
        dnormed = summed((p0, p1, p2, p3), cols) * gain[:, cols]
        scaled[:, cols] = dnormed
        square += jnp.sum(rows * rows, axis=-1, keepdims=True)
        along += jnp.sum(dnormed * rows, axis=-1, keepdims=True)
    inv = lax.rsqrt(square / D + EPSILON)
    pull = inv * inv * inv * (along / D)
    for c in range(NC):
        cols = chunk(c)
        upstream = slot_grad(meta, gl, 0, cols)
        if received:
            upstream = upstream + inc[0, :, cols].astype(F32)
        rows = hidden[0, :, cols].astype(F32)
        out[:, cols] = (upstream + inv * scaled[:, cols] - rows * pull).astype(BF)


def backward_share(meta, cur, inc, gl, gain, parts):
    received = inc is not None
    operands = [meta, cur] + ([inc] if received else []) + [gl, gain, *parts]
    return call(
        functools.partial(backward_share_kernel, received),
        len(operands),
        shaped(BLOCK, D),
        "backward_share",
        [pltpu.VMEM((BLOCK, D), F32)],
    )(*operands)


def precise(a, b, dims):
    return lax.dot_general(
        a, b, (dims, ((), ())), precision=lax.Precision.HIGHEST, preferred_element_type=F32
    )


def pool_sum_kernel(meta, p0, p1, p2, p3, out):
    total = p0[...].astype(F32) + p1[...].astype(F32) + p2[...].astype(F32) + p3[...].astype(F32)
    out[...] = total.astype(BF)


def loss_kernel(meta, positives, *refs):
    raw, losses, gl = refs
    pairs = DP
    lines = raw.shape[0] // DP
    half = lines // 2

    def joined(seq):
        pieces = []
        for c in range(half):
            at = seq * half + c
            every = [raw[i * lines + at : i * lines + at + 1, :] for i in range(pairs)]
            pieces.append(jnp.concatenate([line.astype(F32) for line in every], axis=0))
        return jnp.concatenate(pieces, axis=1)

    q, z = joined(0), joined(1)
    row = lax.broadcasted_iota(jnp.int32, (pairs, pairs), 0)
    col = meta[4] ^ lax.broadcasted_iota(jnp.int32, (pairs, pairs), 1)
    target = jnp.zeros((pairs, pairs), F32)
    for i in range(pairs):
        match = (row == i) & (col == positives[meta[4] ^ i])
        target = jnp.where(match, 1.0, target)
    eye = (
        lax.broadcasted_iota(jnp.int32, (pairs, pairs), 0)
        == lax.broadcasted_iota(jnp.int32, (pairs, pairs), 1)
    ).astype(F32)
    narrow = D // 2 ** (WIDTHS - 1)
    lane = lax.broadcasted_iota(jnp.int32, (1, 2 * narrow), 1) < narrow

    def block(x, b):
        if b == WIDTHS - 1:
            return jnp.where(lane, x[:, : 2 * narrow], 0.0)
        if b == WIDTHS - 2:
            return jnp.where(lane, 0.0, x[:, : 2 * narrow])
        return x[:, D // 2 ** (b + 1) : D // 2**b]

    gram = [None] * WIDTHS
    sq = [None] * WIDTHS
    sz = [None] * WIDTHS
    total = (jnp.zeros((pairs, pairs), F32), jnp.zeros((pairs, 1), F32), jnp.zeros((pairs, 1), F32))
    for b in reversed(range(WIDTHS)):
        qb, zb = block(q, b), block(z, b)
        total = (
            total[0] + precise(qb, zb, NT),
            total[1] + jnp.sum(qb * qb, axis=-1, keepdims=True),
            total[2] + jnp.sum(zb * zb, axis=-1, keepdims=True),
        )
        gram[b], sq[b], sz[b] = total
    cross = jnp.zeros((pairs, pairs), F32)
    pull_q = jnp.zeros((pairs, 1), F32)
    pull_z = jnp.zeros((pairs, 1), F32)
    out_lane = lax.broadcasted_iota(jnp.int32, (1, 128), 1)
    loss_row = jnp.zeros((1, 128), F32)

    def flat(column):
        return jnp.sum(column * eye, axis=0, keepdims=True)

    for b in range(WIDTHS):
        width = D // 2**b
        inv_q = lax.rsqrt(sq[b] / width + 1e-06)
        inv_z = lax.rsqrt(sz[b] / width + 1e-06)
        inv_z_row = flat(inv_z)
        weight = inv_q * inv_z_row / (width * SOFTMAX_TEMPER)
        scores = gram[b] * weight
        top = jnp.max(scores, axis=-1, keepdims=True)
        raised = jnp.exp(scores - top)
        norm = jnp.sum(raised, axis=-1, keepdims=True)
        each = jnp.log(norm) + top - jnp.sum(scores * target, axis=-1, keepdims=True)
        loss_row = loss_row + jnp.where(
            out_lane == b, jnp.sum(each, axis=0, keepdims=True) / pairs, 0.0
        )
        dscores = (raised / norm - target) / pairs
        cross = cross + dscores * weight
        ds = dscores * scores
        pull_q = pull_q + jnp.sum(ds, axis=-1, keepdims=True) * inv_q * inv_q / width
        ds_z = jnp.sum(jnp.sum(ds, axis=0, keepdims=True) * eye, axis=-1, keepdims=True)
        pull_z = pull_z + ds_z * inv_z * inv_z / width
        qb, zb = block(q, b), block(z, b)
        dq = precise(cross, zb, NN) - pull_q * qb
        dz = precise(cross, qb, TN) - pull_z * zb
        dq = dq[0:1] / meta[2].astype(F32)
        dz = dz[0:1] / meta[3].astype(F32)
        if b == WIDTHS - 2:
            held_q, held_z = dq, dz
        elif b == WIDTHS - 1:
            gl[0:1, : 2 * narrow] = jnp.where(lane, dq, held_q)
            gl[1:2, : 2 * narrow] = jnp.where(lane, dz, held_z)
        else:
            gl[0:1, width // 2 : width] = dq
            gl[1:2, width // 2 : width] = dz
    losses[...] = loss_row


def loss_and_grad(meta, positives, raw):
    smem, vmem = [pl.BlockSpec(memory_space=space) for space in (pltpu.SMEM, pltpu.VMEM)]
    return pl.pallas_call(
        loss_kernel,
        in_specs=[smem, smem, vmem],
        out_specs=[vmem, vmem],
        out_shape=[shaped(1, 128, dtype=F32), shaped(2, D, dtype=F32)],
        compiler_params=pltpu.CompilerParams(vmem_limit_bytes=VMEM_LIMIT),
        name="loss_grad",
    )(meta, positives, raw)


def flipped(array, k):
    return lax.ppermute(array, "dp", [(j, j ^ k) for j in range(DP)])


def shifted(array, k):
    return lax.ppermute(array, "dp", [(j, (j + k) % DP) for j in range(DP)])


def gathered_pairs(array):
    reach = 1
    while reach < DP:
        array = jnp.concatenate([array, flipped(array, reach)], axis=0)
        reach *= 2
    return array


def gathered_heads(own):
    flip = flipped(own, 1)
    near = shifted(own, 2)
    far = shifted(own, DP - 2)
    flip_near = shifted(flip, 2)
    flip_far = shifted(flip, DP - 2)
    across = shifted(near, 2)
    flip_across = shifted(flip_far, DP - 2)
    return [own, flip, near, far, flip_near, flip_far, across, flip_across]


def head_sources(place):
    wrap = DP - 1
    return [
        place,
        place ^ 1,
        (place - 2) & wrap,
        (place + 2) & wrap,
        ((place - 2) & wrap) ^ 1,
        ((place + 2) & wrap) ^ 1,
        (place - 4) & wrap,
        ((place + 4) & wrap) ^ 1,
    ]


def gathered_rows(blocks):
    rows = [blocks[0]] + [flipped(blocks[k], k) for k in range(1, DP)]
    own = jnp.concatenate(rows, axis=0)
    ahead = [(j, (j + 1) % MP) for j in range(MP)]
    behind = [(j, (j - 1) % MP) for j in range(MP)]
    first = lax.ppermute(own, "mp", ahead)
    third = lax.ppermute(own, "mp", behind)
    second = lax.ppermute(first, "mp", ahead)
    return [own, first, second, third]


def over_mp(arrays):
    got = [arrays[0]]
    for k in range(1, MP):
        pairs = [(j, (j + k) % MP) for j in range(MP)]
        got.append(lax.ppermute(arrays[k], "mp", pairs))
    return got


def turned_kernel(meta, *refs):
    pieces, (normed, mixed) = refs[:DP], refs[DP:]
    for k in range(DP):
        normed[k] = pieces[k][:ROWS, :].T
        mixed[k] = pieces[k][ROWS:, :].T


def turned(meta, pieces):
    out = [shaped(DP, COLS, ROWS), shaped(DP, QC, ROWS)]
    return call(turned_kernel, 1 + DP, out, "turned")(meta, *pieces)


def weight_kernel(meta, normed, mixed, *refs):
    pieces, rows = refs[:DP], refs[DP : DP + MP]
    refs = refs[DP + MP :]
    gain, wq, wk, wv, dq, dk, dv, do = refs[:8]
    scale_outs, row_scr = refs[8:-1], refs[-1]
    total = jnp.zeros((COLS, QC + 2 * KC), F32)
    for source, piece in zip(head_sources(meta[4]), pieces):
        total += dot(normed[meta[4] ^ source], piece[...], NN)
    dq[...] = total[:, :QC]
    dk[...] = total[:, QC : QC + KC]
    dv[...] = total[:, QC + KC :]
    place = pl.ds(pl.multiple_of(meta[4] * COLS, COLS), COLS)
    ones = jnp.ones((8, QC), F32)
    scale = precise(ones, total[:, :QC] * wq[place, :].astype(F32), NT)
    kv = total[:, QC : QC + KC] * wk[place, :].astype(F32)
    kv = kv + total[:, QC + KC :] * wv[place, :].astype(F32)
    scale = scale + precise(ones[:, :KC], kv, NT)
    row_scr[...] = scale[0:1] / gain[:, place]
    for k, out in enumerate(scale_outs):
        at = pl.multiple_of(((meta[0] + k) & (MP - 1)) * 128, 128)
        out[...] = row_scr[:, pl.ds(at, 128)]
    total = jnp.zeros((QC, COLS), F32)
    for k in range(DP):
        dpart = jnp.concatenate([r[k * BLOCK : (k + 1) * BLOCK] for r in rows], axis=0)
        total += dot(mixed[k], dpart, NN)
    do[...] = total


def weight_grads(meta, normed, mixed, pieces, gain, wq, wk, wv):
    sizes = [(COLS, QC), (COLS, KC), (COLS, KC), (QC, COLS)] + [(1, 128)] * MP
    outs = call(
        weight_kernel,
        7 + DP + MP,
        [shaped(*size, dtype=F32) for size in sizes],
        "weight_grads",
        [pltpu.VMEM((1, COLS), F32)],
    )(meta, normed, mixed, *pieces, gain, wq, wk, wv)
    return outs[:4], outs[4:]


def local(entrance, lengths, positives, norm_gains, query_proj, key_proj, value_proj, out_proj):
    gain = norm_gains
    weights = (query_proj[0], key_proj[0], value_proj[0], out_proj[0])
    tables = jnp.asarray(rope_tables())
    places = [lax.axis_index(name).astype(jnp.int32) for name in ("mp", "section", "dp")]
    meta = jnp.stack([places[0], places[1], lengths[0, 0], lengths[0, 1], places[2]])

    cur = entrance.reshape(MP, BLOCK, D)
    arrived = None
    for turn in range(SECTIONS - 1):
        cur, parts = forward_turn(turn, meta, cur, arrived, gain, tables, weights, False)
        if turn == 0:
            parts, (gain, tables, *weights) = parts[:MP], parts[MP:]
        share = forward_share(meta, cur, scattered(parts, turn))
        arrived = sent_on(share, turn, turn + 1)
    cur, (*sent, qkv, pooled) = forward_turn(
        SECTIONS - 1, meta, cur, arrived, gain, tables, weights, True
    )
    pooled = call(pool_sum_kernel, 5, shaped(*pooled.shape), "pool_sum")(
        meta, *over_mp([pooled] * MP)
    )
    losses, gl = loss_and_grad(meta, positives, gathered_pairs(pooled))

    inc, arrived = None, None
    waves = {3: ((1, 3), (6,)), 2: ((5, 7), ()), 1: ((2, 4), ())}
    for turn in reversed(range(1, SECTIONS)):
        outs = backward_turn(turn, meta, inc, arrived, gl, qkv, tables, weights, False)
        if arrived is not None:
            inc, parts = outs[0], outs[1:]
        else:
            parts = outs
        parts = scattered(parts, turn)
        early, late = waves[turn]
        for k in early:
            parts[2], sent[k] = lax.optimization_barrier((parts[2], sent[k]))
            sent[k] = flipped(sent[k], k)
        share = backward_share(meta, cur, inc, gl, gain, parts)
        for k in late:
            share, sent[k] = lax.optimization_barrier((share, sent[k]))
            sent[k] = flipped(sent[k], k)
        arrived = sent_on(share, turn, turn - 1)
        for k in early + late:
            arrived[0], sent[k] = lax.optimization_barrier((arrived[0], sent[k]))
        if turn == 1:
            arrived[0], *sent = lax.optimization_barrier((arrived[0], *sent))
            normed, mixed = turned(meta, sent)
            arrived[1], normed, mixed = lax.optimization_barrier((arrived[1], normed, mixed))
    heads, *blocks = backward_turn(0, meta, inc, arrived, gl, qkv, tables, weights, True)
    pieces = gathered_heads(heads) + gathered_rows(blocks)
    (dq, dk, dv, out_grad), scales = weight_grads(
        meta, normed, mixed, pieces, gain, *weights[:3]
    )
    scale = sum(over_mp(scales))
    return (losses[:, :WIDTHS], scale, dq[None], dk[None], dv[None], out_grad[None])


def solution(mesh):
    in_specs = (
        P("dp", None, None, None),
        P("dp", None),
        P(),
        P("section", None),
        P("section", None, "mp"),
        P("section", None, "mp"),
        P("section", None, "mp"),
        P("section", "mp", None),
    )
    out_specs = (
        P("section", None),
        P("section", ("dp", "mp")),
        P("section", "dp", "mp"),
        P("section", "dp", "mp"),
        P("section", "dp", "mp"),
        P("section", "mp", "dp"),
    )
    return jax.shard_map(local, mesh=mesh, in_specs=in_specs, out_specs=out_specs, check_vma=False)
```

```python
import functools

import jax
import jax.numpy as jnp
import numpy as np
from jax import lax
from jax.experimental import pallas as pl
from jax.experimental.pallas import tpu as pltpu
from jax.sharding import PartitionSpec as P

HEAD = 128
WIDTHS = 7
EPSILON = 1e-05
SOFTMAX_TEMPER = 0.05
ROPE_BASE = 500000.0

LEN = 96
D = 4096
MP = 4
SECTIONS = 4
ROWS = 2 * LEN
BLOCK = ROWS // MP
QC = 512
KC = 128
HEADS = QC // HEAD
CH = 1024
NC = D // CH
SCALE = HEAD**-0.5
BF = jnp.bfloat16
F32 = jnp.float32
VMEM_LIMIT = 16 << 20
DP = 8
COLS = D // DP


def chip_of(section):
    return section // 2


def reduce_pairs(active, shift):
    pairs = []
    aside = {1: 2, 2: 0, 3: DP - 2}[shift]
    for s in range(SECTIONS):
        for d in range(DP):
            here = (s * DP + d) * MP
            if s % 2 == active % 2:
                pairs += [(here + j, here + (j + shift) % MP) for j in range(MP)]
            else:
                there = (s * DP + (d ^ aside)) * MP if aside else ((s ^ 2) * DP + d) * MP
                pairs += [(here + j, there + j) for j in range(MP)]
    return pairs


def hop_pairs(source, target, shift):
    hops = [(source, target)]
    if chip_of(source) == chip_of(target):
        hops.append((source ^ 2, target ^ 2))
    return [(a * MP + j, b * MP + (j + shift) % MP) for a, b in sorted(hops) for j in range(MP)]


def scattered(parts, active):
    arrived = [
        lax.ppermute(parts[(MP - k) % MP], ("section", "dp", "mp"), reduce_pairs(active, k))
        for k in (2, 1, 3)
    ]
    return [parts[0]] + arrived


def sent_on(share, source, target):
    axes = ("section", "mp")
    got = {k: lax.ppermute(share, axes, hop_pairs(source, target, k)) for k in (0, 1, 3, 2)}
    return [got[k] for k in range(MP)]


def rope_tables():
    half = HEAD // 2
    inverse_freq = np.float32(ROPE_BASE) ** (-np.arange(half, dtype=np.float32) * 2.0 / HEAD)
    angles = np.arange(LEN, dtype=np.float32)[:, None] * inverse_freq.astype(np.float32)[None, :]
    cosine, sine = np.cos(angles).astype(np.float32), np.sin(angles).astype(np.float32)
    cosine = np.concatenate([cosine, cosine], axis=1)
    sine = np.concatenate([-sine, sine], axis=1)
    return np.stack([cosine, sine])


class Place:
    def __init__(self, lengths):
        self.lengths = lengths

    def __getitem__(self, i):
        if i in (2, 3):
            return self.lengths[0, i - 2]
        return lax.axis_index({0: "mp", 1: "section", 4: "dp"}[i]).astype(jnp.int32)


def placed(kernel):
    return lambda lengths, *refs: kernel(Place(lengths), *refs)


def block_of(member, slot):
    return (member - slot) & (MP - 1)


def token_of(member, dim):
    shape = (ROWS, 1) if dim == 0 else (1, ROWS)
    i = lax.broadcasted_iota(jnp.int32, shape, dim)
    slot = (
        (i >= BLOCK).astype(jnp.int32)
        + (i >= 2 * BLOCK).astype(jnp.int32)
        + (i >= 3 * BLOCK).astype(jnp.int32)
    )
    return block_of(member, slot) * BLOCK + i - slot * BLOCK


def dot(a, b, dims):
    return lax.dot_general(a, b, (dims, ((), ())), preferred_element_type=F32)


NN = ((1,), (0,))
NT = ((1,), (1,))
TN = ((0,), (0,))


def in_slot_order(tables, member):
    ordered = []
    for t in range(2):
        pieces = []
        for k in range(MP):
            start = (block_of(member, k) & 1) * BLOCK
            pieces.append(tables[t, pl.ds(pl.multiple_of(start, BLOCK), BLOCK), :])
        ordered.append(jnp.concatenate(pieces, axis=0))
    return ordered


def rotated(x, cosine, sine):
    return x * cosine + pltpu.roll(x, HEAD // 2, 1) * sine


def rotated_back(x, cosine, sine):
    return x * cosine - pltpu.roll(x, HEAD // 2, 1) * sine


def attention_mask(member):
    row = token_of(member, 0)
    col = token_of(member, 1)
    first = jnp.where(row >= LEN, LEN, 0)
    return (col <= row) & (col >= first)


def probabilities(query, key, mask):
    scores = dot(query, key, NT) * SCALE
    scores = jnp.where(mask, scores, -1e30)
    top = jnp.max(scores, axis=-1, keepdims=True)
    weights = jnp.exp(scores - top)
    return weights / jnp.sum(weights, axis=-1, keepdims=True)


def slots_at(ref, cols):
    return jnp.concatenate([ref[k, :, cols] for k in range(MP)], axis=0)


def chunk(c):
    return slice(c * CH, (c + 1) * CH)


def valid_tokens(meta, rows):
    token = token_of(meta[0], 1)
    seq = lax.broadcasted_iota(jnp.int32, (rows, ROWS), 0)
    high = jnp.where(seq == 0, meta[2], LEN + meta[3])
    return ((token >= seq * LEN) & (token < high) & (seq < 2)).astype(BF)


def sent_cols(meta, k):
    block = meta[4] ^ k
    return pl.ds(pl.multiple_of(block * COLS, COLS), COLS)


CUBE = ((1, 7, 3, 5), (2, 4), (0, 6))
SOURCES = (0, 1, 2, 3, 6, 7, 4, 5)


def spread(meta, outs, array):
    rows = array.shape[0]
    for out, targets in zip(outs, CUBE):
        for i, k in enumerate(targets):
            out[i * rows : (i + 1) * rows, :] = array[:, sent_cols(meta, k)]


def forward_kernel(turn, last, *refs):
    refs = list(refs)
    meta, cur = refs[:2]
    refs = refs[2:]
    received = turn > 0
    arrivals = [refs.pop(0) for _ in range(MP)] if received else None
    if received:
        gain, tables, wq, wk, wv, wo = refs[:6]
        held = refs[6]
        outs = refs[7:]
        if last:
            *sent, mix_out, qkv_out, pool_out, normed_scr = outs
    else:
        stored = refs[:6]
        held = refs[6]
        outs = refs[7 : 7 + MP]
        gain, tables, wq, wk, wv, wo = refs[7 + MP : 13 + MP]
        sems = refs[13 + MP]
    member = meta[0]
    if received:

        @pl.when(meta[1] == turn)
        def _():
            for k in range(MP):
                held[k] = arrivals[k][...]

        @pl.when(meta[1] != turn)
        def _():
            for k in range(MP):
                held[k] = cur[k]
    else:
        copies = [
            pltpu.make_async_copy(cur.at[block_of(member, k)], held.at[k], sems.at[k])
            for k in range(MP)
        ]
        copies += [
            pltpu.make_async_copy(stored[i], kept, sems.at[MP + i])
            for i, kept in enumerate((gain, tables))
        ]
        small = len(copies)
        for c in range(NC):
            for i, kept in ((2, wq), (3, wk), (4, wv)):
                copies.append(
                    pltpu.make_async_copy(
                        stored[i].at[chunk(c), :], kept.at[chunk(c), :], sems.at[len(copies)]
                    )
                )
        copies.append(pltpu.make_async_copy(stored[5], wo, sems.at[len(copies)]))
        for copy in copies:
            copy.start()
        for copy in copies[:small]:
            copy.wait()
    inv = []
    for k in range(MP):
        rows = held[k].astype(F32)
        inv.append(lax.rsqrt(jnp.mean(rows * rows, axis=-1, keepdims=True) + EPSILON))
    inv = jnp.concatenate(inv, axis=0)
    acc_q = jnp.zeros((ROWS, QC), F32)
    acc_k = jnp.zeros((ROWS, KC), F32)
    acc_v = jnp.zeros((ROWS, KC), F32)
    for c in range(NC):
        cols = chunk(c)
        if not received:
            for copy in copies[small + 3 * c : small + 3 * c + 3]:
                copy.wait()
        normed = (slots_at(held, cols).astype(F32) * inv * gain[:, cols]).astype(BF)
        if last:
            normed_scr[:, cols] = normed
        acc_q += dot(normed, wq[cols, :], NN)
        acc_k += dot(normed, wk[cols, :], NN)
        acc_v += dot(normed, wv[cols, :], NN)
    cosine, sine = in_slot_order(tables, member)
    mask = attention_mask(member)
    key = rotated(acc_k, cosine, sine).astype(BF)
    value = acc_v.astype(BF)
    mixed = []
    for j in range(HEADS):
        cols = slice(j * HEAD, (j + 1) * HEAD)
        query = rotated(acc_q[:, cols], cosine, sine).astype(BF)
        if last:
            qkv_out[:, cols] = query
        weights = probabilities(query, key, mask).astype(BF)
        mixed.append(dot(weights, value, NN).astype(BF))
    mixed = jnp.concatenate(mixed, axis=1)
    if not last:
        if not received:
            copies[-1].wait()
        for c in range(NC):
            cols = chunk(c)
            part = dot(mixed, wo[:, cols], NN).astype(BF)
            for k in range(MP):
                outs[k][:, cols] = part[k * BLOCK : (k + 1) * BLOCK]
        return
    qkv_out[:, QC : QC + KC] = key
    qkv_out[:, QC + KC :] = value
    spread(meta, sent, normed_scr)
    sent[0][4 * ROWS :, :] = mixed
    mix_out[...] = mixed
    pool = valid_tokens(meta, 8)
    row = lax.broadcasted_iota(jnp.int32, (8, 1), 0)
    count = jnp.where(row == 0, meta[2], meta[3]).astype(F32)
    total = dot(pool, mixed, NN)
    top = total.astype(BF)
    low = (total - top.astype(F32)).astype(BF)
    pieces = []
    for c in range(NC):
        cols = chunk(c)
        pooled = dot(top, wo[:, cols], NN) + dot(low, wo[:, cols], NN)
        pooled = pooled + dot(pool, slots_at(held, cols), NN) * (1.0 / MP)
        pieces.append(pooled / count)
    rows = []
    for seq in range(2):
        for c in range(NC):
            for b in range(CH // COLS):
                rows.append(pieces[c][seq : seq + 1, b * COLS : (b + 1) * COLS])
    pool_out[...] = jnp.concatenate(rows, axis=0).astype(BF)


def call(kernel, in_count, out_shape, name, scratch=(), stored=False):
    vmem = pl.BlockSpec(memory_space=pltpu.VMEM)
    source = pl.BlockSpec(memory_space=pl.ANY) if stored else vmem
    return pl.pallas_call(
        placed(kernel),
        in_specs=[pl.BlockSpec(memory_space=pltpu.SMEM)] + [source] * (in_count - 1),
        out_specs=jax.tree.map(lambda _: vmem, out_shape),
        out_shape=out_shape,
        scratch_shapes=list(scratch),
        compiler_params=pltpu.CompilerParams(vmem_limit_bytes=VMEM_LIMIT),
        name=name,
    )


def shaped(*dims, dtype=BF):
    return jax.ShapeDtypeStruct(dims, dtype)


def kept(*dims, dtype=BF):
    return pltpu.VMEM(dims, dtype)


def forward_turn(turn, meta, cur, arrivals, gain, tables, weights, last):
    operands = [meta, cur] + list(arrivals or []) + [gain, tables, *weights]
    out_shape = [kept(MP, BLOCK, D)]
    scratch = ()
    if last:
        out_shape += [shaped(n * ROWS, COLS) for n in (5, 2, 2, 1)]
        out_shape += [shaped(ROWS, QC + 2 * KC), shaped(2 * D // COLS, COLS)]
        scratch = [pltpu.VMEM((ROWS, D), BF)]
    else:
        out_shape += [shaped(BLOCK, D)] * MP
    if turn == 0:
        for array in operands[2:]:
            out_shape.append(kept(*array.shape, dtype=array.dtype))
        scratch = [pltpu.SemaphoreType.DMA((MP + 2 + 3 * NC + 1,))]
    if turn == 0:
        operands[1:] = [pltpu.with_memory_space_constraint(x, pltpu.HBM) for x in operands[1:]]
    outs = call(
        functools.partial(forward_kernel, turn, last),
        len(operands),
        out_shape,
        "forward_last" if last else "forward_turn",
        scratch,
        turn == 0,
    )(*operands)
    return outs[0], outs[1:]


def slot_grad(meta, gl, slot, cols):
    block = block_of(meta[0], slot)
    seq = block >> 1
    token = (block & 1) * BLOCK + lax.broadcasted_iota(jnp.int32, (BLOCK, 1), 0)
    valid = (token < jnp.where(seq == 0, meta[2], meta[3])).astype(F32)
    return valid * gl[pl.ds(seq, 1), cols]


def backward_kernel(turn, received, carried, last, *refs):
    refs = list(refs)
    meta = refs.pop(0)
    inc = refs.pop(0) if carried else None
    arrivals = [refs.pop(0) for _ in range(MP)] if received else None
    gl, qkv, tables, wq, wk, wv, wo = refs[:7]
    refs = refs[7:]
    member = meta[0]
    if last:
        grads, *sent = refs[:4]
        held, dpart_scr = refs[4:]
    else:
        held = refs.pop(0) if received else None
        part_refs, grads = refs[:MP], refs[MP]
    if received:

        @pl.when(meta[1] == turn)
        def _():
            for k in range(MP):
                held[k] = arrivals[k][...]

        @pl.when(meta[1] != turn)
        def _():
            for k in range(MP):
                held[k] = inc[k] if carried else jnp.zeros((BLOCK, D), BF)

    acc = jnp.zeros((ROWS, QC), F32)
    for c in range(NC):
        cols = chunk(c)
        rows = []
        for k in range(MP):
            grad = slot_grad(meta, gl, k, cols)
            if received:
                grad = grad + held[k, :, cols].astype(F32)
            rows.append(grad.astype(BF))
        dpart = jnp.concatenate(rows, axis=0)
        if last:
            dpart_scr[:, cols] = dpart[:BLOCK]
        acc += dot(dpart, wo[:, cols], NT)
    cosine, sine = in_slot_order(tables, member)
    mask = attention_mask(member)
    key = qkv[:, QC : QC + KC]
    value = qkv[:, QC + KC :]
    dkey = jnp.zeros((ROWS, HEAD), F32)
    dvalue = jnp.zeros((ROWS, HEAD), F32)
    for j in range(HEADS):
        cols = slice(j * HEAD, (j + 1) * HEAD)
        query = qkv[:, cols]
        dmix = acc[:, cols].astype(BF)
        weights = probabilities(query, key, mask)
        dvalue += dot(weights.astype(BF), dmix, TN)
        dweights = dot(dmix, value, NT).astype(BF).astype(F32)
        moved = weights * dweights
        dscores = (moved - weights * jnp.sum(moved, axis=-1, keepdims=True)) * SCALE
        dscores = dscores.astype(BF)
        dquery = dot(dscores, key, NN).astype(BF).astype(F32)
        grads[:, cols] = rotated_back(dquery, cosine, sine).astype(BF)
        dkey += dot(dscores, query, TN)
    dkey = dkey.astype(BF).astype(F32)
    grads[:, QC : QC + KC] = rotated_back(dkey, cosine, sine).astype(BF)
    grads[:, QC + KC :] = dvalue.astype(BF)
    if last:
        spread(meta, sent, dpart_scr)
        return
    for c in range(NC):
        cols = chunk(c)
        dnormed = dot(grads[:, :QC], wq[cols, :], NT)
        dnormed += dot(grads[:, QC : QC + KC], wk[cols, :], NT)
        dnormed += dot(grads[:, QC + KC :], wv[cols, :], NT)
        dnormed = dnormed.astype(BF)
        for k in range(MP):
            part_refs[k][:, cols] = dnormed[k * BLOCK : (k + 1) * BLOCK]


def backward_turn(turn, meta, inc, arrivals, gl, qkv, tables, weights, last):
    received = arrivals is not None
    carried = inc is not None
    operands = [meta] + ([inc] if carried else []) + list(arrivals or [])
    operands += [gl, qkv, tables, *weights]
    if last:
        out_shape = [shaped(ROWS, QC + 2 * KC)]
        out_shape += [shaped(n * BLOCK, COLS) for n in (4, 2, 2)]
        scratch = [pltpu.VMEM((MP, BLOCK, D), BF), pltpu.VMEM((BLOCK, D), BF)]
    else:
        out_shape = ([kept(MP, BLOCK, D)] if received else []) + [shaped(BLOCK, D)] * MP
        scratch = [pltpu.VMEM((ROWS, QC + 2 * KC), BF)]
    return call(
        functools.partial(backward_kernel, turn, received, carried, last),
        len(operands),
        out_shape,
        "backward_last" if last else "backward_turn",
        scratch,
    )(*operands)


def summed(parts, cols):
    total = parts[0][:, cols].astype(F32)
    for part in parts[1:]:
        total = total + part[:, cols].astype(F32)
    return total


def forward_share_kernel(meta, hidden, p0, p1, p2, p3, out):
    for c in range(NC):
        cols = chunk(c)
        total = summed((p0, p1, p2, p3), cols)
        out[:, cols] = (hidden[0, :, cols].astype(F32) + total).astype(BF)


def forward_share(meta, cur, parts):
    return call(forward_share_kernel, 6, shaped(BLOCK, D), "forward_share")(meta, cur, *parts)


def backward_share_kernel(received, *refs):
    refs = list(refs)
    meta, hidden = refs.pop(0), refs.pop(0)
    inc = refs.pop(0) if received else None
    gl, gain, p0, p1, p2, p3, out, scaled = refs
    square = jnp.zeros((BLOCK, 1), F32)
    along = jnp.zeros((BLOCK, 1), F32)
    for c in range(NC):
        cols = chunk(c)
        rows = hidden[0, :, cols].astype(F32)
        dnormed = summed((p0, p1, p2, p3), cols) * gain[:, cols]
        scaled[:, cols] = dnormed
        square += jnp.sum(rows * rows, axis=-1, keepdims=True)
        along += jnp.sum(dnormed * rows, axis=-1, keepdims=True)
    inv = lax.rsqrt(square / D + EPSILON)
    pull = inv * inv * inv * (along / D)
    for c in range(NC):
        cols = chunk(c)
        upstream = slot_grad(meta, gl, 0, cols)
        if received:
            upstream = upstream + inc[0, :, cols].astype(F32)
        rows = hidden[0, :, cols].astype(F32)
        out[:, cols] = (upstream + inv * scaled[:, cols] - rows * pull).astype(BF)


def backward_share(meta, cur, inc, gl, gain, parts):
    received = inc is not None
    operands = [meta, cur] + ([inc] if received else []) + [gl, gain, *parts]
    return call(
        functools.partial(backward_share_kernel, received),
        len(operands),
        shaped(BLOCK, D),
        "backward_share",
        [pltpu.VMEM((BLOCK, D), F32)],
    )(*operands)


def precise(a, b, dims):
    return lax.dot_general(
        a, b, (dims, ((), ())), precision=lax.Precision.HIGHEST, preferred_element_type=F32
    )


def pool_sum_kernel(meta, p0, p1, p2, p3, out):
    total = p0[...].astype(F32) + p1[...].astype(F32) + p2[...].astype(F32) + p3[...].astype(F32)
    out[...] = total.astype(BF)


def loss_kernel(meta, positives, *refs):
    raw, losses, gl = refs
    pairs = DP
    lines = raw.shape[0] // DP
    half = lines // 2

    def joined(seq):
        pieces = []
        for c in range(half):
            at = seq * half + c
            every = [raw[i * lines + at : i * lines + at + 1, :] for i in range(pairs)]
            pieces.append(jnp.concatenate([line.astype(F32) for line in every], axis=0))
        return jnp.concatenate(pieces, axis=1)

    q, z = joined(0), joined(1)
    row = lax.broadcasted_iota(jnp.int32, (pairs, pairs), 0)
    col = pair_at(meta[4], lax.broadcasted_iota(jnp.int32, (pairs, pairs), 1))
    target = jnp.zeros((pairs, pairs), F32)
    for i in range(pairs):
        match = (row == i) & (col == positives[pair_at(meta[4], i)])
        target = jnp.where(match, 1.0, target)
    eye = (
        lax.broadcasted_iota(jnp.int32, (pairs, pairs), 0)
        == lax.broadcasted_iota(jnp.int32, (pairs, pairs), 1)
    ).astype(F32)
    narrow = D // 2 ** (WIDTHS - 1)
    lane = lax.broadcasted_iota(jnp.int32, (1, 2 * narrow), 1) < narrow

    def block(x, b):
        if b == WIDTHS - 1:
            return jnp.where(lane, x[:, : 2 * narrow], 0.0)
        if b == WIDTHS - 2:
            return jnp.where(lane, 0.0, x[:, : 2 * narrow])
        return x[:, D // 2 ** (b + 1) : D // 2**b]

    gram = [None] * WIDTHS
    sq = [None] * WIDTHS
    sz = [None] * WIDTHS
    total = (jnp.zeros((pairs, pairs), F32), jnp.zeros((pairs, 1), F32), jnp.zeros((pairs, 1), F32))
    for b in reversed(range(WIDTHS)):
        qb, zb = block(q, b), block(z, b)
        total = (
            total[0] + precise(qb, zb, NT),
            total[1] + jnp.sum(qb * qb, axis=-1, keepdims=True),
            total[2] + jnp.sum(zb * zb, axis=-1, keepdims=True),
        )
        gram[b], sq[b], sz[b] = total
    cross = jnp.zeros((pairs, pairs), F32)
    pull_q = jnp.zeros((pairs, 1), F32)
    pull_z = jnp.zeros((pairs, 1), F32)
    out_lane = lax.broadcasted_iota(jnp.int32, (1, 128), 1)
    loss_row = jnp.zeros((1, 128), F32)

    def flat(column):
        return jnp.sum(column * eye, axis=0, keepdims=True)

    for b in range(WIDTHS):
        width = D // 2**b
        inv_q = lax.rsqrt(sq[b] / width + 1e-06)
        inv_z = lax.rsqrt(sz[b] / width + 1e-06)
        inv_z_row = flat(inv_z)
        weight = inv_q * inv_z_row / (width * SOFTMAX_TEMPER)
        scores = gram[b] * weight
        top = jnp.max(scores, axis=-1, keepdims=True)
        raised = jnp.exp(scores - top)
        norm = jnp.sum(raised, axis=-1, keepdims=True)
        each = jnp.log(norm) + top - jnp.sum(scores * target, axis=-1, keepdims=True)
        loss_row = loss_row + jnp.where(
            out_lane == b, jnp.sum(each, axis=0, keepdims=True) / pairs, 0.0
        )
        dscores = (raised / norm - target) / pairs
        cross = cross + dscores * weight
        ds = dscores * scores
        pull_q = pull_q + jnp.sum(ds, axis=-1, keepdims=True) * inv_q * inv_q / width
        ds_z = jnp.sum(jnp.sum(ds, axis=0, keepdims=True) * eye, axis=-1, keepdims=True)
        pull_z = pull_z + ds_z * inv_z * inv_z / width
        qb, zb = block(q, b), block(z, b)
        dq = precise(cross, zb, NN) - pull_q * qb
        dz = precise(cross, qb, TN) - pull_z * zb
        dq = dq[0:1] / meta[2].astype(F32)
        dz = dz[0:1] / meta[3].astype(F32)
        if b == WIDTHS - 2:
            held_q, held_z = dq, dz
        elif b == WIDTHS - 1:
            gl[0:1, : 2 * narrow] = jnp.where(lane, dq, held_q)
            gl[1:2, : 2 * narrow] = jnp.where(lane, dz, held_z)
        else:
            gl[0:1, width // 2 : width] = dq
            gl[1:2, width // 2 : width] = dz
    losses[...] = loss_row


def loss_and_grad(meta, positives, raw):
    smem, vmem = [pl.BlockSpec(memory_space=space) for space in (pltpu.SMEM, pltpu.VMEM)]
    return pl.pallas_call(
        placed(loss_kernel),
        in_specs=[smem, smem, vmem],
        out_specs=[vmem, vmem],
        out_shape=[shaped(1, 128, dtype=F32), shaped(2, D, dtype=F32)],
        compiler_params=pltpu.CompilerParams(vmem_limit_bytes=VMEM_LIMIT),
        name="loss_grad",
    )(meta, positives, raw)


def flipped(array, k):
    return lax.ppermute(array, "dp", [(j, j ^ k) for j in range(DP)])


def gathered_pairs(array):
    for reach in (2, 6, 1):
        array = jnp.concatenate([array, flipped(array, reach)], axis=0)
    return array


def pair_at(place, slot):
    return place ^ ((slot & 3) << 1) ^ (slot & 2) ^ (slot >> 2)


def gathered_heads(own):
    flip = flipped(own, 1)
    near = flipped(own, 2)
    far = flipped(own, 6)
    flip, near, far = lax.optimization_barrier((flip, near, far))
    flip_near = flipped(flip, 2)
    flip_far = flipped(flip, 6)
    across = flipped(near, 6)
    flip_across = flipped(flip_far, 2)
    return [own, flip, near, far, flip_near, flip_far, across, flip_across]


HEAD_SOURCES = (0, 1, 2, 6, 3, 7, 4, 5)


def second_step(high, first_got, rows):
    return jnp.concatenate([high, first_got[2 * rows : 4 * rows]], axis=0)


def third_step(low, first_got, second_got, rows):
    pieces = [low[rows:], first_got[rows : 2 * rows]]
    pieces += [second_got[rows : 2 * rows], second_got[3 * rows : 4 * rows]]
    return jnp.concatenate(pieces, axis=0)


def gathered_rows(first, high, low):
    one = flipped(first, 1)
    two = flipped(second_step(high, one, BLOCK), 2)
    three = flipped(third_step(low, one, two, BLOCK), 6)
    pieces = [low[:BLOCK], one[:BLOCK], two[:BLOCK], two[2 * BLOCK : 3 * BLOCK], three]
    own = jnp.concatenate(pieces, axis=0)
    ahead = [(j, (j + 1) % MP) for j in range(MP)]
    behind = [(j, (j - 1) % MP) for j in range(MP)]
    first = lax.ppermute(own, "mp", ahead)
    third = lax.ppermute(own, "mp", behind)
    second = lax.ppermute(first, "mp", ahead)
    return [own, first, second, third]


def over_mp(arrays):
    got = [arrays[0]]
    for k in range(1, MP):
        pairs = [(j, (j + k) % MP) for j in range(MP)]
        got.append(lax.ppermute(arrays[k], "mp", pairs))
    return got


def turned_kernel(meta, low, mix, one, two, three, normed, mixed):
    def rows(ref, i):
        return ref[i * ROWS : (i + 1) * ROWS, :]

    normal = [rows(low, 0), rows(one, 0), rows(two, 0), rows(two, 2)]
    normal += [rows(three, i) for i in range(4)]
    blend = [mix[...], rows(one, 4), rows(two, 4), rows(two, 5)]
    blend += [rows(three, 4 + i) for i in range(4)]
    for i, source in enumerate(SOURCES):
        normed[source] = normal[i].T
        mixed[source] = blend[i].T


def turned(meta, *arrays):
    out = [shaped(DP, COLS, ROWS), shaped(DP, QC, ROWS)]
    return call(turned_kernel, 6, out, "turned")(meta, *arrays)


def weight_kernel(meta, normed, *refs):
    pieces, refs = refs[:DP], refs[DP:]
    gain, wq, wk, wv, dq, dk, dv = refs[:7]
    scale_outs, row_scr = refs[7:-1], refs[-1]
    total = jnp.zeros((COLS, QC + 2 * KC), F32)
    for source, piece in zip(HEAD_SOURCES, pieces):
        total += dot(normed[source], piece[...], NN)
    dq[...] = total[:, :QC]
    dk[...] = total[:, QC : QC + KC]
    dv[...] = total[:, QC + KC :]
    place = pl.ds(pl.multiple_of(meta[4] * COLS, COLS), COLS)
    ones = jnp.ones((8, QC), F32)
    scale = precise(ones, total[:, :QC] * wq[place, :].astype(F32), NT)
    kv = total[:, QC : QC + KC] * wk[place, :].astype(F32)
    kv = kv + total[:, QC + KC :] * wv[place, :].astype(F32)
    scale = scale + precise(ones[:, :KC], kv, NT)
    row_scr[...] = scale[0:1] / gain[:, place]
    for k, out in enumerate(scale_outs):
        at = pl.multiple_of(((meta[0] + k) & (MP - 1)) * 128, 128)
        out[...] = row_scr[:, pl.ds(at, 128)]


def weight_grads(meta, normed, pieces, gain, wq, wk, wv):
    sizes = [(COLS, QC), (COLS, KC), (COLS, KC)] + [(1, 128)] * MP
    outs = call(
        weight_kernel,
        6 + DP,
        [shaped(*size, dtype=F32) for size in sizes],
        "weight_grads",
        [pltpu.VMEM((1, COLS), F32)],
    )(meta, normed, *pieces, gain, wq, wk, wv)
    return outs[:3], outs[3:]


def out_kernel(meta, mixed, *refs):
    rows, out = refs[:MP], refs[MP]
    total = jnp.zeros((QC, COLS), F32)
    for k in range(DP):
        dpart = jnp.concatenate([r[k * BLOCK : (k + 1) * BLOCK] for r in rows], axis=0)
        total += dot(mixed[SOURCES[k]], dpart, NN)
    out[...] = total


def out_grads(meta, mixed, rows):
    out = shaped(QC, COLS, dtype=F32)
    return call(out_kernel, 2 + MP, out, "out_grads")(meta, mixed, *rows)


def local(entrance, lengths, positives, norm_gains, query_proj, key_proj, value_proj, out_proj):
    gain = norm_gains
    weights = (query_proj[0], key_proj[0], value_proj[0], out_proj[0])
    tables = jnp.asarray(rope_tables())
    meta = lengths

    cur = entrance.reshape(MP, BLOCK, D)
    arrived = None
    for turn in range(SECTIONS - 1):
        cur, parts = forward_turn(turn, meta, cur, arrived, gain, tables, weights, False)
        if turn == 0:
            parts, (gain, tables, *weights) = parts[:MP], parts[MP:]
        share = forward_share(meta, cur, scattered(parts, turn))
        arrived = sent_on(share, turn, turn + 1)
    cur, (first, high, low, mix, qkv, pooled) = forward_turn(
        SECTIONS - 1, meta, cur, arrived, gain, tables, weights, True
    )
    pools = over_mp([pooled] * MP)
    pools[1], first = lax.optimization_barrier((pools[1], first))
    one = flipped(first, 1)
    pooled = call(pool_sum_kernel, 5, shaped(*pooled.shape), "pool_sum")(meta, *pools)
    raw = gathered_pairs(pooled)
    losses, gl = loss_and_grad(meta, positives, raw)

    inc, arrived = None, None
    for turn in reversed(range(1, SECTIONS)):
        outs = backward_turn(turn, meta, inc, arrived, gl, qkv, tables, weights, False)
        if arrived is not None:
            inc, parts = outs[0], outs[1:]
        else:
            parts = outs
        parts = scattered(parts, turn)
        if turn == 3:
            parts[2], one = lax.optimization_barrier((parts[2], one))
            step = second_step(high, one, ROWS)
            two = flipped(jnp.concatenate([step, mix, one[4 * ROWS :]], axis=0), 2)
        if turn == 2:
            parts[2], two = lax.optimization_barrier((parts[2], two))
            step = third_step(low, one, two, ROWS)
            pieces = [step, mix, one[4 * ROWS :], two[4 * ROWS :]]
            three = flipped(jnp.concatenate(pieces, axis=0), 6)
        share = backward_share(meta, cur, inc, gl, gain, parts)
        arrived = sent_on(share, turn, turn - 1)
        if turn == 1:
            arrived[0], three = lax.optimization_barrier((arrived[0], three))
            normed, mixed = turned(meta, low, mix, one, two, three)
            arrived[1], normed, mixed = lax.optimization_barrier((arrived[1], normed, mixed))
    heads, *blocks = backward_turn(0, meta, inc, arrived, gl, qkv, tables, weights, True)
    pieces = gathered_heads(heads)
    rows = gathered_rows(*blocks)
    (dq, dk, dv), scales = weight_grads(meta, normed, pieces, gain, *weights[:3])
    *scales, rows[2], rows[3] = lax.optimization_barrier((*scales, rows[2], rows[3]))
    scales = over_mp(scales)
    out_grad = out_grads(meta, mixed, rows)
    scale = sum(scales)
    return (losses[:, :WIDTHS], scale, dq[None], dk[None], dv[None], out_grad[None])


def solution(mesh):
    in_specs = (
        P("dp", None, None, None),
        P("dp", None),
        P(),
        P("section", None),
        P("section", None, "mp"),
        P("section", None, "mp"),
        P("section", None, "mp"),
        P("section", "mp", None),
    )
    out_specs = (
        P("section", None),
        P("section", ("dp", "mp")),
        P("section", "dp", "mp"),
        P("section", "dp", "mp"),
        P("section", "dp", "mp"),
        P("section", "mp", "dp"),
    )
    return jax.shard_map(local, mesh=mesh, in_specs=in_specs, out_specs=out_specs, check_vma=False)
```

```python
import functools

import jax
import jax.numpy as jnp
import numpy as np
from jax import lax
from jax.experimental import pallas as pl
from jax.experimental.pallas import tpu as pltpu
from jax.sharding import PartitionSpec as P

HEAD = 128
WIDTHS = 7
EPSILON = 1e-05
SOFTMAX_TEMPER = 0.05
ROPE_BASE = 500000.0

LEN = 96
D = 4096
MP = 4
SECTIONS = 4
ROWS = 2 * LEN
BLOCK = ROWS // MP
QC = 512
KC = 128
HEADS = QC // HEAD
CH = 1024
NC = D // CH
SCALE = HEAD**-0.5
BF = jnp.bfloat16
F32 = jnp.float32
VMEM_LIMIT = 16 << 20
DP = 8
COLS = D // DP


def chip_of(section):
    return section // 2


def reduce_pairs(active, shift):
    pairs = []
    aside = {1: 2, 2: 0, 3: DP - 2}[shift]
    for s in range(SECTIONS):
        for d in range(DP):
            here = (s * DP + d) * MP
            if s % 2 == active % 2:
                pairs += [(here + j, here + (j + shift) % MP) for j in range(MP)]
            else:
                there = (s * DP + (d ^ aside)) * MP if aside else ((s ^ 2) * DP + d) * MP
                pairs += [(here + j, there + j) for j in range(MP)]
    return pairs


def hop_pairs(source, target, shift):
    hops = [(source, target)]
    if chip_of(source) == chip_of(target):
        hops.append((source ^ 2, target ^ 2))
    return [(a * MP + j, b * MP + (j + shift) % MP) for a, b in sorted(hops) for j in range(MP)]


def scattered(parts, active):
    arrived = [
        lax.ppermute(parts[(MP - k) % MP], ("section", "dp", "mp"), reduce_pairs(active, k))
        for k in (2, 1, 3)
    ]
    return [parts[0]] + arrived


def sent_on(share, source, target):
    axes = ("section", "mp")
    got = {k: lax.ppermute(share, axes, hop_pairs(source, target, k)) for k in (0, 1, 3, 2)}
    return [got[k] for k in range(MP)]


def rope_tables():
    half = HEAD // 2
    inverse_freq = np.float32(ROPE_BASE) ** (-np.arange(half, dtype=np.float32) * 2.0 / HEAD)
    angles = np.arange(LEN, dtype=np.float32)[:, None] * inverse_freq.astype(np.float32)[None, :]
    cosine, sine = np.cos(angles).astype(np.float32), np.sin(angles).astype(np.float32)
    cosine = np.concatenate([cosine, cosine], axis=1)
    sine = np.concatenate([-sine, sine], axis=1)
    return np.stack([cosine, sine])


class Place:
    def __init__(self, lengths):
        self.lengths = lengths

    def __getitem__(self, i):
        if i in (2, 3):
            return self.lengths[0, i - 2]
        return lax.axis_index({0: "mp", 1: "section", 4: "dp"}[i]).astype(jnp.int32)


def placed(kernel):
    return lambda lengths, *refs: kernel(Place(lengths), *refs)


def block_of(member, slot):
    return (member - slot) & (MP - 1)


def token_of(member, dim):
    shape = (ROWS, 1) if dim == 0 else (1, ROWS)
    i = lax.broadcasted_iota(jnp.int32, shape, dim)
    slot = (
        (i >= BLOCK).astype(jnp.int32)
        + (i >= 2 * BLOCK).astype(jnp.int32)
        + (i >= 3 * BLOCK).astype(jnp.int32)
    )
    return block_of(member, slot) * BLOCK + i - slot * BLOCK


def dot(a, b, dims):
    return lax.dot_general(a, b, (dims, ((), ())), preferred_element_type=F32)


NN = ((1,), (0,))
NT = ((1,), (1,))
TN = ((0,), (0,))


def in_slot_order(tables, member):
    ordered = []
    for t in range(2):
        pieces = []
        for k in range(MP):
            start = (block_of(member, k) & 1) * BLOCK
            pieces.append(tables[t, pl.ds(pl.multiple_of(start, BLOCK), BLOCK), :])
        ordered.append(jnp.concatenate(pieces, axis=0))
    return ordered


def rotated(x, cosine, sine):
    return x * cosine + pltpu.roll(x, HEAD // 2, 1) * sine


def rotated_back(x, cosine, sine):
    return x * cosine - pltpu.roll(x, HEAD // 2, 1) * sine


def attention_mask(member):
    row = token_of(member, 0)
    col = token_of(member, 1)
    first = jnp.where(row >= LEN, LEN, 0)
    return (col <= row) & (col >= first)


def probabilities(query, key, mask):
    scores = dot(query, key, NT) * SCALE
    scores = jnp.where(mask, scores, -1e30)
    top = jnp.max(scores, axis=-1, keepdims=True)
    weights = jnp.exp(scores - top)
    return weights / jnp.sum(weights, axis=-1, keepdims=True)


def slots_at(ref, cols):
    return jnp.concatenate([ref[k, :, cols] for k in range(MP)], axis=0)


def chunk(c):
    return slice(c * CH, (c + 1) * CH)


def valid_tokens(meta, rows):
    token = token_of(meta[0], 1)
    seq = lax.broadcasted_iota(jnp.int32, (rows, ROWS), 0)
    high = jnp.where(seq == 0, meta[2], LEN + meta[3])
    return ((token >= seq * LEN) & (token < high) & (seq < 2)).astype(BF)


def sent_cols(meta, k):
    block = meta[4] ^ k
    return pl.ds(pl.multiple_of(block * COLS, COLS), COLS)


CUBE = ((1, 7, 3, 5), (2, 4), (0, 6))
SOURCES = (0, 1, 2, 3, 6, 7, 4, 5)


def spread(meta, outs, array):
    rows = array.shape[0]
    for out, targets in zip(outs, CUBE):
        for i, k in enumerate(targets):
            out[i * rows : (i + 1) * rows, :] = array[:, sent_cols(meta, k)]


def forward_kernel(turn, last, *refs):
    refs = list(refs)
    meta, cur = refs[:2]
    refs = refs[2:]
    received = turn > 0
    arrivals = [refs.pop(0) for _ in range(MP)] if received else None
    if received:
        gain, tables, wq, wk, wv, wo = refs[:6]
        held = refs[6]
        outs = refs[7:]
        if last:
            *sent, mix_out, qkv_out, pool_out, normed_scr = outs
    else:
        stored = refs[:6]
        held = refs[6]
        outs = refs[7 : 7 + MP]
        gain, tables, wq, wk, wv, wo = refs[7 + MP : 13 + MP]
        sems = refs[13 + MP]
    member = meta[0]
    if received:

        @pl.when(meta[1] == turn)
        def _():
            for k in range(MP):
                held[k] = arrivals[k][...]

        @pl.when(meta[1] != turn)
        def _():
            for k in range(MP):
                held[k] = cur[k]
    else:
        copies = [
            pltpu.make_async_copy(cur.at[block_of(member, k)], held.at[k], sems.at[k])
            for k in range(MP)
        ]
        copies += [
            pltpu.make_async_copy(stored[i], kept, sems.at[MP + i])
            for i, kept in enumerate((gain, tables))
        ]
        small = len(copies)
        for c in range(NC):
            for i, kept in ((2, wq), (3, wk), (4, wv)):
                copies.append(
                    pltpu.make_async_copy(
                        stored[i].at[chunk(c), :], kept.at[chunk(c), :], sems.at[len(copies)]
                    )
                )
        copies.append(pltpu.make_async_copy(stored[5], wo, sems.at[len(copies)]))
        for copy in copies:
            copy.start()
        for copy in copies[:small]:
            copy.wait()
    inv = []
    for k in range(MP):
        rows = held[k].astype(F32)
        inv.append(lax.rsqrt(jnp.mean(rows * rows, axis=-1, keepdims=True) + EPSILON))
    inv = jnp.concatenate(inv, axis=0)
    acc_q = jnp.zeros((ROWS, QC), F32)
    acc_k = jnp.zeros((ROWS, KC), F32)
    acc_v = jnp.zeros((ROWS, KC), F32)
    for c in range(NC):
        cols = chunk(c)
        if not received:
            for copy in copies[small + 3 * c : small + 3 * c + 3]:
                copy.wait()
        normed = (slots_at(held, cols).astype(F32) * inv * gain[:, cols]).astype(BF)
        if last:
            normed_scr[:, cols] = normed
        acc_q += dot(normed, wq[cols, :], NN)
        acc_k += dot(normed, wk[cols, :], NN)
        acc_v += dot(normed, wv[cols, :], NN)
    cosine, sine = in_slot_order(tables, member)
    mask = attention_mask(member)
    key = rotated(acc_k, cosine, sine).astype(BF)
    value = acc_v.astype(BF)
    mixed = []
    for j in range(HEADS):
        cols = slice(j * HEAD, (j + 1) * HEAD)
        query = rotated(acc_q[:, cols], cosine, sine).astype(BF)
        if last:
            qkv_out[:, cols] = query
        weights = probabilities(query, key, mask).astype(BF)
        mixed.append(dot(weights, value, NN).astype(BF))
    mixed = jnp.concatenate(mixed, axis=1)
    if not last:
        if not received:
            copies[-1].wait()
        for c in range(NC):
            cols = chunk(c)
            part = dot(mixed, wo[:, cols], NN).astype(BF)
            for k in range(MP):
                outs[k][:, cols] = part[k * BLOCK : (k + 1) * BLOCK]
        return
    qkv_out[:, QC : QC + KC] = key
    qkv_out[:, QC + KC :] = value
    spread(meta, sent, normed_scr)
    sent[0][4 * ROWS :, :] = mixed
    mix_out[...] = mixed
    pool = valid_tokens(meta, 8)
    row = lax.broadcasted_iota(jnp.int32, (8, 1), 0)
    count = jnp.where(row == 0, meta[2], meta[3]).astype(F32)
    total = dot(pool, mixed, NN)
    top = total.astype(BF)
    low = (total - top.astype(F32)).astype(BF)
    pieces = []
    for c in range(NC):
        cols = chunk(c)
        pooled = dot(top, wo[:, cols], NN) + dot(low, wo[:, cols], NN)
        pooled = pooled + dot(pool, slots_at(held, cols), NN) * (1.0 / MP)
        pieces.append(pooled / count)
    rows = []
    for seq in range(2):
        for c in range(NC):
            for b in range(CH // COLS):
                rows.append(pieces[c][seq : seq + 1, b * COLS : (b + 1) * COLS])
    pool_out[...] = jnp.concatenate(rows, axis=0).astype(BF)


def call(kernel, in_count, out_shape, name, scratch=(), stored=False):
    vmem = pl.BlockSpec(memory_space=pltpu.VMEM)
    source = pl.BlockSpec(memory_space=pl.ANY) if stored else vmem
    return pl.pallas_call(
        placed(kernel),
        in_specs=[pl.BlockSpec(memory_space=pltpu.SMEM)] + [source] * (in_count - 1),
        out_specs=jax.tree.map(lambda _: vmem, out_shape),
        out_shape=out_shape,
        scratch_shapes=list(scratch),
        compiler_params=pltpu.CompilerParams(vmem_limit_bytes=VMEM_LIMIT),
        name=name,
    )


def shaped(*dims, dtype=BF):
    return jax.ShapeDtypeStruct(dims, dtype)


def kept(*dims, dtype=BF):
    return pltpu.VMEM(dims, dtype)


def forward_turn(turn, meta, cur, arrivals, gain, tables, weights, last):
    operands = [meta, cur] + list(arrivals or []) + [gain, tables, *weights]
    out_shape = [kept(MP, BLOCK, D)]
    scratch = ()
    if last:
        out_shape += [shaped(n * ROWS, COLS) for n in (5, 2, 2, 1)]
        out_shape += [shaped(ROWS, QC + 2 * KC), shaped(2 * D // COLS, COLS)]
        scratch = [pltpu.VMEM((ROWS, D), BF)]
    else:
        out_shape += [shaped(BLOCK, D)] * MP
    if turn == 0:
        for array in operands[2:]:
            out_shape.append(kept(*array.shape, dtype=array.dtype))
        scratch = [pltpu.SemaphoreType.DMA((MP + 2 + 3 * NC + 1,))]
    if turn == 0:
        operands[1:] = [pltpu.with_memory_space_constraint(x, pltpu.HBM) for x in operands[1:]]
    outs = call(
        functools.partial(forward_kernel, turn, last),
        len(operands),
        out_shape,
        "forward_last" if last else "forward_turn",
        scratch,
        turn == 0,
    )(*operands)
    return outs[0], outs[1:]


def slot_grad(meta, gl, slot, cols):
    block = block_of(meta[0], slot)
    seq = block >> 1
    token = (block & 1) * BLOCK + lax.broadcasted_iota(jnp.int32, (BLOCK, 1), 0)
    valid = (token < jnp.where(seq == 0, meta[2], meta[3])).astype(F32)
    return valid * gl[pl.ds(seq, 1), cols]


def backward_kernel(turn, received, carried, last, *refs):
    refs = list(refs)
    meta = refs.pop(0)
    inc = refs.pop(0) if carried else None
    arrivals = [refs.pop(0) for _ in range(MP)] if received else None
    gl, qkv, tables, wq, wk, wv, wo = refs[:7]
    refs = refs[7:]
    member = meta[0]
    if last:
        grads, *sent = refs[:4]
        held, dpart_scr = refs[4:]
    else:
        held = refs.pop(0) if received else None
        part_refs, grads = refs[:MP], refs[MP]
    if received:

        @pl.when(meta[1] == turn)
        def _():
            for k in range(MP):
                held[k] = arrivals[k][...]

        @pl.when(meta[1] != turn)
        def _():
            for k in range(MP):
                held[k] = inc[k] if carried else jnp.zeros((BLOCK, D), BF)

    acc = jnp.zeros((ROWS, QC), F32)
    for c in range(NC):
        cols = chunk(c)
        rows = []
        for k in range(MP):
            grad = slot_grad(meta, gl, k, cols)
            if received:
                grad = grad + held[k, :, cols].astype(F32)
            rows.append(grad.astype(BF))
        dpart = jnp.concatenate(rows, axis=0)
        if last:
            dpart_scr[:, cols] = dpart[:BLOCK]
        acc += dot(dpart, wo[:, cols], NT)
    cosine, sine = in_slot_order(tables, member)
    mask = attention_mask(member)
    key = qkv[:, QC : QC + KC]
    value = qkv[:, QC + KC :]
    dkey = jnp.zeros((ROWS, HEAD), F32)
    dvalue = jnp.zeros((ROWS, HEAD), F32)
    for j in range(HEADS):
        cols = slice(j * HEAD, (j + 1) * HEAD)
        query = qkv[:, cols]
        dmix = acc[:, cols].astype(BF)
        weights = probabilities(query, key, mask)
        dvalue += dot(weights.astype(BF), dmix, TN)
        dweights = dot(dmix, value, NT).astype(BF).astype(F32)
        moved = weights * dweights
        dscores = (moved - weights * jnp.sum(moved, axis=-1, keepdims=True)) * SCALE
        dscores = dscores.astype(BF)
        dquery = dot(dscores, key, NN).astype(BF).astype(F32)
        grads[:, cols] = rotated_back(dquery, cosine, sine).astype(BF)
        dkey += dot(dscores, query, TN)
    dkey = dkey.astype(BF).astype(F32)
    grads[:, QC : QC + KC] = rotated_back(dkey, cosine, sine).astype(BF)
    grads[:, QC + KC :] = dvalue.astype(BF)
    if last:
        spread(meta, sent, dpart_scr)
        return
    for c in range(NC):
        cols = chunk(c)
        dnormed = dot(grads[:, :QC], wq[cols, :], NT)
        dnormed += dot(grads[:, QC : QC + KC], wk[cols, :], NT)
        dnormed += dot(grads[:, QC + KC :], wv[cols, :], NT)
        dnormed = dnormed.astype(BF)
        for k in range(MP):
            part_refs[k][:, cols] = dnormed[k * BLOCK : (k + 1) * BLOCK]


def backward_turn(turn, meta, inc, arrivals, gl, qkv, tables, weights, last):
    received = arrivals is not None
    carried = inc is not None
    operands = [meta] + ([inc] if carried else []) + list(arrivals or [])
    operands += [gl, qkv, tables, *weights]
    if last:
        out_shape = [shaped(ROWS, QC + 2 * KC)]
        out_shape += [shaped(n * BLOCK, COLS) for n in (4, 2, 2)]
        scratch = [pltpu.VMEM((MP, BLOCK, D), BF), pltpu.VMEM((BLOCK, D), BF)]
    else:
        out_shape = ([kept(MP, BLOCK, D)] if received else []) + [shaped(BLOCK, D)] * MP
        scratch = [pltpu.VMEM((ROWS, QC + 2 * KC), BF)]
    return call(
        functools.partial(backward_kernel, turn, received, carried, last),
        len(operands),
        out_shape,
        "backward_last" if last else "backward_turn",
        scratch,
    )(*operands)


def summed(parts, cols):
    total = parts[0][:, cols].astype(F32)
    for part in parts[1:]:
        total = total + part[:, cols].astype(F32)
    return total


def forward_share_kernel(meta, hidden, p0, p1, p2, p3, out):
    for c in range(NC):
        cols = chunk(c)
        total = summed((p0, p1, p2, p3), cols)
        out[:, cols] = (hidden[0, :, cols].astype(F32) + total).astype(BF)


def forward_share(meta, cur, parts):
    return call(forward_share_kernel, 6, shaped(BLOCK, D), "forward_share")(meta, cur, *parts)


def backward_share_kernel(received, *refs):
    refs = list(refs)
    meta, hidden = refs.pop(0), refs.pop(0)
    inc = refs.pop(0) if received else None
    gl, gain, p0, p1, p2, p3, out, scaled = refs
    square = jnp.zeros((BLOCK, 1), F32)
    along = jnp.zeros((BLOCK, 1), F32)
    for c in range(NC):
        cols = chunk(c)
        rows = hidden[0, :, cols].astype(F32)
        dnormed = summed((p0, p1, p2, p3), cols) * gain[:, cols]
        scaled[:, cols] = dnormed
        square += jnp.sum(rows * rows, axis=-1, keepdims=True)
        along += jnp.sum(dnormed * rows, axis=-1, keepdims=True)
    inv = lax.rsqrt(square / D + EPSILON)
    pull = inv * inv * inv * (along / D)
    for c in range(NC):
        cols = chunk(c)
        upstream = slot_grad(meta, gl, 0, cols)
        if received:
            upstream = upstream + inc[0, :, cols].astype(F32)
        rows = hidden[0, :, cols].astype(F32)
        out[:, cols] = (upstream + inv * scaled[:, cols] - rows * pull).astype(BF)


def backward_share(meta, cur, inc, gl, gain, parts):
    received = inc is not None
    operands = [meta, cur] + ([inc] if received else []) + [gl, gain, *parts]
    return call(
        functools.partial(backward_share_kernel, received),
        len(operands),
        shaped(BLOCK, D),
        "backward_share",
        [pltpu.VMEM((BLOCK, D), F32)],
    )(*operands)


def precise(a, b, dims):
    return lax.dot_general(
        a, b, (dims, ((), ())), precision=lax.Precision.HIGHEST, preferred_element_type=F32
    )


def pool_sum_kernel(meta, p0, p1, p2, p3, out):
    total = p0[...].astype(F32) + p1[...].astype(F32) + p2[...].astype(F32) + p3[...].astype(F32)
    out[...] = total.astype(BF)


def loss_kernel(meta, positives, *refs):
    raw, losses, gl = refs
    pairs = DP
    lines = raw.shape[0] // DP
    half = lines // 2

    def joined(seq):
        pieces = []
        for c in range(half):
            at = seq * half + c
            every = [raw[i * lines + at : i * lines + at + 1, :] for i in range(pairs)]
            pieces.append(jnp.concatenate([line.astype(F32) for line in every], axis=0))
        return jnp.concatenate(pieces, axis=1)

    q, z = joined(0), joined(1)
    row = lax.broadcasted_iota(jnp.int32, (pairs, pairs), 0)
    col = pair_at(meta[4], lax.broadcasted_iota(jnp.int32, (pairs, pairs), 1))
    target = jnp.zeros((pairs, pairs), F32)
    for i in range(pairs):
        match = (row == i) & (col == positives[pair_at(meta[4], i)])
        target = jnp.where(match, 1.0, target)
    eye = (
        lax.broadcasted_iota(jnp.int32, (pairs, pairs), 0)
        == lax.broadcasted_iota(jnp.int32, (pairs, pairs), 1)
    ).astype(F32)
    narrow = D // 2 ** (WIDTHS - 1)
    lane = lax.broadcasted_iota(jnp.int32, (1, 2 * narrow), 1) < narrow

    def block(x, b):
        if b == WIDTHS - 1:
            return jnp.where(lane, x[:, : 2 * narrow], 0.0)
        if b == WIDTHS - 2:
            return jnp.where(lane, 0.0, x[:, : 2 * narrow])
        return x[:, D // 2 ** (b + 1) : D // 2**b]

    gram = [None] * WIDTHS
    sq = [None] * WIDTHS
    sz = [None] * WIDTHS
    total = (jnp.zeros((pairs, pairs), F32), jnp.zeros((pairs, 1), F32), jnp.zeros((pairs, 1), F32))
    for b in reversed(range(WIDTHS)):
        qb, zb = block(q, b), block(z, b)
        total = (
            total[0] + precise(qb, zb, NT),
            total[1] + jnp.sum(qb * qb, axis=-1, keepdims=True),
            total[2] + jnp.sum(zb * zb, axis=-1, keepdims=True),
        )
        gram[b], sq[b], sz[b] = total
    cross = jnp.zeros((pairs, pairs), F32)
    pull_q = jnp.zeros((pairs, 1), F32)
    pull_z = jnp.zeros((pairs, 1), F32)
    out_lane = lax.broadcasted_iota(jnp.int32, (1, 128), 1)
    loss_row = jnp.zeros((1, 128), F32)

    def flat(column):
        return jnp.sum(column * eye, axis=0, keepdims=True)

    for b in range(WIDTHS):
        width = D // 2**b
        inv_q = lax.rsqrt(sq[b] / width + 1e-06)
        inv_z = lax.rsqrt(sz[b] / width + 1e-06)
        inv_z_row = flat(inv_z)
        weight = inv_q * inv_z_row / (width * SOFTMAX_TEMPER)
        scores = gram[b] * weight
        top = jnp.max(scores, axis=-1, keepdims=True)
        raised = jnp.exp(scores - top)
        norm = jnp.sum(raised, axis=-1, keepdims=True)
        each = jnp.log(norm) + top - jnp.sum(scores * target, axis=-1, keepdims=True)
        loss_row = loss_row + jnp.where(
            out_lane == b, jnp.sum(each, axis=0, keepdims=True) / pairs, 0.0
        )
        dscores = (raised / norm - target) / pairs
        cross = cross + dscores * weight
        ds = dscores * scores
        pull_q = pull_q + jnp.sum(ds, axis=-1, keepdims=True) * inv_q * inv_q / width
        ds_z = jnp.sum(jnp.sum(ds, axis=0, keepdims=True) * eye, axis=-1, keepdims=True)
        pull_z = pull_z + ds_z * inv_z * inv_z / width
        qb, zb = block(q, b), block(z, b)
        dq = precise(cross, zb, NN) - pull_q * qb
        dz = precise(cross, qb, TN) - pull_z * zb
        dq = dq[0:1] / meta[2].astype(F32)
        dz = dz[0:1] / meta[3].astype(F32)
        if b == WIDTHS - 2:
            held_q, held_z = dq, dz
        elif b == WIDTHS - 1:
            gl[0:1, : 2 * narrow] = jnp.where(lane, dq, held_q)
            gl[1:2, : 2 * narrow] = jnp.where(lane, dz, held_z)
        else:
            gl[0:1, width // 2 : width] = dq
            gl[1:2, width // 2 : width] = dz
    losses[...] = loss_row


def loss_and_grad(meta, positives, raw):
    smem, vmem = [pl.BlockSpec(memory_space=space) for space in (pltpu.SMEM, pltpu.VMEM)]
    return pl.pallas_call(
        placed(loss_kernel),
        in_specs=[smem, smem, vmem],
        out_specs=[vmem, vmem],
        out_shape=[shaped(1, 128, dtype=F32), shaped(2, D, dtype=F32)],
        compiler_params=pltpu.CompilerParams(vmem_limit_bytes=VMEM_LIMIT),
        name="loss_grad",
    )(meta, positives, raw)


def flipped(array, k):
    return lax.ppermute(array, "dp", [(j, j ^ k) for j in range(DP)])


def gathered_pairs(array, first):
    array = jnp.concatenate([array, flipped(array, 1)], axis=0)
    array, first = lax.optimization_barrier((array, first))
    one = flipped(first, 1)
    for reach in (2, 6):
        array = jnp.concatenate([array, flipped(array, reach)], axis=0)
    return array, one


def pair_at(place, slot):
    return place ^ slot ^ ((slot >> 2) << 1)


def gathered_heads(own):
    flip = flipped(own, 1)
    near = flipped(own, 2)
    far = flipped(own, 6)
    flip, near, far = lax.optimization_barrier((flip, near, far))
    flip_near = flipped(flip, 2)
    flip_far = flipped(flip, 6)
    across = flipped(near, 6)
    flip_across = flipped(flip_far, 2)
    return [own, flip, near, far, flip_near, flip_far, across, flip_across]


HEAD_SOURCES = (0, 1, 2, 6, 3, 7, 4, 5)


def second_step(high, first_got, rows):
    return jnp.concatenate([high, first_got[2 * rows : 4 * rows]], axis=0)


def third_step(low, first_got, second_got, rows):
    pieces = [low[rows:], first_got[rows : 2 * rows]]
    pieces += [second_got[rows : 2 * rows], second_got[3 * rows : 4 * rows]]
    return jnp.concatenate(pieces, axis=0)


def gathered_rows(first, high, low):
    one = flipped(first, 1)
    two = flipped(second_step(high, one, BLOCK), 2)
    three = flipped(third_step(low, one, two, BLOCK), 6)
    pieces = [low[:BLOCK], one[:BLOCK], two[:BLOCK], two[2 * BLOCK : 3 * BLOCK], three]
    own = jnp.concatenate(pieces, axis=0)
    ahead = [(j, (j + 1) % MP) for j in range(MP)]
    behind = [(j, (j - 1) % MP) for j in range(MP)]
    first = lax.ppermute(own, "mp", ahead)
    third = lax.ppermute(own, "mp", behind)
    second = lax.ppermute(first, "mp", ahead)
    return [own, first, second, third]


def over_mp(arrays):
    got = [arrays[0]]
    for k in range(1, MP):
        pairs = [(j, (j + k) % MP) for j in range(MP)]
        got.append(lax.ppermute(arrays[k], "mp", pairs))
    return got


def turned_kernel(meta, low, mix, one, two, three, normed, mixed):
    def rows(ref, i):
        return ref[i * ROWS : (i + 1) * ROWS, :]

    normal = [rows(low, 0), rows(one, 0), rows(two, 0), rows(two, 2)]
    normal += [rows(three, i) for i in range(4)]
    blend = [mix[...], rows(one, 4), rows(two, 4), rows(two, 5)]
    blend += [rows(three, 4 + i) for i in range(4)]
    for i, source in enumerate(SOURCES):
        normed[source] = normal[i].T
        mixed[source] = blend[i].T


def turned(meta, *arrays):
    out = [shaped(DP, COLS, ROWS), shaped(DP, QC, ROWS)]
    return call(turned_kernel, 6, out, "turned")(meta, *arrays)


def row_sums(values):
    ones = jnp.ones((8, values.shape[1]), BF)
    top = values.astype(BF)
    rest = values - top.astype(F32)
    middle = rest.astype(BF)
    low = (rest - middle.astype(F32)).astype(BF)
    return dot(ones, top, NT) + dot(ones, middle, NT) + dot(ones, low, NT)


def weight_kernel(meta, normed, *refs):
    pieces, refs = refs[:DP], refs[DP:]
    gain, wq, wk, wv, dq, dk, dv = refs[:7]
    scale_outs, row_scr = refs[7:-1], refs[-1]
    total = jnp.zeros((COLS, QC + 2 * KC), F32)
    for source, piece in zip(HEAD_SOURCES, pieces):
        total += dot(normed[source], piece[...], NN)
    dq[...] = total[:, :QC]
    dk[...] = total[:, QC : QC + KC]
    dv[...] = total[:, QC + KC :]
    place = pl.ds(pl.multiple_of(meta[4] * COLS, COLS), COLS)
    scale = row_sums(total[:, :QC] * wq[place, :].astype(F32))
    kv = total[:, QC : QC + KC] * wk[place, :].astype(F32)
    kv = kv + total[:, QC + KC :] * wv[place, :].astype(F32)
    scale = scale + row_sums(kv)
    row_scr[...] = scale[0:1] / gain[:, place]
    for k, out in enumerate(scale_outs):
        at = pl.multiple_of(((meta[0] + k) & (MP - 1)) * 128, 128)
        out[...] = row_scr[:, pl.ds(at, 128)]


def weight_grads(meta, normed, pieces, gain, wq, wk, wv):
    sizes = [(COLS, QC), (COLS, KC), (COLS, KC)] + [(1, 128)] * MP
    outs = call(
        weight_kernel,
        6 + DP,
        [shaped(*size, dtype=F32) for size in sizes],
        "weight_grads",
        [pltpu.VMEM((1, COLS), F32)],
    )(meta, normed, *pieces, gain, wq, wk, wv)
    return outs[:3], outs[3:]


def out_kernel(meta, mixed, *refs):
    rows, out = refs[:MP], refs[MP]
    total = jnp.zeros((QC, COLS), F32)
    for k in range(DP):
        dpart = jnp.concatenate([r[k * BLOCK : (k + 1) * BLOCK] for r in rows], axis=0)
        total += dot(mixed[SOURCES[k]], dpart, NN)
    out[...] = total


def out_grads(meta, mixed, rows):
    out = shaped(QC, COLS, dtype=F32)
    return call(out_kernel, 2 + MP, out, "out_grads")(meta, mixed, *rows)


def local(entrance, lengths, positives, norm_gains, query_proj, key_proj, value_proj, out_proj):
    gain = norm_gains
    weights = (query_proj[0], key_proj[0], value_proj[0], out_proj[0])
    tables = jnp.asarray(rope_tables())
    meta = lengths

    cur = entrance.reshape(MP, BLOCK, D)
    arrived = None
    for turn in range(SECTIONS - 1):
        cur, parts = forward_turn(turn, meta, cur, arrived, gain, tables, weights, False)
        if turn == 0:
            parts, (gain, tables, *weights) = parts[:MP], parts[MP:]
        share = forward_share(meta, cur, scattered(parts, turn))
        arrived = sent_on(share, turn, turn + 1)
    cur, (first, high, low, mix, qkv, pooled) = forward_turn(
        SECTIONS - 1, meta, cur, arrived, gain, tables, weights, True
    )
    pools = over_mp([pooled] * MP)
    pooled = call(pool_sum_kernel, 5, shaped(*pooled.shape), "pool_sum")(meta, *pools)
    raw, one = gathered_pairs(pooled, first)
    losses, gl = loss_and_grad(meta, positives, raw)

    inc, arrived = None, None
    for turn in reversed(range(1, SECTIONS)):
        outs = backward_turn(turn, meta, inc, arrived, gl, qkv, tables, weights, False)
        if arrived is not None:
            inc, parts = outs[0], outs[1:]
        else:
            parts = outs
        parts = scattered(parts, turn)
        if turn == 3:
            parts[3], one = lax.optimization_barrier((parts[3], one))
            step = second_step(high, one, ROWS)
            two = flipped(jnp.concatenate([step, mix, one[4 * ROWS :]], axis=0), 2)
        if turn == 2:
            parts[3], two = lax.optimization_barrier((parts[3], two))
            step = third_step(low, one, two, ROWS)
            pieces = [step, mix, one[4 * ROWS :], two[4 * ROWS :]]
            three = flipped(jnp.concatenate(pieces, axis=0), 6)
        share = backward_share(meta, cur, inc, gl, gain, parts)
        arrived = sent_on(share, turn, turn - 1)
        if turn == 1:
            arrived[0], three = lax.optimization_barrier((arrived[0], three))
            normed, mixed = turned(meta, low, mix, one, two, three)
            arrived[1], normed, mixed = lax.optimization_barrier((arrived[1], normed, mixed))
    heads, *blocks = backward_turn(0, meta, inc, arrived, gl, qkv, tables, weights, True)
    pieces = gathered_heads(heads)
    rows = gathered_rows(*blocks)
    (dq, dk, dv), scales = weight_grads(meta, normed, pieces, gain, *weights[:3])
    scales = over_mp(scales)
    out_grad = out_grads(meta, mixed, rows)
    scale = sum(scales)
    return (losses[:, :WIDTHS], scale, dq[None], dk[None], dv[None], out_grad[None])


def solution(mesh):
    in_specs = (
        P("dp", None, None, None),
        P("dp", None),
        P(),
        P("section", None),
        P("section", None, "mp"),
        P("section", None, "mp"),
        P("section", None, "mp"),
        P("section", "mp", None),
    )
    out_specs = (
        P("section", None),
        P("section", ("dp", "mp")),
        P("section", "dp", "mp"),
        P("section", "dp", "mp"),
        P("section", "dp", "mp"),
        P("section", "mp", "dp"),
    )
    return jax.shard_map(local, mesh=mesh, in_specs=in_specs, out_specs=out_specs, check_vma=False)
```

```python
import functools

import jax
import jax.numpy as jnp
import numpy as np
from jax import lax
from jax.experimental import pallas as pl
from jax.experimental.pallas import tpu as pltpu
from jax.sharding import PartitionSpec as P

HEAD = 128
WIDTHS = 7
EPSILON = 1e-05
SOFTMAX_TEMPER = 0.05
ROPE_BASE = 500000.0

LEN = 96
D = 4096
MP = 4
SECTIONS = 4
ROWS = 2 * LEN
BLOCK = ROWS // MP
QC = 512
KC = 128
HEADS = QC // HEAD
CH = 1024
NC = D // CH
SCALE = HEAD**-0.5
BF = jnp.bfloat16
F32 = jnp.float32
VMEM_LIMIT = 16 << 20
DP = 8
COLS = D // DP


def chip_of(section):
    return section // 2


def reduce_pairs(active, shift):
    pairs = []
    aside = {1: 2, 2: 0, 3: DP - 2}[shift]
    for s in range(SECTIONS):
        for d in range(DP):
            here = (s * DP + d) * MP
            if s % 2 == active % 2:
                pairs += [(here + j, here + (j + shift) % MP) for j in range(MP)]
            else:
                there = (s * DP + (d ^ aside)) * MP if aside else ((s ^ 2) * DP + d) * MP
                pairs += [(here + j, there + j) for j in range(MP)]
    return pairs


def hop_pairs(source, target, shift):
    hops = [(source, target)]
    if chip_of(source) == chip_of(target):
        hops.append((source ^ 2, target ^ 2))
    return [(a * MP + j, b * MP + (j + shift) % MP) for a, b in sorted(hops) for j in range(MP)]


def scattered(parts, active):
    arrived = [
        lax.ppermute(parts[(MP - k) % MP], ("section", "dp", "mp"), reduce_pairs(active, k))
        for k in (2, 1, 3)
    ]
    return [parts[0]] + arrived


def sent_on(share, source, target):
    axes = ("section", "mp")
    got = {k: lax.ppermute(share, axes, hop_pairs(source, target, k)) for k in (0, 1, 3, 2)}
    return [got[k] for k in range(MP)]


def rope_tables():
    half = HEAD // 2
    inverse_freq = np.float32(ROPE_BASE) ** (-np.arange(half, dtype=np.float32) * 2.0 / HEAD)
    angles = np.arange(LEN, dtype=np.float32)[:, None] * inverse_freq.astype(np.float32)[None, :]
    cosine, sine = np.cos(angles).astype(np.float32), np.sin(angles).astype(np.float32)
    cosine = np.concatenate([cosine, cosine], axis=1)
    sine = np.concatenate([-sine, sine], axis=1)
    return np.stack([cosine, sine])


class Place:
    def __init__(self, lengths):
        self.lengths = lengths

    def __getitem__(self, i):
        if i in (2, 3):
            return self.lengths[0, i - 2]
        return lax.axis_index({0: "mp", 1: "section", 4: "dp"}[i]).astype(jnp.int32)


def placed(kernel):
    return lambda lengths, *refs: kernel(Place(lengths), *refs)


def block_of(member, slot):
    return (member - slot) & (MP - 1)


def token_of(member, dim):
    shape = (ROWS, 1) if dim == 0 else (1, ROWS)
    i = lax.broadcasted_iota(jnp.int32, shape, dim)
    slot = (
        (i >= BLOCK).astype(jnp.int32)
        + (i >= 2 * BLOCK).astype(jnp.int32)
        + (i >= 3 * BLOCK).astype(jnp.int32)
    )
    return block_of(member, slot) * BLOCK + i - slot * BLOCK


def dot(a, b, dims):
    return lax.dot_general(a, b, (dims, ((), ())), preferred_element_type=F32)


NN = ((1,), (0,))
NT = ((1,), (1,))
TN = ((0,), (0,))


def in_slot_order(tables, member):
    ordered = []
    for t in range(2):
        pieces = []
        for k in range(MP):
            start = (block_of(member, k) & 1) * BLOCK
            pieces.append(tables[t, pl.ds(pl.multiple_of(start, BLOCK), BLOCK), :])
        ordered.append(jnp.concatenate(pieces, axis=0))
    return ordered


def rotated(x, cosine, sine):
    return x * cosine + pltpu.roll(x, HEAD // 2, 1) * sine


def rotated_back(x, cosine, sine):
    return x * cosine - pltpu.roll(x, HEAD // 2, 1) * sine


def attention_mask(member):
    row = token_of(member, 0)
    col = token_of(member, 1)
    first = jnp.where(row >= LEN, LEN, 0)
    return (col <= row) & (col >= first)


def probabilities(query, key, mask):
    scores = dot(query, key, NT) * SCALE
    scores = jnp.where(mask, scores, -1e30)
    top = jnp.max(scores, axis=-1, keepdims=True)
    weights = jnp.exp(scores - top)
    return weights / jnp.sum(weights, axis=-1, keepdims=True)


def slots_at(ref, cols):
    return jnp.concatenate([ref[k, :, cols] for k in range(MP)], axis=0)


def chunk(c):
    return slice(c * CH, (c + 1) * CH)


def valid_tokens(meta, rows):
    token = token_of(meta[0], 1)
    seq = lax.broadcasted_iota(jnp.int32, (rows, ROWS), 0)
    high = jnp.where(seq == 0, meta[2], LEN + meta[3])
    return ((token >= seq * LEN) & (token < high) & (seq < 2)).astype(BF)


def sent_cols(meta, k):
    block = meta[4] ^ k
    return pl.ds(pl.multiple_of(block * COLS, COLS), COLS)


CUBE = ((1, 7, 3, 5), (2, 4), (0, 6))
SOURCES = (0, 1, 2, 3, 6, 7, 4, 5)


def spread(meta, outs, array):
    rows = array.shape[0]
    for out, targets in zip(outs, CUBE):
        for i, k in enumerate(targets):
            out[i * rows : (i + 1) * rows, :] = array[:, sent_cols(meta, k)]


def forward_kernel(turn, last, *refs):
    refs = list(refs)
    meta, cur = refs[:2]
    refs = refs[2:]
    received = turn > 0
    arrivals = [refs.pop(0) for _ in range(MP)] if received else None
    if received:
        gain, tables, wq, wk, wv, wo = refs[:6]
        held = refs[6]
        outs = refs[7:]
        if last:
            *sent, mix_out, qkv_out, pool_out, normed_scr = outs
    else:
        stored = refs[:6]
        held = refs[6]
        outs = refs[7 : 7 + MP]
        gain, tables, wq, wk, wv, wo = refs[7 + MP : 13 + MP]
        sems = refs[13 + MP]
    member = meta[0]
    if received:

        @pl.when(meta[1] == turn)
        def _():
            for k in range(MP):
                held[k] = arrivals[k][...]

        @pl.when(meta[1] != turn)
        def _():
            for k in range(MP):
                held[k] = cur[k]
    else:
        copies = [
            pltpu.make_async_copy(cur.at[block_of(member, k)], held.at[k], sems.at[k])
            for k in range(MP)
        ]
        copies += [
            pltpu.make_async_copy(stored[i], kept, sems.at[MP + i])
            for i, kept in enumerate((gain, tables))
        ]
        small = len(copies)
        for c in range(NC):
            for i, kept in ((2, wq), (3, wk), (4, wv)):
                copies.append(
                    pltpu.make_async_copy(
                        stored[i].at[chunk(c), :], kept.at[chunk(c), :], sems.at[len(copies)]
                    )
                )
        copies.append(pltpu.make_async_copy(stored[5], wo, sems.at[len(copies)]))
        for copy in copies:
            copy.start()
        for copy in copies[:small]:
            copy.wait()
    inv = []
    for k in range(MP):
        rows = held[k].astype(F32)
        inv.append(lax.rsqrt(jnp.mean(rows * rows, axis=-1, keepdims=True) + EPSILON))
    inv = jnp.concatenate(inv, axis=0)
    acc_q = jnp.zeros((ROWS, QC), F32)
    acc_k = jnp.zeros((ROWS, KC), F32)
    acc_v = jnp.zeros((ROWS, KC), F32)
    for c in range(NC):
        cols = chunk(c)
        if not received:
            for copy in copies[small + 3 * c : small + 3 * c + 3]:
                copy.wait()
        normed = (slots_at(held, cols).astype(F32) * inv * gain[:, cols]).astype(BF)
        if last:
            normed_scr[:, cols] = normed
        acc_q += dot(normed, wq[cols, :], NN)
        acc_k += dot(normed, wk[cols, :], NN)
        acc_v += dot(normed, wv[cols, :], NN)
    cosine, sine = in_slot_order(tables, member)
    mask = attention_mask(member)
    key = rotated(acc_k, cosine, sine).astype(BF)
    value = acc_v.astype(BF)
    mixed = []
    for j in range(HEADS):
        cols = slice(j * HEAD, (j + 1) * HEAD)
        query = rotated(acc_q[:, cols], cosine, sine).astype(BF)
        if last:
            qkv_out[:, cols] = query
        weights = probabilities(query, key, mask).astype(BF)
        mixed.append(dot(weights, value, NN).astype(BF))
    mixed = jnp.concatenate(mixed, axis=1)
    if not last:
        if not received:
            copies[-1].wait()
        for c in range(NC):
            cols = chunk(c)
            part = dot(mixed, wo[:, cols], NN).astype(BF)
            for k in range(MP):
                outs[k][:, cols] = part[k * BLOCK : (k + 1) * BLOCK]
        return
    qkv_out[:, QC : QC + KC] = key
    qkv_out[:, QC + KC :] = value
    spread(meta, sent, normed_scr)
    sent[0][4 * ROWS :, :] = mixed
    mix_out[...] = mixed
    pool = valid_tokens(meta, 8)
    row = lax.broadcasted_iota(jnp.int32, (8, 1), 0)
    count = jnp.where(row == 0, meta[2], meta[3]).astype(F32)
    total = dot(pool, mixed, NN)
    top = total.astype(BF)
    low = (total - top.astype(F32)).astype(BF)
    pieces = []
    for c in range(NC):
        cols = chunk(c)
        pooled = dot(top, wo[:, cols], NN) + dot(low, wo[:, cols], NN)
        pooled = pooled + dot(pool, slots_at(held, cols), NN) * (1.0 / MP)
        pieces.append(pooled / count)
    rows = []
    for seq in range(2):
        for c in range(NC):
            for b in range(CH // COLS):
                rows.append(pieces[c][seq : seq + 1, b * COLS : (b + 1) * COLS])
    pool_out[...] = jnp.concatenate(rows, axis=0).astype(BF)


def call(kernel, in_count, out_shape, name, scratch=(), stored=False):
    vmem = pl.BlockSpec(memory_space=pltpu.VMEM)
    source = pl.BlockSpec(memory_space=pl.ANY) if stored else vmem
    return pl.pallas_call(
        placed(kernel),
        in_specs=[pl.BlockSpec(memory_space=pltpu.SMEM)] + [source] * (in_count - 1),
        out_specs=jax.tree.map(lambda _: vmem, out_shape),
        out_shape=out_shape,
        scratch_shapes=list(scratch),
        compiler_params=pltpu.CompilerParams(vmem_limit_bytes=VMEM_LIMIT),
        name=name,
    )


def shaped(*dims, dtype=BF):
    return jax.ShapeDtypeStruct(dims, dtype)


def kept(*dims, dtype=BF):
    return pltpu.VMEM(dims, dtype)


def forward_turn(turn, meta, cur, arrivals, gain, tables, weights, last):
    operands = [meta, cur] + list(arrivals or []) + [gain, tables, *weights]
    out_shape = [kept(MP, BLOCK, D)]
    scratch = ()
    if last:
        out_shape += [shaped(n * ROWS, COLS) for n in (5, 2, 2, 1)]
        out_shape += [shaped(ROWS, QC + 2 * KC), shaped(2 * D // COLS, COLS)]
        scratch = [pltpu.VMEM((ROWS, D), BF)]
    else:
        out_shape += [shaped(BLOCK, D)] * MP
    if turn == 0:
        for array in operands[2:]:
            out_shape.append(kept(*array.shape, dtype=array.dtype))
        scratch = [pltpu.SemaphoreType.DMA((MP + 2 + 3 * NC + 1,))]
    if turn == 0:
        operands[1:] = [pltpu.with_memory_space_constraint(x, pltpu.HBM) for x in operands[1:]]
    outs = call(
        functools.partial(forward_kernel, turn, last),
        len(operands),
        out_shape,
        "forward_last" if last else "forward_turn",
        scratch,
        turn == 0,
    )(*operands)
    return outs[0], outs[1:]


def slot_grad(meta, gl, slot, cols):
    block = block_of(meta[0], slot)
    seq = block >> 1
    token = (block & 1) * BLOCK + lax.broadcasted_iota(jnp.int32, (BLOCK, 1), 0)
    valid = (token < jnp.where(seq == 0, meta[2], meta[3])).astype(F32)
    return valid * gl[pl.ds(seq, 1), cols]


def backward_kernel(turn, received, carried, last, *refs):
    refs = list(refs)
    meta = refs.pop(0)
    inc = refs.pop(0) if carried else None
    arrivals = [refs.pop(0) for _ in range(MP)] if received else None
    gl, qkv, tables, wq, wk, wv, wo = refs[:7]
    refs = refs[7:]
    member = meta[0]
    if last:
        grads, *sent = refs[:4]
        held, dpart_scr = refs[4:]
    else:
        held = refs.pop(0) if received else None
        part_refs, grads = refs[:MP], refs[MP]
    if received:

        @pl.when(meta[1] == turn)
        def _():
            for k in range(MP):
                held[k] = arrivals[k][...]

        @pl.when(meta[1] != turn)
        def _():
            for k in range(MP):
                held[k] = inc[k] if carried else jnp.zeros((BLOCK, D), BF)

    acc = jnp.zeros((ROWS, QC), F32)
    for c in range(NC):
        cols = chunk(c)
        rows = []
        for k in range(MP):
            grad = slot_grad(meta, gl, k, cols)
            if received:
                grad = grad + held[k, :, cols].astype(F32)
            rows.append(grad.astype(BF))
        dpart = jnp.concatenate(rows, axis=0)
        if last:
            dpart_scr[:, cols] = dpart[:BLOCK]
        acc += dot(dpart, wo[:, cols], NT)
    cosine, sine = in_slot_order(tables, member)
    mask = attention_mask(member)
    key = qkv[:, QC : QC + KC]
    value = qkv[:, QC + KC :]
    dkey = jnp.zeros((ROWS, HEAD), F32)
    dvalue = jnp.zeros((ROWS, HEAD), F32)
    for j in range(HEADS):
        cols = slice(j * HEAD, (j + 1) * HEAD)
        query = qkv[:, cols]
        dmix = acc[:, cols].astype(BF)
        weights = probabilities(query, key, mask)
        dvalue += dot(weights.astype(BF), dmix, TN)
        dweights = dot(dmix, value, NT).astype(BF).astype(F32)
        moved = weights * dweights
        dscores = (moved - weights * jnp.sum(moved, axis=-1, keepdims=True)) * SCALE
        dscores = dscores.astype(BF)
        dquery = dot(dscores, key, NN).astype(BF).astype(F32)
        grads[:, cols] = rotated_back(dquery, cosine, sine).astype(BF)
        dkey += dot(dscores, query, TN)
    dkey = dkey.astype(BF).astype(F32)
    grads[:, QC : QC + KC] = rotated_back(dkey, cosine, sine).astype(BF)
    grads[:, QC + KC :] = dvalue.astype(BF)
    if last:
        spread(meta, sent, dpart_scr)
        return
    for c in range(NC):
        cols = chunk(c)
        dnormed = dot(grads[:, :QC], wq[cols, :], NT)
        dnormed += dot(grads[:, QC : QC + KC], wk[cols, :], NT)
        dnormed += dot(grads[:, QC + KC :], wv[cols, :], NT)
        dnormed = dnormed.astype(BF)
        for k in range(MP):
            part_refs[k][:, cols] = dnormed[k * BLOCK : (k + 1) * BLOCK]


def backward_turn(turn, meta, inc, arrivals, gl, qkv, tables, weights, last):
    received = arrivals is not None
    carried = inc is not None
    operands = [meta] + ([inc] if carried else []) + list(arrivals or [])
    operands += [gl, qkv, tables, *weights]
    if last:
        out_shape = [shaped(ROWS, QC + 2 * KC)]
        out_shape += [shaped(n * BLOCK, COLS) for n in (4, 2, 2)]
        scratch = [pltpu.VMEM((MP, BLOCK, D), BF), pltpu.VMEM((BLOCK, D), BF)]
    else:
        out_shape = ([kept(MP, BLOCK, D)] if received else []) + [shaped(BLOCK, D)] * MP
        scratch = [pltpu.VMEM((ROWS, QC + 2 * KC), BF)]
    return call(
        functools.partial(backward_kernel, turn, received, carried, last),
        len(operands),
        out_shape,
        "backward_last" if last else "backward_turn",
        scratch,
    )(*operands)


def summed(parts, cols):
    total = parts[0][:, cols].astype(F32)
    for part in parts[1:]:
        total = total + part[:, cols].astype(F32)
    return total


def forward_share_kernel(meta, hidden, p0, p1, p2, p3, out):
    for c in range(NC):
        cols = chunk(c)
        total = summed((p0, p1, p2, p3), cols)
        out[:, cols] = (hidden[0, :, cols].astype(F32) + total).astype(BF)


def forward_share(meta, cur, parts):
    return call(forward_share_kernel, 6, shaped(BLOCK, D), "forward_share")(meta, cur, *parts)


def backward_share_kernel(received, *refs):
    refs = list(refs)
    meta, hidden = refs.pop(0), refs.pop(0)
    inc = refs.pop(0) if received else None
    gl, gain, p0, p1, p2, p3, out, scaled = refs
    square = jnp.zeros((BLOCK, 1), F32)
    along = jnp.zeros((BLOCK, 1), F32)
    for c in range(NC):
        cols = chunk(c)
        rows = hidden[0, :, cols].astype(F32)
        dnormed = summed((p0, p1, p2, p3), cols) * gain[:, cols]
        scaled[:, cols] = dnormed
        square += jnp.sum(rows * rows, axis=-1, keepdims=True)
        along += jnp.sum(dnormed * rows, axis=-1, keepdims=True)
    inv = lax.rsqrt(square / D + EPSILON)
    pull = inv * inv * inv * (along / D)
    for c in range(NC):
        cols = chunk(c)
        upstream = slot_grad(meta, gl, 0, cols)
        if received:
            upstream = upstream + inc[0, :, cols].astype(F32)
        rows = hidden[0, :, cols].astype(F32)
        out[:, cols] = (upstream + inv * scaled[:, cols] - rows * pull).astype(BF)


def backward_share(meta, cur, inc, gl, gain, parts):
    received = inc is not None
    operands = [meta, cur] + ([inc] if received else []) + [gl, gain, *parts]
    return call(
        functools.partial(backward_share_kernel, received),
        len(operands),
        shaped(BLOCK, D),
        "backward_share",
        [pltpu.VMEM((BLOCK, D), F32)],
    )(*operands)


def precise(a, b, dims):
    return lax.dot_general(
        a, b, (dims, ((), ())), precision=lax.Precision.HIGHEST, preferred_element_type=F32
    )


def pool_sum_kernel(meta, p0, p1, p2, p3, out):
    total = p0[...].astype(F32) + p1[...].astype(F32) + p2[...].astype(F32) + p3[...].astype(F32)
    out[...] = total.astype(BF)


def loss_kernel(meta, positives, *refs):
    raw, losses, gl = refs
    pairs = DP
    lines = raw.shape[0] // DP
    half = lines // 2

    def joined(seq):
        pieces = []
        for c in range(half):
            at = seq * half + c
            every = [raw[i * lines + at : i * lines + at + 1, :] for i in range(pairs)]
            pieces.append(jnp.concatenate([line.astype(F32) for line in every], axis=0))
        return jnp.concatenate(pieces, axis=1)

    q, z = joined(0), joined(1)
    row = lax.broadcasted_iota(jnp.int32, (pairs, pairs), 0)
    col = pair_at(meta[4], lax.broadcasted_iota(jnp.int32, (pairs, pairs), 1))
    target = jnp.zeros((pairs, pairs), F32)
    for i in range(pairs):
        match = (row == i) & (col == positives[pair_at(meta[4], i)])
        target = jnp.where(match, 1.0, target)
    eye = (
        lax.broadcasted_iota(jnp.int32, (pairs, pairs), 0)
        == lax.broadcasted_iota(jnp.int32, (pairs, pairs), 1)
    ).astype(F32)
    narrow = D // 2 ** (WIDTHS - 1)
    lane = lax.broadcasted_iota(jnp.int32, (1, 2 * narrow), 1) < narrow

    def block(x, b):
        if b == WIDTHS - 1:
            return jnp.where(lane, x[:, : 2 * narrow], 0.0)
        if b == WIDTHS - 2:
            return jnp.where(lane, 0.0, x[:, : 2 * narrow])
        return x[:, D // 2 ** (b + 1) : D // 2**b]

    gram = [None] * WIDTHS
    sq = [None] * WIDTHS
    sz = [None] * WIDTHS
    total = (jnp.zeros((pairs, pairs), F32), jnp.zeros((pairs, 1), F32), jnp.zeros((pairs, 1), F32))
    for b in reversed(range(WIDTHS)):
        qb, zb = block(q, b), block(z, b)
        total = (
            total[0] + precise(qb, zb, NT),
            total[1] + jnp.sum(qb * qb, axis=-1, keepdims=True),
            total[2] + jnp.sum(zb * zb, axis=-1, keepdims=True),
        )
        gram[b], sq[b], sz[b] = total
    cross = jnp.zeros((pairs, pairs), F32)
    pull_q = jnp.zeros((pairs, 1), F32)
    pull_z = jnp.zeros((pairs, 1), F32)
    out_lane = lax.broadcasted_iota(jnp.int32, (1, 128), 1)
    loss_row = jnp.zeros((1, 128), F32)

    def flat(column):
        return jnp.sum(column * eye, axis=0, keepdims=True)

    for b in range(WIDTHS):
        width = D // 2**b
        inv_q = lax.rsqrt(sq[b] / width + 1e-06)
        inv_z = lax.rsqrt(sz[b] / width + 1e-06)
        inv_z_row = flat(inv_z)
        weight = inv_q * inv_z_row / (width * SOFTMAX_TEMPER)
        scores = gram[b] * weight
        top = jnp.max(scores, axis=-1, keepdims=True)
        raised = jnp.exp(scores - top)
        norm = jnp.sum(raised, axis=-1, keepdims=True)
        each = jnp.log(norm) + top - jnp.sum(scores * target, axis=-1, keepdims=True)
        loss_row = loss_row + jnp.where(
            out_lane == b, jnp.sum(each, axis=0, keepdims=True) / pairs, 0.0
        )
        dscores = (raised / norm - target) / pairs
        cross = cross + dscores * weight
        ds = dscores * scores
        pull_q = pull_q + jnp.sum(ds, axis=-1, keepdims=True) * inv_q * inv_q / width
        ds_z = jnp.sum(jnp.sum(ds, axis=0, keepdims=True) * eye, axis=-1, keepdims=True)
        pull_z = pull_z + ds_z * inv_z * inv_z / width
        qb, zb = block(q, b), block(z, b)
        dq = precise(cross, zb, NN) - pull_q * qb
        dz = precise(cross, qb, TN) - pull_z * zb
        dq = dq[0:1] / meta[2].astype(F32)
        dz = dz[0:1] / meta[3].astype(F32)
        if b == WIDTHS - 2:
            held_q, held_z = dq, dz
        elif b == WIDTHS - 1:
            gl[0:1, : 2 * narrow] = jnp.where(lane, dq, held_q)
            gl[1:2, : 2 * narrow] = jnp.where(lane, dz, held_z)
        else:
            gl[0:1, width // 2 : width] = dq
            gl[1:2, width // 2 : width] = dz
    losses[...] = loss_row


def loss_and_grad(meta, positives, raw):
    smem, vmem = [pl.BlockSpec(memory_space=space) for space in (pltpu.SMEM, pltpu.VMEM)]
    return pl.pallas_call(
        placed(loss_kernel),
        in_specs=[smem, smem, vmem],
        out_specs=[vmem, vmem],
        out_shape=[shaped(1, 128, dtype=F32), shaped(2, D, dtype=F32)],
        compiler_params=pltpu.CompilerParams(vmem_limit_bytes=VMEM_LIMIT),
        name="loss_grad",
    )(meta, positives, raw)


def flipped(array, k):
    return lax.ppermute(array, "dp", [(j, j ^ k) for j in range(DP)])


def gathered_pairs(array, first):
    array = jnp.concatenate([array, flipped(array, 1)], axis=0)
    array, first = lax.optimization_barrier((array, first))
    one = flipped(first, 1)
    for reach in (2, 6):
        array = jnp.concatenate([array, flipped(array, reach)], axis=0)
    return array, one


def pair_at(place, slot):
    return place ^ slot ^ ((slot >> 2) << 1)


def gathered_heads(own):
    flip = flipped(own, 1)
    near = flipped(own, 2)
    far = flipped(own, 6)
    flip, near, far = lax.optimization_barrier((flip, near, far))
    flip_near = flipped(flip, 2)
    flip_far = flipped(flip, 6)
    across = flipped(near, 6)
    flip_across = flipped(flip_far, 2)
    return [own, flip, near, far, flip_near, flip_far, across, flip_across]


HEAD_SOURCES = (0, 1, 2, 6, 3, 7, 4, 5)


def second_step(high, first_got, rows):
    return jnp.concatenate([high, first_got[2 * rows : 4 * rows]], axis=0)


def third_step(low, first_got, second_got, rows):
    pieces = [low[rows:], first_got[rows : 2 * rows]]
    pieces += [second_got[rows : 2 * rows], second_got[3 * rows : 4 * rows]]
    return jnp.concatenate(pieces, axis=0)


def gathered_rows(first, high, low):
    one = flipped(first, 1)
    two = flipped(second_step(high, one, BLOCK), 2)
    three = flipped(third_step(low, one, two, BLOCK), 6)
    pieces = [low[:BLOCK], one[:BLOCK], two[:BLOCK], two[2 * BLOCK : 3 * BLOCK], three]
    own = jnp.concatenate(pieces, axis=0)
    ahead = [(j, (j + 1) % MP) for j in range(MP)]
    behind = [(j, (j - 1) % MP) for j in range(MP)]
    first = lax.ppermute(own, "mp", ahead)
    third = lax.ppermute(own, "mp", behind)
    second = lax.ppermute(own, "mp", [(j, (j + 2) % MP) for j in range(MP)])
    return [own, first, second, third]


def over_mp(arrays):
    got = [arrays[0]]
    for k in range(1, MP):
        pairs = [(j, (j + k) % MP) for j in range(MP)]
        got.append(lax.ppermute(arrays[k], "mp", pairs))
    return got


def turned_kernel(meta, low, mix, one, two, three, normed, mixed):
    def rows(ref, i):
        return ref[i * ROWS : (i + 1) * ROWS, :]

    normal = [rows(low, 0), rows(one, 0), rows(two, 0), rows(two, 2)]
    normal += [rows(three, i) for i in range(4)]
    blend = [mix[...], rows(one, 4), rows(two, 4), rows(two, 5)]
    blend += [rows(three, 4 + i) for i in range(4)]
    for i, source in enumerate(SOURCES):
        normed[source] = normal[i].T
        mixed[source] = blend[i].T


def turned(meta, *arrays):
    out = [shaped(DP, COLS, ROWS), shaped(DP, QC, ROWS)]
    return call(turned_kernel, 6, out, "turned")(meta, *arrays)


def row_sums(values):
    ones = jnp.ones((8, values.shape[1]), BF)
    top = values.astype(BF)
    rest = values - top.astype(F32)
    middle = rest.astype(BF)
    low = (rest - middle.astype(F32)).astype(BF)
    return dot(ones, top, NT) + dot(ones, middle, NT) + dot(ones, low, NT)


def weight_kernel(meta, normed, *refs):
    pieces, refs = refs[:DP], refs[DP:]
    gain, wq, wk, wv, dq, dk, dv = refs[:7]
    scale_outs, row_scr = refs[7:-1], refs[-1]
    total = jnp.zeros((COLS, QC + 2 * KC), F32)
    for source, piece in zip(HEAD_SOURCES, pieces):
        total += dot(normed[source], piece[...], NN)
    dq[...] = total[:, :QC]
    dk[...] = total[:, QC : QC + KC]
    dv[...] = total[:, QC + KC :]
    place = pl.ds(pl.multiple_of(meta[4] * COLS, COLS), COLS)
    scale = row_sums(total[:, :QC] * wq[place, :].astype(F32))
    kv = total[:, QC : QC + KC] * wk[place, :].astype(F32)
    kv = kv + total[:, QC + KC :] * wv[place, :].astype(F32)
    scale = scale + row_sums(kv)
    row_scr[...] = scale[0:1] / gain[:, place]
    for k, out in enumerate(scale_outs):
        at = pl.multiple_of(((meta[0] + k) & (MP - 1)) * 128, 128)
        out[...] = row_scr[:, pl.ds(at, 128)]


def weight_grads(meta, normed, pieces, gain, wq, wk, wv):
    sizes = [(COLS, QC), (COLS, KC), (COLS, KC)] + [(1, 128)] * MP
    outs = call(
        weight_kernel,
        6 + DP,
        [shaped(*size, dtype=F32) for size in sizes],
        "weight_grads",
        [pltpu.VMEM((1, COLS), F32)],
    )(meta, normed, *pieces, gain, wq, wk, wv)
    return outs[:3], outs[3:]


def out_kernel(meta, mixed, *refs):
    rows, out = refs[:MP], refs[MP]
    total = jnp.zeros((QC, COLS), F32)
    for k in range(DP):
        dpart = jnp.concatenate([r[k * BLOCK : (k + 1) * BLOCK] for r in rows], axis=0)
        total += dot(mixed[SOURCES[k]], dpart, NN)
    out[...] = total


def out_grads(meta, mixed, rows):
    out = shaped(QC, COLS, dtype=F32)
    return call(out_kernel, 2 + MP, out, "out_grads")(meta, mixed, *rows)


def local(entrance, lengths, positives, norm_gains, query_proj, key_proj, value_proj, out_proj):
    gain = norm_gains
    weights = (query_proj[0], key_proj[0], value_proj[0], out_proj[0])
    tables = jnp.asarray(rope_tables())
    meta = lengths

    cur = entrance.reshape(MP, BLOCK, D)
    arrived = None
    for turn in range(SECTIONS - 1):
        cur, parts = forward_turn(turn, meta, cur, arrived, gain, tables, weights, False)
        if turn == 0:
            parts, (gain, tables, *weights) = parts[:MP], parts[MP:]
        share = forward_share(meta, cur, scattered(parts, turn))
        arrived = sent_on(share, turn, turn + 1)
    cur, (first, high, low, mix, qkv, pooled) = forward_turn(
        SECTIONS - 1, meta, cur, arrived, gain, tables, weights, True
    )
    pools = over_mp([pooled] * MP)
    pooled = call(pool_sum_kernel, 5, shaped(*pooled.shape), "pool_sum")(meta, *pools)
    raw, one = gathered_pairs(pooled, first)
    losses, gl = loss_and_grad(meta, positives, raw)

    inc, arrived = None, None
    for turn in reversed(range(1, SECTIONS)):
        outs = backward_turn(turn, meta, inc, arrived, gl, qkv, tables, weights, False)
        if arrived is not None:
            inc, parts = outs[0], outs[1:]
        else:
            parts = outs
        parts = scattered(parts, turn)
        if turn == 3:
            parts[3], one = lax.optimization_barrier((parts[3], one))
            step = second_step(high, one, ROWS)
            two = flipped(jnp.concatenate([step, mix, one[4 * ROWS :]], axis=0), 2)
        if turn == 2:
            parts[3], two = lax.optimization_barrier((parts[3], two))
            step = third_step(low, one, two, ROWS)
            pieces = [step, mix, one[4 * ROWS :], two[4 * ROWS :]]
            three = flipped(jnp.concatenate(pieces, axis=0), 6)
        share = backward_share(meta, cur, inc, gl, gain, parts)
        arrived = sent_on(share, turn, turn - 1)
        if turn == 1:
            arrived[0], three = lax.optimization_barrier((arrived[0], three))
            normed, mixed = turned(meta, low, mix, one, two, three)
            arrived[1], normed, mixed = lax.optimization_barrier((arrived[1], normed, mixed))
    heads, *blocks = backward_turn(0, meta, inc, arrived, gl, qkv, tables, weights, True)
    pieces = gathered_heads(heads)
    rows = gathered_rows(*blocks)
    (dq, dk, dv), scales = weight_grads(meta, normed, pieces, gain, *weights[:3])
    scales = over_mp(scales)
    out_grad = out_grads(meta, mixed, rows)
    scale = sum(scales)
    return (losses[:, :WIDTHS], scale, dq[None], dk[None], dv[None], out_grad[None])


def solution(mesh):
    in_specs = (
        P("dp", None, None, None),
        P("dp", None),
        P(),
        P("section", None),
        P("section", None, "mp"),
        P("section", None, "mp"),
        P("section", None, "mp"),
        P("section", "mp", None),
    )
    out_specs = (
        P("section", None),
        P("section", ("dp", "mp")),
        P("section", "dp", "mp"),
        P("section", "dp", "mp"),
        P("section", "dp", "mp"),
        P("section", "mp", "dp"),
    )
    return jax.shard_map(local, mesh=mesh, in_specs=in_specs, out_specs=out_specs, check_vma=False)
```
